512 devices in a mesh: gx: 64 (over x, y, z_hi), gy: 8 (over z_lo, core).
Axes of the slice: x: 4, y: 4, z: 16 (z_hi: 4, z_lo: 4; z = z_hi * 4 + z_lo), core: 2. Of those that a mesh axis runs over, the one named last changes fastest.
Arguments:
- positions: float32 [3, 512, 32, 4], P(None, 'gx', 'gy'), may hold values from 0 to 1536, as said below
- occupied: int32 [512, 32, 4], P('gx', 'gy'), may hold values from 0 to 1
- species: int32 [512, 32, 4], P('gx', 'gy'), may hold values from 0 to 9
- neighbours: int32 [512, 32, 4, 12], P('gx', 'gy'), may hold values from 0 to 383, as said below
- embedding: bfloat16 [10, 128], replicated, may hold values from -6 to 6
- radial_first: bfloat16 [2, 8, 64], replicated, may hold values from -6 to 6
- radial_second: bfloat16 [2, 64, 64], replicated, may hold values from -0.75 to 0.75
- radial_third: bfloat16 [2, 64, 64], replicated, may hold values from -0.75 to 0.75
- radial_last: bfloat16 [2, 64, 384], replicated, may hold values from -1.5 to 1.5
- up_weight: bfloat16 [2, 128, 128], replicated, may hold values from -0.5 to 0.5
- product_weight: float32 [2, 10, 4, 128], replicated, may hold values from -3 to 3
- out_weight: bfloat16 [2, 128, 128], replicated, may hold values from -0.5 to 0.5
- read_linear: float32 [1, 128], replicated, may hold values from -0.5 to 0.5
- read_hidden: bfloat16 [128, 16], replicated, may hold values from -0.5 to 0.5
- read_last: float32 [16], replicated, may hold values from -1.5 to 1.5
Outputs:
- energies: float32 [512, 32, 4], P('gx', 'gy')
- forces: float32 [3, 512, 32, 4], P(None, 'gx', 'gy')
The draws below stay inside these ranges and needn't reach their ends.
Inputs may be any that keep to these rules, and one draw needn't show every extreme that they name: `positions`: each coordinate of site (x, y, z) lies within 0.22 * 2.2 of its site's centre 2.2 (x + 0.5, y + 0.5, z + 0.5). `neighbours`: a site's 12 slots name distinct other sites inside the depth range whose offset (dx, dy, dz) in sites has dx^2 + dy^2 + dz^2 <= 5, as (p * 8 + q) * 4 + s in the block of its domain extended by two sites on each side along the long axis and across.
All inputs are finite; a program needn't handle non-finite values.
Results may differ from the reference program's by a relative error of at most 0.035.
Values may be sent and summed in bfloat16 or wider, within the bound.
A program may use at most 64 MiB of HBM per device.

```python
import math
import jax
import jax.numpy as jnp
import numpy as np
from jax import lax

CHANNELS = 128
RADIAL = 64
BESSEL = 8
SPECIES = 10
READ = 16
LAYERS = 2
SLOTS = 12
SITES_X = 8
SITES_Y = 4
SITES_Z = 4
GRID_X = 512
GRID_Y = 32
N_GX = 64
N_GY = 8


SPACING = 2.2


def offset_table():
    reaches = np.arange(-2, 3)
    offsets_all = np.stack(np.meshgrid(reaches, reaches, reaches, indexing='ij'), -1).reshape(-1, 3)
    lengths = np.sum(offsets_all * offsets_all, axis=1)
    keep_rows = (lengths > 0) & (lengths <= 5)
    return offsets_all[keep_rows].astype(np.int32)


def draw_positions(key, part):
    lattice = jnp.stack(jnp.meshgrid(jnp.arange(GRID_X), jnp.arange(GRID_Y), jnp.arange(SITES_Z), indexing='ij'), 0).astype(jnp.float32)
    jitter = jnp.clip(0.08 * jax.random.normal(key, lattice.shape, jnp.float32), -0.22, 0.22)
    return (lattice + 0.5 + jitter) * SPACING


def draw_occupied(key, part):
    column = jnp.arange(GRID_X)[:, None, None]
    protein = (column >= GRID_X // 4) & (column < 3 * GRID_X // 4)
    coin_flip = jax.random.randint(key, (GRID_X, GRID_Y, SITES_Z), 0, 2)
    return jnp.where(protein, 1, coin_flip).astype(jnp.int32)


def draw_neighbours(key, part):
    offsets = offset_table()
    candidates = offsets.shape[0]
    depth = jnp.arange(SITES_Z)[:, None] + jnp.asarray(offsets[:, 2])[None, :]
    inside = (depth >= 0) & (depth < SITES_Z)
    planar = offsets[:, 2] == 0
    far_face = planar & (np.abs(offsets[:, 0]) + np.abs(offsets[:, 1]) == 2) & ((offsets[:, 0] == 0) | (offsets[:, 1] == 0))
    diagonal = planar & (np.abs(offsets[:, 0]) == 1) & (np.abs(offsets[:, 1]) == 1)
    forced = jnp.asarray(far_face | diagonal)
    order_key, shuffle_key = jax.random.split(key)
    labels = jnp.arange(candidates, dtype=jnp.int32)
    scores = jax.random.randint(order_key, (GRID_X, GRID_Y, SITES_Z, candidates), 0, 2 ** 20) * 128 + labels
    scores = jnp.where(forced, 2 ** 28 + labels, scores)
    scores = jnp.where(inside[None, None], scores, -1 - labels)
    chosen = lax.top_k(scores, SLOTS)[1]
    shuffle = jax.random.randint(shuffle_key, chosen.shape, 0, 2 ** 20) * 128 + jnp.arange(SLOTS, dtype=jnp.int32)
    placing = lax.top_k(shuffle, SLOTS)[1]
    chosen = jnp.take_along_axis(chosen, placing, -1)
    moves = jnp.asarray(offsets)[chosen]
    site_x = (jnp.arange(GRID_X) % SITES_X)[:, None, None, None]
    site_y = (jnp.arange(GRID_Y) % SITES_Y)[None, :, None, None]
    site_z = jnp.arange(SITES_Z)[None, None, :, None]
    index = ((site_x + moves[..., 0] + 2) * (SITES_Y + 4) + site_y + moves[..., 1] + 2) * SITES_Z + site_z + moves[..., 2]
    return index.astype(jnp.int32)


def with_ends(drawn, rng, low, high):
    longest = drawn.shape.index(max(drawn.shape))
    spots = []
    for shift in (0, 1):
        where = [jax.random.randint(jax.random.fold_in(rng, axis), (), 0, length) for axis, length in enumerate(drawn.shape)]
        where[longest] = (where[longest] + shift) % drawn.shape[longest]
        spots.append(tuple(where))
    return drawn.at[spots[0]].set(low).at[spots[1]].set(high)


def rank_table(count, skew):
    loads = [(1 << 20) // math.isqrt(standing ** skew) + 1 for standing in range(1, count + 1)]
    scale = 1 + sum(loads) // (1 << 30)
    return np.cumsum(np.array([max(1, weight // scale) for weight in loads]))


def ranked_ids(rng, extent, count, lean):
    grid = rank_table(count, lean)
    lot = jax.random.randint(jax.random.fold_in(rng, 1), extent, 0, int(grid[count - 1]))
    rank = jnp.searchsorted(jnp.asarray(grid, jnp.int32), lot, side="right")
    return jax.random.permutation(jax.random.fold_in(rng, 2), count)[rank].astype(jnp.int32)


def scatter_about(key, extent, spread, limit, kind=jnp.bfloat16):
    return jnp.clip(spread * jax.random.normal(key, extent, jnp.float32), -limit, limit).astype(kind)


def setup_inputs(seed: int = 0) -> dict:
    arg_keys = jax.random.split(jax.random.key(seed), 16)
    positions = draw_positions(jax.random.fold_in(arg_keys[15], 71), 0)
    occupied = draw_occupied(jax.random.fold_in(arg_keys[15], 71), 0)
    species = with_ends(ranked_ids(arg_keys[2], (GRID_X, GRID_Y, SITES_Z), SPECIES, 2), jax.random.fold_in(arg_keys[2], 3), 0, SPECIES - 1).astype(jnp.int32)
    neighbours = draw_neighbours(jax.random.fold_in(arg_keys[15], 71), 0)
    embedding = scatter_about(arg_keys[4], (SPECIES, CHANNELS), 1.0, 6.0)
    radial_first = scatter_about(arg_keys[5], (LAYERS, BESSEL, RADIAL), 1 ** -0.5, 6.0)
    radial_second = scatter_about(arg_keys[6], (LAYERS, RADIAL, RADIAL), RADIAL ** -0.5, 0.75)
    radial_third = scatter_about(arg_keys[7], (LAYERS, RADIAL, RADIAL), RADIAL ** -0.5, 0.75)
    radial_last = scatter_about(arg_keys[8], (LAYERS, RADIAL, 3 * CHANNELS), (RADIAL // 4) ** -0.5, 1.5)
    up_weight = scatter_about(arg_keys[9], (LAYERS, CHANNELS, CHANNELS), CHANNELS ** -0.5, 0.5)
    product_weight = scatter_about(arg_keys[10], (LAYERS, SPECIES, 4, CHANNELS), 0.5, 3.0, jnp.float32)
    out_weight = scatter_about(arg_keys[11], (LAYERS, CHANNELS, CHANNELS), CHANNELS ** -0.5, 0.5)
    read_linear = scatter_about(arg_keys[12], (LAYERS - 1, CHANNELS), CHANNELS ** -0.5, 0.5, jnp.float32)
    read_hidden = scatter_about(arg_keys[13], (CHANNELS, READ), CHANNELS ** -0.5, 0.5)
    read_last = scatter_about(arg_keys[14], (READ,), READ ** -0.5, 1.5, jnp.float32)
    return {"positions": positions, "occupied": occupied, "species": species, "neighbours": neighbours, "embedding": embedding, "radial_first": radial_first, "radial_second": radial_second, "radial_third": radial_third, "radial_last": radial_last, "up_weight": up_weight, "product_weight": product_weight, "out_weight": out_weight, "read_linear": read_linear, "read_hidden": read_hidden, "read_last": read_last}


CUTOFF = 5.0

def rounded(value):
    fixed = lax.stop_gradient(value)
    lowered = lax.optimization_barrier(fixed.astype(jnp.bfloat16)).astype(jnp.float32)
    return value + (lowered - fixed)

def species_weights(one_hot, mix_table):
    return jnp.einsum('xyzs,sjc->xyzjc', one_hot, mix_table, precision=lax.Precision.HIGHEST)

def edge_block(ghost_values, geometry, slot_index, centre_ids, mixing, radial):
    layer_one, layer_two, layer_three, layer_out = radial
    channels = ghost_values.shape[1]
    block_rows, slot_count = slot_index.shape
    bessel_count = layer_one.shape[0]
    centre = geometry[:, centre_ids]
    neighbour = geometry[:, slot_index]
    displace = neighbour[:3] - centre[:3, :, None]
    weight = centre[3][:, None] * neighbour[3]
    squared = lax.optimization_barrier(jnp.sum(displace * displace, axis=0))
    distance = jnp.sqrt(jnp.where(weight > 0, squared, 1.0))
    direction = displace / distance
    scaled = distance / CUTOFF
    degrees = jnp.arange(1, bessel_count + 1).astype(jnp.float32)
    bessel = math.sqrt(2.0 / CUTOFF) * jnp.sin(math.pi * scaled[..., None] * degrees) / distance[..., None]
    inside = jnp.minimum(scaled, 1.0)
    envelope = 1.0 - 28.0 * inside ** 6 + 48.0 * inside ** 7 - 21.0 * inside ** 8
    envelope = jnp.where(scaled < 1.0, envelope, 0.0)
    hidden = rounded(bessel.reshape(-1, bessel_count))
    for matrix in (layer_one, layer_two, layer_three):
        hidden = rounded(jax.nn.silu(jnp.dot(hidden.astype(jnp.bfloat16), matrix, preferred_element_type=jnp.float32)))
    radial_out = jnp.dot(hidden.astype(jnp.bfloat16), layer_out, preferred_element_type=jnp.float32)
    radial_out = radial_out.reshape(block_rows, slot_count, 3, channels) * (envelope * weight)[..., None, None]
    gathered = ghost_values[slot_index]
    weighted = radial_out * gathered[:, :, None, :]
    factor = 1.0 / math.sqrt(slot_count)
    along_x = direction[0]
    along_y = direction[1]
    along_z = direction[2]
    root_three = math.sqrt(3.0)
    root_five = math.sqrt(5.0)
    root_fifteen = math.sqrt(15.0)
    first_degree = root_three * direction
    second_degree = jnp.stack([root_fifteen * along_x * along_y, root_fifteen * along_y * along_z, 0.5 * root_five * (3.0 * along_z * along_z - 1.0), root_fifteen * along_x * along_z, 0.5 * root_fifteen * (along_x * along_x - along_y * along_y)], axis=0)
    scalar_part = factor * lax.optimization_barrier(jnp.sum(weighted[:, :, 0], axis=1))
    vector_part = factor * jnp.einsum('mbk,bkc->bmc', first_degree, weighted[:, :, 1], precision=lax.Precision.HIGHEST)
    tensor_part = factor * jnp.einsum('mbk,bkc->bmc', second_degree, weighted[:, :, 2], precision=lax.Precision.HIGHEST)
    return mixing[:, 0] * scalar_part + mixing[:, 1] * scalar_part * scalar_part + mixing[:, 2] * lax.optimization_barrier(jnp.sum(vector_part * vector_part, axis=1)) + mixing[:, 3] * lax.optimization_barrier(jnp.sum(tensor_part * tensor_part, axis=1))

def interact(ghost_values, geometry, neighbours, mixing, radial):
    size_x, size_y, size_z, slot_count = neighbours.shape
    channels = ghost_values.shape[-1]
    extended = ghost_values.shape[0] * ghost_values.shape[1] * size_z
    flat_values = ghost_values.reshape(extended, channels)
    flat_geometry = geometry.reshape(geometry.shape[0], extended)
    atoms_here = size_x * size_y * size_z
    serial = jnp.arange(atoms_here, dtype=jnp.int32)
    index_x = serial // (size_y * size_z)
    index_y = serial // size_z % size_y
    index_z = serial % size_z
    centres = ((index_x + 2) * (size_y + 4) + index_y + 2) * size_z + index_z
    block_size = math.gcd(atoms_here, 128)
    blocks = atoms_here // block_size

    def per_block(inputs):
        slot_index, centre_ids, mixing_rows = inputs
        return edge_block(flat_values, flat_geometry, slot_index, centre_ids, mixing_rows, radial)
    result = lax.map(jax.checkpoint(per_block), (neighbours.reshape(blocks, block_size, slot_count), centres.reshape(blocks, block_size), mixing.reshape(blocks, block_size, 4, channels)))
    return result.reshape(size_x, size_y, size_z, channels)

def project_up(current, matrix):
    channels = current.shape[-1]
    product = jnp.dot(current.astype(jnp.bfloat16).reshape(-1, channels), matrix, preferred_element_type=jnp.float32)
    return rounded(product.reshape(current.shape))

def update(current, messages, matrix, present):
    channels = current.shape[-1]
    mixed = jnp.dot(rounded(messages).astype(jnp.bfloat16).reshape(-1, channels), matrix, preferred_element_type=jnp.float32)
    return rounded(current + present[..., None] * mixed.reshape(current.shape))

def readout(states, present, read_linear, read_hidden, read_last):
    energy_sum = jnp.zeros(present.shape, jnp.float32)
    for layer_index in range(len(states) - 1):
        energy_sum = energy_sum + lax.optimization_barrier(jnp.sum(states[layer_index] * read_linear[layer_index], axis=-1))
    final_state = states[-1]
    channels = final_state.shape[-1]
    hidden = jax.nn.silu(jnp.dot(final_state.astype(jnp.bfloat16).reshape(-1, channels), read_hidden, preferred_element_type=jnp.float32))
    energy_sum = energy_sum + lax.optimization_barrier(jnp.sum(hidden * read_last, axis=-1)).reshape(present.shape)
    return present * energy_sum

def reference(positions, occupied, species, neighbours, embedding, radial_first, radial_second, radial_third, radial_last, up_weight, product_weight, out_weight, read_linear, read_hidden, read_last):
    present = occupied.astype(jnp.float32)
    species_count = embedding.shape[0]
    one_hot = (species[..., None] == jnp.arange(species_count, dtype=jnp.int32)).astype(jnp.float32)
    initial = jnp.dot(one_hot.astype(jnp.bfloat16).reshape(-1, species_count), embedding, preferred_element_type=jnp.float32)
    initial = initial.reshape(GRID_X, GRID_Y, SITES_Z, CHANNELS) * present[..., None]
    domains = N_GX * N_GY

    def by_domain(array):
        trailing = array.shape[2:]
        regrouped = array.reshape((N_GX, SITES_X, N_GY, SITES_Y) + trailing)
        return jnp.moveaxis(regrouped, 2, 1).reshape((domains, SITES_X, SITES_Y) + trailing)
    neighbour_blocks = by_domain(neighbours)
    hot_blocks = by_domain(one_hot)

    def energy_of(coords):
        geometry = jnp.concatenate([coords, present[None]], axis=0)
        padded_geometry = jnp.pad(geometry, ((0, 0), (2, 2), (2, 2), (0, 0)))
        current = initial
        states = []
        for layer_index in range(LAYERS):
            radial = (radial_first[layer_index], radial_second[layer_index], radial_third[layer_index], radial_last[layer_index])
            lifted = project_up(current, up_weight[layer_index])
            padded_values = jnp.pad(lifted, ((2, 2), (2, 2), (0, 0), (0, 0)))
            mix_table = product_weight[layer_index]

            def per_domain(inputs):
                domain, slot_block, hot_block = inputs
                start_x = (domain // N_GY * SITES_X).astype(jnp.int32)
                start_y = (domain % N_GY * SITES_Y).astype(jnp.int32)
                anchor = jnp.zeros((), jnp.int32)
                values = lax.dynamic_slice(padded_values, (start_x, start_y, anchor, anchor), (SITES_X + 4, SITES_Y + 4, SITES_Z, CHANNELS))
                local_geometry = lax.dynamic_slice(padded_geometry, (anchor, start_x, start_y, anchor), (4, SITES_X + 4, SITES_Y + 4, SITES_Z))
                return interact(values, local_geometry, slot_block, species_weights(hot_block, mix_table), radial)
            messages = lax.map(per_domain, (jnp.arange(domains, dtype=jnp.int32), neighbour_blocks, hot_blocks))
            messages = jnp.moveaxis(messages.reshape(N_GX, N_GY, SITES_X, SITES_Y, SITES_Z, CHANNELS), 1, 2)
            messages = messages.reshape(GRID_X, GRID_Y, SITES_Z, CHANNELS)
            current = update(current, messages, out_weight[layer_index], present)
            states.append(current)
        energies = readout(states, present, read_linear, read_hidden, read_last)
        return (jnp.sum(energies), energies)
    gradient, energies = jax.grad(energy_of, has_aux=True)(positions)
    return (energies, -gradient)
```

```python
import math

import jax
import jax.numpy as jnp
from jax import lax
from jax.experimental import pallas as pl
from jax.experimental.pallas import tpu as pltpu
from jax.sharding import PartitionSpec as P

F32 = jnp.float32
BF16 = jnp.bfloat16
MESH = pl.DeviceIdType.MESH
CUTOFF = 5.0
SLOTS = 12
SITES = 128
EDGES = SITES * SLOTS
GHOSTS = 256
EXT = SITES + GHOSTS
CH = 128
RAD = 64
BES = 8
LAYERS = 2

DIRS = ((-1, 0), (1, 0), (-1, -1), (-1, 1), (1, -1), (1, 1), (0, -1), (0, 1))
OFF = (0, 32, 64, 80, 96, 112, 128, 192)
LEN = (32, 32, 16, 16, 16, 16, 64, 64)
OPP = (1, 0, 5, 4, 3, 2, 7, 6)

NT = (((1,), (1,)), ((), ()))
TN = (((0,), (0,)), ((), ()))
NN = (((1,), (0,)), ((), ()))


def dot(a, b, dims=NN):
    return lax.dot_general(a, b, dims, preferred_element_type=F32)


def dot_exact(a, b, dims=NN):
    return lax.dot_general(a, b, dims, preferred_element_type=F32, precision=lax.Precision.HIGHEST)


def iota(shape, dim):
    return lax.broadcasted_iota(jnp.int32, shape, dim)


def split3(x):
    high = x.astype(BF16).astype(F32)
    rest = x - high
    middle = rest.astype(BF16).astype(F32)
    return jnp.concatenate([high, middle, rest - middle], axis=0).astype(BF16)


def split2(x):
    high = x.astype(BF16).astype(F32)
    return jnp.concatenate([high, x - high], axis=0).astype(BF16)


def strip_site(direction, row):
    dx, dy = DIRS[direction]
    per_x = 16 if dy == 0 else 8
    x0 = 6 if dx == 1 else 0
    y0 = 2 if dy == 1 else 0
    return (x0 + row // per_x) * 16 + y0 * 4 + row % per_x


def silu_parts(z):
    s = 0.5 + 0.5 * jnp.tanh(0.5 * z)
    g = z * s
    return g, s + g * (1.0 - s)


ROOT3 = math.sqrt(3.0)
ROOT5 = math.sqrt(5.0)
ROOT15 = math.sqrt(15.0)
FACTOR = 1.0 / math.sqrt(SLOTS)


def kernel(
    n_gx,
    n_gy,
    pos_ref,
    occ_ref,
    spec_ref,
    nbr_ref,
    emb_ref,
    w1_ref,
    w2_ref,
    w3_ref,
    w4_ref,
    up_ref,
    pw_ref,
    ow_ref,
    rl_ref,
    rh_ref,
    rlast_ref,
    en_ref,
    force_ref,
    raw,
    nb,
    geo,
    sel,
    ps,
    oh,
    snd1,
    rcv1,
    snd2,
    rcv2,
    snd3,
    rcv3,
    snd4,
    rcv4,
    gs,
    bs,
    ye,
    bd,
    mix,
    dsilu,
    q,
    u,
    a,
    msg,
    dq,
    du,
    s_acc,
    send_sem,
    recv_sem,
):
    gx = lax.axis_index("gx")
    gy = lax.axis_index("gy")
    peers = []
    inside = []
    for dx, dy in DIRS:
        px, py = gx + dx, gy + dy
        peers.append((lax.rem(px + n_gx, n_gx), lax.rem(py + n_gy, n_gy)))
        inside.append((px >= 0) & (px < n_gx) & (py >= 0) & (py < n_gy))

    barrier = pltpu.get_barrier_semaphore()
    for peer in peers:
        pl.semaphore_signal(barrier, inc=1, device_id=peer, device_id_type=MESH)

    raw[...] = jnp.zeros_like(raw)
    for y in range(4):
        for c in range(3):
            raw[c * 16 + y * 4 : c * 16 + y * 4 + 4, 0:8] = pos_ref[c, y]
        raw[48 + y * 4 : 52 + y * 4, 0:8] = occ_ref[y].astype(F32)
        raw[64 + y * 4 : 68 + y * 4, 0:8] = spec_ref[y].astype(F32)
    x_pick = (iota((SITES, SITES), 0) == iota((SITES, SITES), 1) // 16).astype(F32)
    spread = dot_exact(raw[...], x_pick)
    yz_mask = iota((80, SITES), 0) % 16 == iota((80, SITES), 1) % 16
    spread = jnp.where(yz_mask, spread, 0.0)
    geo[...] = jnp.zeros_like(geo)
    for f in range(5):
        geo[f : f + 1, 0:SITES] = jnp.sum(spread[f * 16 : f * 16 + 16], axis=0, keepdims=True)

    lane = iota((SITES, SITES), 1)
    site = iota((SITES, SITES), 0)
    for d in range(8):
        row = lane - OFF[OPP[d]] % SITES
        hit = (row >= 0) & (row < LEN[d]) & (strip_site(d, row) == site)
        sel[:, d * SITES : (d + 1) * SITES] = jnp.where(hit, 1.0, 0.0).astype(BF16)
        rows = iota((LEN[d], SITES), 0)
        hit = strip_site(d, rows) == iota((LEN[d], SITES), 1)
        ps[OFF[d] : OFF[d] + LEN[d], :] = jnp.where(hit, 1.0, 0.0).astype(BF16)
    placed = dot(split3(geo[:, 0:SITES]), sel[...])
    placed = placed[0:8] + placed[8:16] + placed[16:24]
    for d in range(8):
        snd1[d] = placed[:, d * SITES : (d + 1) * SITES]

    pl.semaphore_wait(barrier, 8)

    copies = []

    def exchange(phase, sources, targets):
        started = []
        for d in range(8):
            copy = pltpu.make_async_remote_copy(
                src_ref=sources(d),
                dst_ref=targets(OPP[d]),
                send_sem=send_sem.at[phase, d],
                recv_sem=recv_sem.at[phase, OPP[d]],
                device_id=peers[d],
                device_id_type=MESH,
            )
            copy.start()
            started.append(copy)
        copies.extend(started)

        def finish():
            for d in range(8):
                pltpu.make_async_remote_copy(
                    src_ref=sources(OPP[d]),
                    dst_ref=targets(d),
                    send_sem=send_sem.at[phase, OPP[d]],
                    recv_sem=recv_sem.at[phase, d],
                    device_id=peers[OPP[d]],
                    device_id_type=MESH,
                ).wait_recv()

        return finish

    arrived1 = exchange(0, lambda d: snd1.at[d], lambda d: rcv1.at[d])

    nb[...] = jnp.zeros_like(nb)
    for x in range(8):
        for y in range(4):
            nb[x * 16 + y * 4 : x * 16 + y * 4 + 4, 0:SLOTS] = nbr_ref[x, y].astype(F32)
    index = nb[...].T[0:16].astype(jnp.int32)
    s = index & 3
    yy = (index >> 2) & 7
    xx = index >> 5
    x_lo, x_hi, y_lo, y_hi = xx < 2, xx >= 10, yy < 2, yy >= 6
    rx = jnp.where(x_lo, xx, jnp.where(x_hi, xx - 10, xx - 2))
    ry = jnp.where(y_lo, yy, jnp.where(y_hi, yy - 6, yy - 2))
    per_x = jnp.where(y_lo | y_hi, 8, 16)
    base_lo = jnp.where(y_lo, OFF[2], jnp.where(y_hi, OFF[3], OFF[0]))
    base_hi = jnp.where(y_lo, OFF[4], jnp.where(y_hi, OFF[5], OFF[1]))
    base_mid = jnp.where(y_lo, OFF[6], jnp.where(y_hi, OFF[7], -SITES))
    base = jnp.where(x_lo, base_lo, jnp.where(x_hi, base_hi, base_mid))
    place = base + SITES + rx * per_x + ry * 4 + s
    ext_row = iota((EXT, SITES), 0)
    for k in range(SLOTS):
        hit = ext_row == place[k : k + 1]
        oh[:, k * SITES : (k + 1) * SITES] = jnp.where(hit, 1.0, 0.0).astype(BF16)

    present = geo[3:4, 0:SITES]
    own_hot = (geo[4:5, 0:SITES].astype(jnp.int32) == iota((16, SITES), 0)).astype(F32)
    for layer in range(LAYERS):
        for j in range(4):
            table = pw_ref[layer, :, j, :]
            mix[layer, j] = dot_exact(table, own_hot[0:10], TN)
    h0 = dot(emb_ref[...].astype(F32), own_hot[0:10], TN) * present
    lifted_table = dot(emb_ref[...], up_ref[0]).astype(BF16).astype(F32)

    arrived1()
    for f in range(2):
        tile = jnp.zeros((8, SITES), F32)
        for d in range(8):
            if OFF[d] // SITES == f:
                tile = tile + jnp.where(inside[d], rcv1[d], 0.0)
        geo[:, (f + 1) * SITES : (f + 2) * SITES] = tile

    gathered = dot(split3(geo[...]), oh[...])
    gathered = gathered[0:8] + gathered[8:16] + gathered[16:24]
    for k in range(SLOTS):
        gs[k * 8 : k * 8 + 8, :] = gathered[:, k * SITES : (k + 1) * SITES]
    ext_hot = (geo[4:5, :].astype(jnp.int32) == iota((16, EXT), 0)).astype(F32)
    u0 = dot(lifted_table, ext_hot[0:10], TN).astype(BF16)
    u[0] = dot(u0, oh[...])

    def rows_of(ref, m):
        return ref[pl.ds(m, SLOTS, stride=8), :]

    disp = [rows_of(gs, c) - geo[c : c + 1, 0:SITES] for c in range(3)]
    w = rows_of(gs, 3) * present
    squared = disp[0] * disp[0] + disp[1] * disp[1] + disp[2] * disp[2]
    dist = jnp.sqrt(jnp.where(w > 0, squared, 1.0))
    inv = 1.0 / dist
    nx, ny, nz = [c * inv for c in disp]
    scaled = jnp.minimum(dist * (1.0 / CUTOFF), 1.0)
    u2 = scaled * scaled
    u5 = u2 * u2 * scaled
    u6 = u5 * scaled
    env = 1.0 - 28.0 * u6 + 48.0 * u6 * scaled - 21.0 * u6 * u2
    env = jnp.where(scaled < 1.0, env, 0.0)
    gap = 1.0 - scaled
    slope = (-168.0 / CUTOFF) * u5 * gap * gap
    env_w = env * w
    slope_w = slope * w
    ye_scale = FACTOR * env_w
    harmonics = [
        ROOT3 * nx,
        ROOT3 * ny,
        ROOT3 * nz,
        ROOT15 * nx * ny,
        ROOT15 * ny * nz,
        0.5 * ROOT5 * (3.0 * nz * nz - 1.0),
        ROOT15 * nx * nz,
        0.5 * ROOT15 * (nx * nx - ny * ny),
    ]
    ye[0, 0:SLOTS] = ye_scale
    for m in range(8):
        ye[m + 1, 0:SLOTS] = ye_scale * harmonics[m]
    theta = math.pi * scaled
    sin1 = jnp.sin(theta)
    cos1 = jnp.cos(theta)
    twice = 2.0 * cos1
    sin_before, cos_before = jnp.zeros_like(sin1), jnp.ones_like(cos1)
    sin_m, cos_m = sin1, cos1
    amplitude = math.sqrt(2.0 / CUTOFF) * inv
    for m in range(BES):
        value = amplitude * sin_m
        bs[pl.ds(m, SLOTS, stride=8), :] = value
        bd[m, 0:SLOTS] = amplitude * ((m + 1) * math.pi / CUTOFF) * cos_m - value * inv
        sin_m, sin_before = twice * sin_m - sin_before, sin_m
        cos_m, cos_before = twice * cos_m - cos_before, cos_m

    def radial(layer):
        hidden = jnp.concatenate([bs[k * 8 : k * 8 + 8, :] for k in range(SLOTS)], axis=1)
        hidden = hidden.astype(BF16)
        for step, ref in enumerate((w1_ref, w2_ref, w3_ref)):
            z = dot(ref[layer], hidden, TN)
            g, slope_g = silu_parts(z)
            dsilu[layer, step] = slope_g
            hidden = g.astype(BF16)
        q[layer] = dot(w4_ref[layer], hidden, TN)

    def aggregate(layer):
        def body(block, carry):
            c0 = pl.multiple_of(block * 32, 32)
            acc = [jnp.zeros((32, SITES), F32) for _ in range(9)]
            for k in range(SLOTS):
                lanes = slice(k * SITES, (k + 1) * SITES)
                uk = u[layer, pl.ds(c0, 32), lanes]
                v = [q[layer, pl.ds(L * CH + c0, 32), lanes] * uk for L in range(3)]
                for m in range(9):
                    degree = 0 if m == 0 else (1 if m < 4 else 2)
                    acc[m] = acc[m] + ye[m, k : k + 1, :] * v[degree]
            for m in range(9):
                a[layer, m, pl.ds(c0, 32), :] = acc[m]
            p = [mix[layer, j, pl.ds(c0, 32), :] for j in range(4)]
            first = acc[1] * acc[1] + acc[2] * acc[2] + acc[3] * acc[3]
            second = acc[4] * acc[4] + acc[5] * acc[5] + acc[6] * acc[6]
            second = second + acc[7] * acc[7] + acc[8] * acc[8]
            result = p[0] * acc[0] + p[1] * acc[0] * acc[0] + p[2] * first + p[3] * second
            msg[pl.ds(c0, 32), :] = result.astype(BF16)
            return carry

        lax.fori_loop(0, CH // 32, body, 0)

    def aggregate_back(layer, msg_grad_ref, with_du):
        def body(block, carry):
            c0 = pl.multiple_of(block * 32, 32)
            g = msg_grad_ref[pl.ds(c0, 32), :]
            p = [mix[layer, j, pl.ds(c0, 32), :] for j in range(4)]
            a0 = a[layer, 0, pl.ds(c0, 32), :]
            scale1 = 2.0 * p[2] * g
            scale2 = 2.0 * p[3] * g
            da = [g * (p[0] + 2.0 * p[1] * a0)]
            for m in range(1, 9):
                da.append((scale1 if m < 4 else scale2) * a[layer, m, pl.ds(c0, 32), :])
            for k in range(SLOTS):
                lanes = slice(k * SITES, (k + 1) * SITES)
                uk = u[layer, pl.ds(c0, 32), lanes]
                qk = [q[layer, pl.ds(L * CH + c0, 32), lanes] for L in range(3)]
                v = [one * uk for one in qk]
                dv = [None, None, None]
                for m in range(9):
                    degree = 0 if m == 0 else (1 if m < 4 else 2)
                    term = ye[m, k : k + 1, :] * da[m]
                    dv[degree] = term if dv[degree] is None else dv[degree] + term
                    part = da[m] * v[degree]
                    part = part[0:8] + part[8:16] + part[16:24] + part[24:32]
                    at = (m * SLOTS + k) * 8
                    s_acc[at : at + 8, :] += part
                for L in range(3):
                    dq[pl.ds(L * CH + c0, 32), lanes] = (dv[L] * uk).astype(BF16)
                if with_du:
                    total = dv[0] * qk[0] + dv[1] * qk[1] + dv[2] * qk[2]
                    du[pl.ds(c0, 32), lanes] = total.astype(BF16)
            return carry

        lax.fori_loop(0, CH // 32, body, 0)

    def radial_back(layer):
        grad = dot(w4_ref[layer], dq[...])
        for step, ref in ((2, w3_ref), (1, w2_ref), (0, w1_ref)):
            dz = (grad * dsilu[layer, step]).astype(BF16)
            grad = dot(ref[layer], dz)
        return grad

    s_acc[...] = jnp.zeros_like(s_acc)
    radial(0)
    aggregate(0)
    mixed = dot(ow_ref[0], msg[...], TN)
    h1 = (h0 + present * mixed).astype(BF16)
    u1 = dot(up_ref[1], h1, TN).astype(BF16)
    snd2[...] = dot(ps[...], u1, NT).astype(BF16)
    arrived2 = exchange(
        1,
        lambda d: snd2.at[pl.ds(OFF[d], LEN[d])],
        lambda d: rcv2.at[pl.ds(OFF[d], LEN[d])],
    )
    radial(1)
    near = dot(u1, oh[0:SITES, :])
    arrived2()
    u[1] = near + dot(rcv2[...], oh[SITES:EXT, :], TN)
    aggregate(1)
    mixed = dot(ow_ref[1], msg[...], TN)
    h2 = (h1.astype(F32) + present * mixed).astype(BF16)

    diagonal = iota((CH, CH), 0) == iota((CH, CH), 1)
    linear = jnp.sum(jnp.where(diagonal, rl_ref[...], 0.0), axis=1, keepdims=True)
    small = iota((16, 16), 0) == iota((16, 16), 1)
    last = jnp.sum(jnp.where(small, rlast_ref[...], 0.0), axis=1, keepdims=True)
    z = dot(rh_ref[...], h2)
    g, slope_g = silu_parts(z)
    energy = jnp.sum(h1.astype(F32) * linear, axis=0, keepdims=True)
    energy = present * (energy + jnp.sum(g * last, axis=0, keepdims=True))
    dz = (present * last * slope_g).astype(BF16)
    dh2 = dot(rh_ref[...], dz, TN)
    dmixed = (present * dh2).astype(BF16)
    snd_grad = dot(ow_ref[1], dmixed)
    a_grad = mix
    del a_grad
    gs_grad = du
    del gs_grad
    bm = nb
    bm[...] = snd_grad
    aggregate_back(1, bm, True)
    snd3[...] = dot(oh[SITES:EXT, :], du[...], NT).astype(BF16)
    arrived3 = exchange(
        2,
        lambda d: snd3.at[pl.ds(OFF[d], LEN[d])],
        lambda d: rcv3.at[pl.ds(OFF[d], LEN[d])],
    )
    near = dot(du[...], oh[0:SITES, :], NT)
    bessel_grad = radial_back(1)
    arrived3()
    du1 = near + dot(rcv3[...], ps[...], TN)
    dh1 = dh2 + linear * present + dot(up_ref[1], du1.astype(BF16))
    dmixed = (present * dh1).astype(BF16)
    bm[...] = dot(ow_ref[0], dmixed)
    aggregate_back(0, bm, False)
    bessel_grad = bessel_grad + radial_back(0)

    for k in range(SLOTS):
        gs[k * 8 : k * 8 + 8, :] = bessel_grad[:, k * SITES : (k + 1) * SITES]
    dr = rows_of(gs, 0) * bd[0, 0:SLOTS]
    for m in range(1, BES):
        dr = dr + rows_of(gs, m) * bd[m, 0:SLOTS]

    def total_of(m):
        at = m * SLOTS * 8
        out = s_acc[pl.ds(at, SLOTS, stride=8), :]
        for j in range(1, 8):
            out = out + s_acc[pl.ds(at + j, SLOTS, stride=8), :]
        return FACTOR * out

    sums = [total_of(m) for m in range(9)]
    d_env = sums[0]
    for m in range(8):
        d_env = d_env + sums[m + 1] * harmonics[m]
    dr = dr + d_env * slope_w
    dy = [env_w * one for one in sums[1:]]
    dnx = ROOT3 * dy[0] + ROOT15 * (dy[3] * ny + dy[6] * nz + dy[7] * nx)
    dny = ROOT3 * dy[1] + ROOT15 * (dy[3] * nx + dy[4] * nz - dy[7] * ny)
    dnz = ROOT3 * dy[2] + ROOT15 * (dy[4] * ny + dy[6] * nx) + (3.0 * ROOT5) * dy[5] * nz
    radial_part = dr - inv * (dnx * nx + dny * ny + dnz * nz)
    gs[...] = jnp.zeros_like(gs)
    centre = []
    for c, (dn, n) in enumerate(((dnx, nx), (dny, ny), (dnz, nz))):
        dd = dn * inv + radial_part * n
        gs[pl.ds(c, SLOTS, stride=8), :] = dd
        centre.append(jnp.sum(dd, axis=0, keepdims=True))
    edge_grad = jnp.concatenate([gs[k * 8 : k * 8 + 8, :] for k in range(SLOTS)], axis=1)
    scattered = dot(split3(edge_grad), oh[...], NT)
    scattered = scattered[0:8] + scattered[8:16] + scattered[16:24]
    for f in range(2):
        snd4[f] = scattered[:, (f + 1) * SITES : (f + 2) * SITES]
    arrived4 = exchange(3, lambda d: snd4.at[OFF[d] // SITES], lambda d: rcv4.at[d])
    arrived4()
    returned = jnp.concatenate([rcv4[d] for d in range(8)], axis=1)
    back = dot(split3(returned), sel[...], NT)
    back = back[0:8] + back[8:16] + back[16:24] + scattered[:, 0:SITES]

    rows = [jnp.broadcast_to(centre[c] - back[c : c + 1], (16, SITES)) for c in range(3)]
    rows.append(jnp.broadcast_to(energy, (16, SITES)))
    full = jnp.concatenate(rows, axis=0)
    full = jnp.where(yz_mask[0:64], full, 0.0)
    out = dot_exact(full, x_pick, NT)
    for y in range(4):
        for c in range(3):
            force_ref[c, y] = out[c * 16 + y * 4 : c * 16 + y * 4 + 4, 0:8]
        en_ref[y] = out[48 + y * 4 : 52 + y * 4, 0:8]
    for copy in copies:
        copy.wait_send()


def shards(
    positions,
    occupied,
    species,
    neighbours,
    embedding,
    radial_first,
    radial_second,
    radial_third,
    radial_last,
    up_weight,
    product_weight,
    out_weight,
    read_linear,
    read_hidden,
    read_last,
):
    n_gx, n_gy = lax.axis_size("gx"), lax.axis_size("gy")
    vmem = pl.BlockSpec(memory_space=pltpu.VMEM)

    def run(*refs):
        kernel(n_gx, n_gy, *refs)

    energies, forces = pl.pallas_call(
        run,
        out_shape=(
            jax.ShapeDtypeStruct((4, 4, 8), F32),
            jax.ShapeDtypeStruct((3, 4, 4, 8), F32),
        ),
        in_specs=[vmem] * 15,
        out_specs=(vmem, vmem),
        scratch_shapes=[
            pltpu.VMEM((80, SITES), F32),
            pltpu.VMEM((SITES, SITES), F32),
            pltpu.VMEM((8, EXT), F32),
            pltpu.VMEM((SITES, 8 * SITES), BF16),
            pltpu.VMEM((GHOSTS, SITES), BF16),
            pltpu.VMEM((EXT, EDGES), BF16),
            pltpu.VMEM((8, 8, SITES), F32),
            pltpu.VMEM((8, 8, SITES), F32),
            pltpu.VMEM((GHOSTS, CH), BF16),
            pltpu.VMEM((GHOSTS, CH), BF16),
            pltpu.VMEM((GHOSTS, CH), BF16),
            pltpu.VMEM((GHOSTS, CH), BF16),
            pltpu.VMEM((2, 8, SITES), F32),
            pltpu.VMEM((8, 8, SITES), F32),
            pltpu.VMEM((SLOTS * 8, SITES), F32),
            pltpu.VMEM((SLOTS * 8, SITES), F32),
            pltpu.VMEM((9, 16, SITES), F32),
            pltpu.VMEM((BES, 16, SITES), F32),
            pltpu.VMEM((LAYERS, 4, CH, SITES), F32),
            pltpu.VMEM((LAYERS, 3, RAD, EDGES), F32),
            pltpu.VMEM((LAYERS, 3 * CH, EDGES), F32),
            pltpu.VMEM((LAYERS, CH, EDGES), F32),
            pltpu.VMEM((LAYERS, 9, CH, SITES), F32),
            pltpu.VMEM((CH, SITES), BF16),
            pltpu.VMEM((3 * CH, EDGES), BF16),
            pltpu.VMEM((CH, EDGES), BF16),
            pltpu.VMEM((9 * SLOTS * 8, SITES), F32),
            pltpu.SemaphoreType.DMA((4, 8)),
            pltpu.SemaphoreType.DMA((4, 8)),
        ],
        compiler_params=pltpu.CompilerParams(
            collective_id=0, has_side_effects=True, vmem_limit_bytes=48 * 1024 * 1024
        ),
    )(
        positions.transpose(0, 2, 3, 1),
        occupied.transpose(1, 2, 0),
        species.transpose(1, 2, 0),
        neighbours,
        embedding,
        radial_first,
        radial_second,
        radial_third,
        radial_last,
        up_weight,
        product_weight,
        out_weight,
        read_linear,
        read_hidden.T,
        read_last.reshape(1, -1),
    )
    return energies.transpose(2, 0, 1), forces.transpose(0, 3, 1, 2)


def solution(mesh):
    in_specs = (
        P(None, "gx", "gy", None),
        P("gx", "gy", None),
        P("gx", "gy", None),
        P("gx", "gy", None, None),
        P(),
        P(),
        P(),
        P(),
        P(),
        P(),
        P(),
        P(),
        P(),
        P(),
        P(),
    )
    out_specs = (P("gx", "gy", None), P(None, "gx", "gy", None))
    return jax.shard_map(shards, mesh=mesh, in_specs=in_specs, out_specs=out_specs, check_vma=False)
```

```python
import functools
import math

import jax
import jax.numpy as jnp
from jax import lax
from jax.experimental import pallas as pl
from jax.experimental.pallas import tpu as pltpu
from jax.sharding import PartitionSpec as P

F32 = jnp.float32
BF16 = jnp.bfloat16
MESH = pl.DeviceIdType.MESH
CUTOFF = 5.0
SLOTS = 12
SITES = 128
EDGES = SITES * SLOTS
GHOSTS = 304
EXT = SITES + GHOSTS
CH = 128
RAD = 64
BES = 8
LAYERS = 2

LEFT, RIGHT, ACROSS = 128, 256, 384

NT = (((1,), (1,)), ((), ()))
TN = (((0,), (0,)), ((), ()))
NN = (((1,), (0,)), ((), ()))


def dot(a, b, dims=NN):
    return lax.dot_general(a, b, dims, preferred_element_type=F32)


def dot_exact(a, b, dims=NN):
    return lax.dot_general(a, b, dims, preferred_element_type=F32, precision=lax.Precision.HIGHEST)


def iota(shape, dim):
    return lax.broadcasted_iota(jnp.int32, shape, dim)


def split3(x):
    high = x.astype(BF16).astype(F32)
    rest = x - high
    middle = rest.astype(BF16).astype(F32)
    return jnp.concatenate([high, middle, rest - middle], axis=0).astype(BF16)


def split2(x):
    high = x.astype(BF16).astype(F32)
    return jnp.concatenate([high, x - high], axis=0).astype(BF16)


def silu_parts(z):
    s = 0.5 + 0.5 * jnp.tanh(0.5 * z)
    g = z * s
    return g, s + g * (1.0 - s)


ROOT3 = math.sqrt(3.0)
ROOT5 = math.sqrt(5.0)
ROOT15 = math.sqrt(15.0)
FACTOR = 1.0 / math.sqrt(SLOTS)


def kernel(n_gx, *refs):
    inputs, refs = refs[:15], refs[15:]
    (en_ref, force_ref), refs = refs[:2], refs[2:]
    held, refs = refs[:15], refs[15:]
    (raw, nb, tile, geo, ps, oh, rcv1, snd2, rcv2, snd3, rcv3, snd4, rcv4), refs = refs[:13], refs[13:]
    (gs, bs, ye, bd, mix, dsilu, q, u, a, msg, dq, du, s_acc), refs = refs[:13], refs[13:]
    fetch_sem, send_sem, recv_sem = refs
    (pos_ref, occ_ref, spec_ref, nbr_ref, emb_ref, w1_ref, w2_ref, w3_ref, w4_ref), more = held[:9], held[9:]
    up_ref, pw_ref, ow_ref, rl_ref, rh_ref, rlast_ref = more

    fetches = []
    for i in range(15):
        fetch = pltpu.make_async_copy(inputs[i], held[i], fetch_sem.at[i])
        fetch.start()
        fetches.append(fetch)

    gx = lax.axis_index("gx")
    gy = lax.axis_index("gy")
    j, c = gy // 2, gy % 2
    own_half, own_slot = gy // 4, gy % 4
    edge = (gy == 3) | (gy == 4)
    halo_gy = 4 - c
    first, last_gx = gx == 0, gx == n_gx - 1
    has_left = jnp.logical_not((j == 0) & first)
    has_right = jnp.logical_not((j == 3) & last_gx)
    has_other = ((j == 0) | (j == 3)) & has_left & has_right
    other_gx = jnp.where(j == 0, gx - 1, gx + 1)
    left = (jnp.where(j == 0, gx - 1, gx), jnp.where(j == 0, 6, 2 * j - 2))
    right = (jnp.where(j == 3, gx + 1, gx), jnp.where(j == 3, 0, 2 * j + 2))
    always = gx >= 0
    regions = (
        (has_left, (left[0], left[1] + c), 0, 128),
        (has_right, (right[0], right[1] + c), 128, 128),
        (always, (gx, 2 * j + 1 - c), 256, 16),
        (has_left, (left[0], left[1] + 1 - c), 272, 16),
        (has_right, (right[0], right[1] + 1 - c), 288, 16),
    )
    facing = (1, 0, 2, 4, 3)
    owners = []
    for group in range(2):
        for m in range(5):
            owner_gy = 4 * c + m if m < 4 else halo_gy
            if group == 0:
                owners.append((owner_gy != gy, owner_gy == gy, (gx, owner_gy)))
            else:
                owners.append((has_other, None, (other_gx, owner_gy)))
    readers = []
    for side in range(2):
        half = own_half if side == 0 else 1 - own_half
        slot = own_slot if side == 0 else 4
        wanted = always if side == 0 else edge
        for p in range(4):
            here = 2 * p + half == gy
            readers.append((wanted & jnp.logical_not(here), wanted & here, (gx, 2 * p + half), slot))
        readers.append((wanted & jnp.logical_not(first), None, (gx - 1, 6 + half), slot + 5))
        readers.append((wanted & jnp.logical_not(last_gx), None, (gx + 1, half), slot + 5))

    rcv1[...] = jnp.zeros_like(rcv1)
    rcv2[...] = jnp.zeros_like(rcv2)
    rcv3[...] = jnp.zeros_like(rcv3)
    rcv4[...] = jnp.zeros_like(rcv4)
    barrier = pltpu.get_barrier_semaphore()

    def greet(there, device):
        @pl.when(there)
        def _():
            pl.semaphore_signal(barrier, inc=1, device_id=device, device_id_type=MESH)

    for there, _, device in owners:
        greet(there, device)
    for there, device, _, _ in regions:
        greet(there, device)
    greetings = jnp.int32(0)
    for there, _, _, _ in readers + list(regions):
        greetings = greetings + there.astype(jnp.int32)

    sent = []

    def send(there, here, device, source, target, phase, at, slot):
        def remote():
            return pltpu.make_async_remote_copy(
                src_ref=source,
                dst_ref=target,
                send_sem=send_sem.at[phase, at],
                recv_sem=recv_sem.at[phase, slot],
                device_id=device,
                device_id_type=MESH,
            )

        @pl.when(there)
        def _():
            remote().start()

        if here is not None:

            @pl.when(here)
            def _():
                pltpu.make_async_copy(source, target, recv_sem.at[phase, slot]).start()

        sent.append((there, remote))

    def receive(there, target, phase, slot):
        @pl.when(there)
        def _():
            pltpu.make_async_copy(target, target, recv_sem.at[phase, slot]).wait()

    raw[...] = jnp.zeros_like(raw)
    nb[...] = jnp.zeros_like(nb)
    tile[...] = jnp.zeros_like(tile)
    x_pick = (iota((SITES, SITES), 0) == iota((SITES, SITES), 1) // 16).astype(F32)
    yz_mask = iota((80, SITES), 0) % 16 == iota((80, SITES), 1) % 16
    for i in range(4):
        fetches[i].wait()
    for y in range(4):
        for axis in range(3):
            raw[axis * 16 + y * 4 : axis * 16 + y * 4 + 4, 0:8] = pos_ref[axis, y]
        raw[48 + y * 4 : 52 + y * 4, 0:8] = occ_ref[y].astype(F32)
        raw[64 + y * 4 : 68 + y * 4, 0:8] = spec_ref[y].astype(F32)
    for x in range(8):
        for y in range(4):
            nb[x * 16 + y * 4 : x * 16 + y * 4 + 4, 0:SLOTS] = nbr_ref[x, y].astype(F32)
    spread = jnp.where(yz_mask, dot_exact(raw[...], x_pick), 0.0)
    for f in range(5):
        tile[f : f + 1, :] = jnp.sum(spread[f * 16 : f * 16 + 16], axis=0, keepdims=True)
    tile[8:24, :] = nb[...].T[0:16]

    pl.semaphore_wait(barrier, greetings)
    for at, (there, here, device, slot) in enumerate(readers):
        rows = 24 if at < 4 else 8
        send(there, here, device, tile.at[0:rows], rcv1.at[slot, 0:rows], 0, at, slot)

    rows = iota((GHOSTS, SITES), 0)
    y_strip = 14 * (1 - c)
    strip = rows % 16 // 8 * 64 + (y_strip + rows % 8 // 4) * 4 + rows % 4
    hit = jnp.where(rows < 256, rows % 128, strip) == iota((GHOSTS, SITES), 1)
    ps[...] = jnp.where(hit, 1.0, 0.0).astype(BF16)
    for i in range(4, 15):
        fetches[i].wait()
    lifted_table = dot(emb_ref[...], up_ref[0]).astype(BF16).astype(F32)
    s_acc[...] = jnp.zeros_like(s_acc)
    geo[...] = jnp.zeros_like(geo)

    for slot in range(10):
        rows = 24 if slot < 4 else 8
        receive(always if slot < 5 else has_other, rcv1.at[slot, 0:rows], 0, slot)

    lane = iota((8, SITES), 1)
    no = gx < 0
    slabs = (
        (2 * j, no),
        (jnp.where(j == 0, 6, 2 * j - 2), j == 0),
        (jnp.where(j == 3, 0, 2 * j + 2), j == 3),
    )
    y_halo = 2 * c

    def slab_shift(x0, m, x):
        return lax.rem(2 * SITES + x * 64 + m * 16 - (x0 + x) * 16, SITES)

    def strip_shift(x0, r, x):
        return lax.rem(2 * SITES + r * 16 + x * 8 - (x0 + x) * 16 - y_halo * 4, SITES)

    for r, (x0, other) in enumerate(slabs):
        out = jnp.zeros((8, SITES), F32)
        for m in range(4):
            source = rcv1[m, 0:8]
            if r > 0:
                source = jnp.where(other, rcv1[5 + m, 0:8], source)
            for x in range(2):
                moved = pltpu.roll(source, slab_shift(x0, m, x), 1)
                out = jnp.where(lane // 16 == x * 4 + m, moved, out)
        geo[:, r * SITES : (r + 1) * SITES] = out
    out = jnp.zeros((8, SITES), F32)
    for r, (x0, other) in enumerate(slabs):
        source = rcv1[4, 0:8]
        if r > 0:
            source = jnp.where(other, rcv1[9, 0:8], source)
        for x in range(2):
            moved = pltpu.roll(source, strip_shift(x0, r, x), 1)
            out = jnp.where(lane // 8 == r * 2 + x, moved, out)
    geo[:, 3 * SITES : 4 * SITES] = out

    lane16 = iota((16, SITES), 1)
    index = jnp.zeros((16, SITES), F32)
    for m in range(4):
        for x in range(2):
            moved = pltpu.roll(rcv1[m, 8:24], slab_shift(2 * j, m, x), 1)
            index = jnp.where(lane16 // 16 == x * 4 + m, moved, index)
    index = index.astype(jnp.int32)
    z = index & 3
    y = ((index >> 2) & 7) - 2 + lane16 // 16 % 4 * 4
    x = (index >> 5) - 2 - 2 * j
    inner = (x & 1) * 64 + y * 4 + z + jnp.where(x < 0, LEFT, jnp.where(x > 1, RIGHT, 0))
    outer = (x & 1) * 8 + (y & 1) * 4 + z + jnp.where(x < 0, ACROSS + 16, jnp.where(x > 1, ACROSS + 32, ACROSS))
    beyond = jnp.where(c == 0, y - 16, -1 - y) >= 0
    place = jnp.where((y >= 0) & (y < 16), inner, jnp.where(beyond, outer, -1))
    ext_row = iota((EXT, SITES), 0)
    for k in range(SLOTS):
        hit = ext_row == place[k : k + 1]
        oh[:, k * SITES : (k + 1) * SITES] = jnp.where(hit, 1.0, 0.0).astype(BF16)

    gathered = dot(split3(geo[:, 0:EXT]), oh[...])
    gathered = gathered[0:8] + gathered[8:16] + gathered[16:24]
    for k in range(SLOTS):
        gs[k * 8 : k * 8 + 8, :] = gathered[:, k * SITES : (k + 1) * SITES]
    ext_hot = (geo[4:5, 0:EXT].astype(jnp.int32) == iota((16, EXT), 0)).astype(F32)
    u0 = dot(lifted_table, ext_hot[0:10], TN).astype(BF16)
    u[0] = dot(u0, oh[...])

    present = geo[3:4, 0:SITES]
    own_hot = ext_hot[:, 0:SITES]
    for layer in range(LAYERS):
        for k in range(4):
            mix[layer, k] = dot_exact(pw_ref[layer, :, k, :], own_hot[0:10], TN)
    h0 = dot(emb_ref[...].astype(F32), own_hot[0:10], TN) * present

    def rows_of(ref, m):
        return ref[pl.ds(m, SLOTS, stride=8), :]

    disp = [rows_of(gs, c) - geo[c : c + 1, 0:SITES] for c in range(3)]
    w = rows_of(gs, 3) * present
    squared = disp[0] * disp[0] + disp[1] * disp[1] + disp[2] * disp[2]
    dist = jnp.sqrt(jnp.where(w > 0, squared, 1.0))
    inv = 1.0 / dist
    nx, ny, nz = [c * inv for c in disp]
    scaled = jnp.minimum(dist * (1.0 / CUTOFF), 1.0)
    u2 = scaled * scaled
    u5 = u2 * u2 * scaled
    u6 = u5 * scaled
    env = 1.0 - 28.0 * u6 + 48.0 * u6 * scaled - 21.0 * u6 * u2
    env = jnp.where(scaled < 1.0, env, 0.0)
    gap = 1.0 - scaled
    slope = (-168.0 / CUTOFF) * u5 * gap * gap
    env_w = env * w
    slope_w = slope * w
    ye_scale = FACTOR * env_w
    harmonics = [
        ROOT3 * nx,
        ROOT3 * ny,
        ROOT3 * nz,
        ROOT15 * nx * ny,
        ROOT15 * ny * nz,
        0.5 * ROOT5 * (3.0 * nz * nz - 1.0),
        ROOT15 * nx * nz,
        0.5 * ROOT15 * (nx * nx - ny * ny),
    ]
    ye[0, 0:SLOTS] = ye_scale
    for m in range(8):
        ye[m + 1, 0:SLOTS] = ye_scale * harmonics[m]
    theta = math.pi * scaled
    sin1 = jnp.sin(theta)
    cos1 = jnp.cos(theta)
    twice = 2.0 * cos1
    sin_before, cos_before = jnp.zeros_like(sin1), jnp.ones_like(cos1)
    sin_m, cos_m = sin1, cos1
    amplitude = math.sqrt(2.0 / CUTOFF) * inv
    for m in range(BES):
        value = amplitude * sin_m
        bs[pl.ds(m, SLOTS, stride=8), :] = value
        bd[m, 0:SLOTS] = amplitude * ((m + 1) * math.pi / CUTOFF) * cos_m - value * inv
        sin_m, sin_before = twice * sin_m - sin_before, sin_m
        cos_m, cos_before = twice * cos_m - cos_before, cos_m

    def radial(layer):
        hidden = jnp.concatenate([bs[k * 8 : k * 8 + 8, :] for k in range(SLOTS)], axis=1)
        hidden = hidden.astype(BF16)
        for step, ref in enumerate((w1_ref, w2_ref, w3_ref)):
            z = dot(ref[layer], hidden, TN)
            g, slope_g = silu_parts(z)
            dsilu[layer, step] = slope_g
            hidden = g.astype(BF16)
        q[layer] = dot(w4_ref[layer], hidden, TN)

    def aggregate(layer):
        def body(block, carry):
            c0 = pl.multiple_of(block * 32, 32)
            acc = [jnp.zeros((32, SITES), F32) for _ in range(9)]
            for k in range(SLOTS):
                lanes = slice(k * SITES, (k + 1) * SITES)
                uk = u[layer, pl.ds(c0, 32), lanes]
                v = [q[layer, pl.ds(L * CH + c0, 32), lanes] * uk for L in range(3)]
                for m in range(9):
                    degree = 0 if m == 0 else (1 if m < 4 else 2)
                    acc[m] = acc[m] + ye[m, k : k + 1, :] * v[degree]
            for m in range(9):
                a[layer, m, pl.ds(c0, 32), :] = acc[m]
            p = [mix[layer, j, pl.ds(c0, 32), :] for j in range(4)]
            first = acc[1] * acc[1] + acc[2] * acc[2] + acc[3] * acc[3]
            second = acc[4] * acc[4] + acc[5] * acc[5] + acc[6] * acc[6]
            second = second + acc[7] * acc[7] + acc[8] * acc[8]
            result = p[0] * acc[0] + p[1] * acc[0] * acc[0] + p[2] * first + p[3] * second
            msg[pl.ds(c0, 32), :] = result.astype(BF16)
            return carry

        lax.fori_loop(0, CH // 32, body, 0)

    def aggregate_back(layer, msg_grad_ref, with_du):
        def body(block, carry):
            c0 = pl.multiple_of(block * 32, 32)
            g = msg_grad_ref[pl.ds(c0, 32), :]
            p = [mix[layer, j, pl.ds(c0, 32), :] for j in range(4)]
            a0 = a[layer, 0, pl.ds(c0, 32), :]
            scale1 = 2.0 * p[2] * g
            scale2 = 2.0 * p[3] * g
            da = [g * (p[0] + 2.0 * p[1] * a0)]
            for m in range(1, 9):
                da.append((scale1 if m < 4 else scale2) * a[layer, m, pl.ds(c0, 32), :])
            for k in range(SLOTS):
                lanes = slice(k * SITES, (k + 1) * SITES)
                uk = u[layer, pl.ds(c0, 32), lanes]
                qk = [q[layer, pl.ds(L * CH + c0, 32), lanes] for L in range(3)]
                v = [one * uk for one in qk]
                dv = [None, None, None]
                for m in range(9):
                    degree = 0 if m == 0 else (1 if m < 4 else 2)
                    term = ye[m, k : k + 1, :] * da[m]
                    dv[degree] = term if dv[degree] is None else dv[degree] + term
                    part = da[m] * v[degree]
                    part = part[0:8] + part[8:16] + part[16:24] + part[24:32]
                    at = (m * SLOTS + k) * 8
                    s_acc[at : at + 8, :] += part
                for L in range(3):
                    dq[pl.ds(L * CH + c0, 32), lanes] = (dv[L] * uk).astype(BF16)
                if with_du:
                    total = dv[0] * qk[0] + dv[1] * qk[1] + dv[2] * qk[2]
                    du[pl.ds(c0, 32), lanes] = total.astype(BF16)
            return carry

        lax.fori_loop(0, CH // 32, body, 0)

    def radial_back(layer):
        grad = dot(w4_ref[layer], dq[...])
        for step, ref in ((2, w3_ref), (1, w2_ref), (0, w1_ref)):
            dz = (grad * dsilu[layer, step]).astype(BF16)
            grad = dot(ref[layer], dz)
        return grad

    radial(0)
    aggregate(0)
    mixed = dot(ow_ref[0], msg[...], TN)
    h1 = (h0 + present * mixed).astype(BF16)
    u1 = dot(up_ref[1], h1, TN).astype(BF16)
    snd2[...] = dot(ps[128:272, :], u1, NT).astype(BF16)
    for r, (there, device, start, size) in enumerate(regions):
        source = snd2.at[0:128] if r < 2 else snd2.at[128:144]
        start = regions[facing[r]][2]
        send(there, None, device, source, rcv2.at[start : start + size], 1, r, facing[r])
    radial(1)
    near = dot(u1, oh[0:SITES, :])
    for r, (there, _, start, size) in enumerate(regions):
        receive(there, rcv2.at[start : start + size], 1, r)
    u[1] = near + dot(rcv2[...], oh[SITES:EXT, :], TN)
    aggregate(1)
    mixed = dot(ow_ref[1], msg[...], TN)
    h2 = (h1.astype(F32) + present * mixed).astype(BF16)

    diagonal = iota((CH, CH), 0) == iota((CH, CH), 1)
    linear = jnp.sum(jnp.where(diagonal, rl_ref[...], 0.0), axis=1, keepdims=True)
    small = iota((16, 16), 0) == iota((16, 16), 1)
    last = jnp.sum(jnp.where(small, rlast_ref[...], 0.0), axis=1, keepdims=True)
    z = dot(rh_ref[...], h2)
    g, slope_g = silu_parts(z)
    energy = jnp.sum(h1.astype(F32) * linear, axis=0, keepdims=True)
    energy = present * (energy + jnp.sum(g * last, axis=0, keepdims=True))
    dz = (present * last * slope_g).astype(BF16)
    dh2 = dot(rh_ref[...], dz, TN)
    dmixed = (present * dh2).astype(BF16)
    message_grad = dot(ow_ref[1], dmixed)
    bm = nb
    bm[...] = message_grad
    aggregate_back(1, bm, True)
    snd3[...] = dot(oh[SITES:EXT, :], du[...], NT).astype(BF16)
    for r, (there, device, start, size) in enumerate(regions):
        target = regions[facing[r]][2]
        source = snd3.at[start : start + size]
        send(there, None, device, source, rcv3.at[target : target + size], 2, r, facing[r])
    near = dot(du[...], oh[0:SITES, :], NT)
    bessel_grad = radial_back(1)
    for r, (there, _, start, size) in enumerate(regions):
        receive(there, rcv3.at[start : start + size], 2, r)
    du1 = near + dot(rcv3[...], ps[...], TN)
    dh1 = dh2 + linear * present + dot(up_ref[1], du1.astype(BF16))
    dmixed = (present * dh1).astype(BF16)
    bm[...] = dot(ow_ref[0], dmixed)
    aggregate_back(0, bm, False)
    bessel_grad = bessel_grad + radial_back(0)

    for k in range(SLOTS):
        gs[k * 8 : k * 8 + 8, :] = bessel_grad[:, k * SITES : (k + 1) * SITES]
    dr = rows_of(gs, 0) * bd[0, 0:SLOTS]
    for m in range(1, BES):
        dr = dr + rows_of(gs, m) * bd[m, 0:SLOTS]

    def total_of(m):
        at = m * SLOTS * 8
        out = s_acc[pl.ds(at, SLOTS, stride=8), :]
        for j in range(1, 8):
            out = out + s_acc[pl.ds(at + j, SLOTS, stride=8), :]
        return FACTOR * out

    sums = [total_of(m) for m in range(9)]
    d_env = sums[0]
    for m in range(8):
        d_env = d_env + sums[m + 1] * harmonics[m]
    dr = dr + d_env * slope_w
    dy = [env_w * one for one in sums[1:]]
    dnx = ROOT3 * dy[0] + ROOT15 * (dy[3] * ny + dy[6] * nz + dy[7] * nx)
    dny = ROOT3 * dy[1] + ROOT15 * (dy[3] * nx + dy[4] * nz - dy[7] * ny)
    dnz = ROOT3 * dy[2] + ROOT15 * (dy[4] * ny + dy[6] * nx) + (3.0 * ROOT5) * dy[5] * nz
    radial_part = dr - inv * (dnx * nx + dny * ny + dnz * nz)
    gs[...] = jnp.zeros_like(gs)
    centre = []
    for axis, (dn, n) in enumerate(((dnx, nx), (dny, ny), (dnz, nz))):
        dd = dn * inv + radial_part * n
        gs[pl.ds(axis, SLOTS, stride=8), :] = dd
        centre.append(jnp.sum(dd, axis=0, keepdims=True))
    edge_grad = jnp.concatenate([gs[k * 8 : k * 8 + 8, :] for k in range(SLOTS)], axis=1)
    scattered = dot(split3(edge_grad), oh[...], NT)
    geo[:, 0:EXT] = scattered[0:8] + scattered[8:16] + scattered[16:24]
    for axis in range(3):
        geo[axis : axis + 1, 0:SITES] = geo[axis : axis + 1, 0:SITES] - centre[axis]
    geo[3:4, 0:SITES] = energy

    for m in range(4):
        tiles = [jnp.zeros((8, SITES), F32) for _ in range(2)]
        for r, (x0, other) in enumerate(slabs):
            for x in range(2):
                moved = pltpu.roll(geo[:, r * SITES : (r + 1) * SITES], lax.rem(SITES - slab_shift(x0, m, x), SITES), 1)
                tiles[0] = jnp.where(lane // 16 == jnp.where(other, -1, x0 + x), moved, tiles[0])
                if r > 0:
                    tiles[1] = jnp.where(lane // 16 == jnp.where(other, x0 + x, -1), moved, tiles[1])
        snd4[m] = tiles[0]
        snd4[5 + m] = tiles[1]
    tiles = [jnp.zeros((8, SITES), F32) for _ in range(2)]
    for r, (x0, other) in enumerate(slabs):
        for x in range(2):
            moved = pltpu.roll(geo[:, 3 * SITES :], lax.rem(SITES - strip_shift(x0, r, x), SITES), 1)
            at = 2 * (x0 + x) + c
            tiles[0] = jnp.where(lane // 8 == jnp.where(other, -1, at), moved, tiles[0])
            tiles[1] = jnp.where(lane // 8 == jnp.where(other, at, -1), moved, tiles[1])
    snd4[4] = tiles[0]
    snd4[9] = tiles[1]
    for at, (there, here, device) in enumerate(owners):
        slot = j if at < 5 else jnp.where(j == 0, 5, 4)
        slot = slot + (6 if at % 5 == 4 else 0)
        send(there, here, device, snd4.at[at], rcv4.at[slot], 3, at, slot)
    for at, (there, here, _, _) in enumerate(readers):
        wanted = there if here is None else there | here
        receive(wanted, rcv4.at[at], 3, at)
    back = rcv4[0]
    for at in range(1, 12):
        back = back + rcv4[at]

    rows = [jnp.broadcast_to(-back[axis : axis + 1], (16, SITES)) for axis in range(3)]
    rows.append(jnp.broadcast_to(back[3:4], (16, SITES)))
    full = jnp.where(yz_mask[0:64], jnp.concatenate(rows, axis=0), 0.0)
    out = dot_exact(full, x_pick, NT)
    for y in range(4):
        for axis in range(3):
            force_ref[axis, y] = out[axis * 16 + y * 4 : axis * 16 + y * 4 + 4, 0:8]
        en_ref[y] = out[48 + y * 4 : 52 + y * 4, 0:8]
    for there, remote in sent:

        @pl.when(there)
        def _():
            remote().wait_send()


def shards(
    positions,
    occupied,
    species,
    neighbours,
    embedding,
    radial_first,
    radial_second,
    radial_third,
    radial_last,
    up_weight,
    product_weight,
    out_weight,
    read_linear,
    read_hidden,
    read_last,
):
    n_gx = lax.axis_size("gx")
    vmem = pl.BlockSpec(memory_space=pltpu.VMEM)
    operands = (
        positions.transpose(0, 2, 3, 1),
        occupied.transpose(1, 2, 0),
        species.transpose(1, 2, 0),
        neighbours,
        embedding,
        radial_first,
        radial_second,
        radial_third,
        radial_last,
        up_weight,
        product_weight,
        out_weight,
        read_linear,
        read_hidden.T,
        read_last.reshape(1, -1),
    )
    energies, forces = pl.pallas_call(
        functools.partial(kernel, n_gx),
        out_shape=(
            jax.ShapeDtypeStruct((4, 4, 8), F32),
            jax.ShapeDtypeStruct((3, 4, 4, 8), F32),
        ),
        in_specs=[pl.BlockSpec(memory_space=pltpu.HBM)] * 15,
        out_specs=(vmem, vmem),
        scratch_shapes=[pltpu.VMEM(one.shape, one.dtype) for one in operands]
        + [
            pltpu.VMEM((80, SITES), F32),
            pltpu.VMEM((SITES, SITES), F32),
            pltpu.VMEM((24, SITES), F32),
            pltpu.VMEM((8, 4 * SITES), F32),
            pltpu.VMEM((GHOSTS, SITES), BF16),
            pltpu.VMEM((EXT, EDGES), BF16),
            pltpu.VMEM((10, 24, SITES), F32),
            pltpu.VMEM((144, CH), BF16),
            pltpu.VMEM((GHOSTS, CH), BF16),
            pltpu.VMEM((GHOSTS, CH), BF16),
            pltpu.VMEM((GHOSTS, CH), BF16),
            pltpu.VMEM((10, 8, SITES), F32),
            pltpu.VMEM((12, 8, SITES), F32),
            pltpu.VMEM((SLOTS * 8, SITES), F32),
            pltpu.VMEM((SLOTS * 8, SITES), F32),
            pltpu.VMEM((9, 16, SITES), F32),
            pltpu.VMEM((BES, 16, SITES), F32),
            pltpu.VMEM((LAYERS, 4, CH, SITES), F32),
            pltpu.VMEM((LAYERS, 3, RAD, EDGES), F32),
            pltpu.VMEM((LAYERS, 3 * CH, EDGES), F32),
            pltpu.VMEM((LAYERS, CH, EDGES), F32),
            pltpu.VMEM((LAYERS, 9, CH, SITES), F32),
            pltpu.VMEM((CH, SITES), BF16),
            pltpu.VMEM((3 * CH, EDGES), BF16),
            pltpu.VMEM((CH, EDGES), BF16),
            pltpu.VMEM((9 * SLOTS * 8, SITES), F32),
            pltpu.SemaphoreType.DMA((15,)),
            pltpu.SemaphoreType.DMA((4, 12)),
            pltpu.SemaphoreType.DMA((4, 12)),
        ],
        compiler_params=pltpu.CompilerParams(
            collective_id=0, has_side_effects=True, vmem_limit_bytes=60 * 1024 * 1024
        ),
    )(*operands)
    return energies.transpose(2, 0, 1), forces.transpose(0, 3, 1, 2)


def solution(mesh):
    in_specs = (
        P(None, "gx", "gy", None),
        P("gx", "gy", None),
        P("gx", "gy", None),
        P("gx", "gy", None, None),
        P(),
        P(),
        P(),
        P(),
        P(),
        P(),
        P(),
        P(),
        P(),
        P(),
        P(),
    )
    out_specs = (P("gx", "gy", None), P(None, "gx", "gy", None))
    return jax.shard_map(shards, mesh=mesh, in_specs=in_specs, out_specs=out_specs, check_vma=False)
```

```python
import functools
import math

import jax
import jax.numpy as jnp
from jax import lax
from jax.experimental import pallas as pl
from jax.experimental.pallas import tpu as pltpu
from jax.sharding import PartitionSpec as P

F32 = jnp.float32
BF16 = jnp.bfloat16
MESH = pl.DeviceIdType.MESH
CUTOFF = 5.0
SLOTS = 12
SITES = 128
EDGES = SITES * SLOTS
GHOSTS = 304
EXT = SITES + GHOSTS
CH = 128
RAD = 64
BES = 8
LAYERS = 2

LEFT, RIGHT, ACROSS = 128, 256, 384

NT = (((1,), (1,)), ((), ()))
TN = (((0,), (0,)), ((), ()))
NN = (((1,), (0,)), ((), ()))


def dot(a, b, dims=NN):
    return lax.dot_general(a, b, dims, preferred_element_type=F32)


def dot_exact(a, b, dims=NN):
    return lax.dot_general(a, b, dims, preferred_element_type=F32, precision=lax.Precision.HIGHEST)


def iota(shape, dim):
    return lax.broadcasted_iota(jnp.int32, shape, dim)


def split3(x):
    high = x.astype(BF16).astype(F32)
    rest = x - high
    middle = rest.astype(BF16).astype(F32)
    return jnp.concatenate([high, middle, rest - middle], axis=0).astype(BF16)


def split2(x):
    high = x.astype(BF16).astype(F32)
    return jnp.concatenate([high, x - high], axis=0).astype(BF16)


def silu_parts(z):
    s = 0.5 + 0.5 * jnp.tanh(0.5 * z)
    g = z * s
    return g, s + g * (1.0 - s)


ROOT3 = math.sqrt(3.0)
ROOT5 = math.sqrt(5.0)
ROOT15 = math.sqrt(15.0)
FACTOR = 1.0 / math.sqrt(SLOTS)


def kernel(n_gx, *refs):
    inputs, refs = refs[:15], refs[15:]
    (en_ref, force_ref), refs = refs[:2], refs[2:]
    held, refs = refs[:15], refs[15:]
    (raw, nb, tile, geo, ps, oh, rcv1, snd2, rcv2, snd3, rcv3, snd4, rcv4), refs = refs[:13], refs[13:]
    (gs, bs, ye, bd, mix, dsilu, q, u, a, msg, dq, du, s_acc), refs = refs[:13], refs[13:]
    fetch_sem, send_sem, recv_sem = refs
    (pos_ref, occ_ref, spec_ref, nbr_ref, emb_ref, w1_ref, w2_ref, w3_ref, w4_ref), more = held[:9], held[9:]
    up_ref, pw_ref, ow_ref, rl_ref, rh_ref, rlast_ref = more

    fetches = []
    for i in range(15):
        fetch = pltpu.make_async_copy(inputs[i], held[i], fetch_sem.at[i])
        fetch.start()
        fetches.append(fetch)

    gx = lax.axis_index("gx")
    gy = lax.axis_index("gy")

    def computed_at(x_block):
        return jnp.where(x_block // 16 % 2 == 1, x_block // 16 * 16 + 12 - x_block // 4 % 4 * 4 + x_block % 4, x_block)

    block = computed_at(gx)
    j, c = gy // 2, gy % 2
    own_half, own_slot = gy // 4, gy % 4
    edge = (gy == 3) | (gy == 4)
    halo_gy = 4 - c
    first, last_gx = gx == 0, gx == n_gx - 1
    has_left = jnp.logical_not((j == 0) & (block == 0))
    has_right = jnp.logical_not((j == 3) & (block == n_gx - 1))
    has_other = ((j == 0) | (j == 3)) & has_left & has_right
    other_gx = jnp.where(j == 0, block - 1, block + 1)
    left = (computed_at(jnp.where(j == 0, block - 1, block)), jnp.where(j == 0, 6, 2 * j - 2))
    right = (computed_at(jnp.where(j == 3, block + 1, block)), jnp.where(j == 3, 0, 2 * j + 2))
    always = gx >= 0
    regions = (
        (has_left, (left[0], left[1] + c), 0, 128),
        (has_right, (right[0], right[1] + c), 128, 128),
        (always, (gx, 2 * j + 1 - c), 256, 16),
        (has_left, (left[0], left[1] + 1 - c), 272, 16),
        (has_right, (right[0], right[1] + 1 - c), 288, 16),
    )
    facing = (1, 0, 2, 4, 3)
    owners = []
    for group in range(2):
        for m in range(5):
            owner_gy = 4 * c + m if m < 4 else halo_gy
            if group == 0:
                here = (owner_gy == gy) & (block == gx)
                owners.append((jnp.logical_not(here), here, (block, owner_gy)))
            else:
                owners.append((has_other, None, (other_gx, owner_gy)))
    readers = []
    for side in range(2):
        half = own_half if side == 0 else 1 - own_half
        slot = own_slot if side == 0 else 4
        wanted = always if side == 0 else edge
        for p in range(4):
            here = (2 * p + half == gy) & (block == gx)
            readers.append((wanted & jnp.logical_not(here), wanted & here, (computed_at(gx), 2 * p + half), slot))
        readers.append((wanted & jnp.logical_not(first), None, (computed_at(gx - 1), 6 + half), slot + 5))
        readers.append((wanted & jnp.logical_not(last_gx), None, (computed_at(gx + 1), half), slot + 5))

    rcv1[...] = jnp.zeros_like(rcv1)
    rcv2[...] = jnp.zeros_like(rcv2)
    rcv3[...] = jnp.zeros_like(rcv3)
    rcv4[...] = jnp.zeros_like(rcv4)
    barrier = pltpu.get_barrier_semaphore()

    def greet(there, device):
        @pl.when(there)
        def _():
            pl.semaphore_signal(barrier, inc=1, device_id=device, device_id_type=MESH)

    for there, _, device in owners:
        greet(there, device)
    for there, device, _, _ in regions:
        greet(there, device)
    greetings = jnp.int32(0)
    for there, _, _, _ in readers + list(regions):
        greetings = greetings + there.astype(jnp.int32)

    sent = []

    def send(there, here, device, source, target, phase, at, slot):
        def remote():
            return pltpu.make_async_remote_copy(
                src_ref=source,
                dst_ref=target,
                send_sem=send_sem.at[phase, at],
                recv_sem=recv_sem.at[phase, slot],
                device_id=device,
                device_id_type=MESH,
            )

        @pl.when(there)
        def _():
            remote().start()

        if here is not None:

            @pl.when(here)
            def _():
                pltpu.make_async_copy(source, target, recv_sem.at[phase, slot]).start()

        sent.append((there, remote))

    def receive(there, target, phase, slot):
        @pl.when(there)
        def _():
            pltpu.make_async_copy(target, target, recv_sem.at[phase, slot]).wait()

    raw[...] = jnp.zeros_like(raw)
    nb[...] = jnp.zeros_like(nb)
    tile[...] = jnp.zeros_like(tile)
    x_pick = (iota((SITES, SITES), 0) == iota((SITES, SITES), 1) // 16).astype(F32)
    yz_mask = iota((80, SITES), 0) % 16 == iota((80, SITES), 1) % 16
    for i in range(4):
        fetches[i].wait()
    for y in range(4):
        for axis in range(3):
            raw[axis * 16 + y * 4 : axis * 16 + y * 4 + 4, 0:8] = pos_ref[axis, y]
        raw[48 + y * 4 : 52 + y * 4, 0:8] = occ_ref[y].astype(F32)
        raw[64 + y * 4 : 68 + y * 4, 0:8] = spec_ref[y].astype(F32)
    for x in range(8):
        for y in range(4):
            nb[x * 16 + y * 4 : x * 16 + y * 4 + 4, 0:SLOTS] = nbr_ref[x, y].astype(F32)
    spread = jnp.where(yz_mask, dot_exact(raw[...], x_pick), 0.0)
    for f in range(5):
        tile[f : f + 1, :] = jnp.sum(spread[f * 16 : f * 16 + 16], axis=0, keepdims=True)
    tile[8:24, :] = nb[...].T[0:16]

    pl.semaphore_wait(barrier, greetings)
    for at in (4, 5, 0, 1, 2, 3, 10, 11, 6, 7, 8, 9):
        there, here, device, slot = readers[at]
        rows = 24 if at < 4 else 8
        send(there, here, device, tile.at[0:rows], rcv1.at[slot, 0:rows], 0, at, slot)

    rows = iota((GHOSTS, SITES), 0)
    y_strip = 14 * (1 - c)
    strip = rows % 16 // 8 * 64 + (y_strip + rows % 8 // 4) * 4 + rows % 4
    hit = jnp.where(rows < 256, rows % 128, strip) == iota((GHOSTS, SITES), 1)
    ps[...] = jnp.where(hit, 1.0, 0.0).astype(BF16)
    for i in range(4, 15):
        fetches[i].wait()
    lifted_table = dot(emb_ref[...], up_ref[0]).astype(BF16).astype(F32)
    s_acc[...] = jnp.zeros_like(s_acc)
    geo[...] = jnp.zeros_like(geo)

    for slot in range(10):
        rows = 24 if slot < 4 else 8
        receive(always if slot < 5 else has_other, rcv1.at[slot, 0:rows], 0, slot)

    lane = iota((8, SITES), 1)
    no = gx < 0
    slabs = (
        (2 * j, no),
        (jnp.where(j == 0, 6, 2 * j - 2), j == 0),
        (jnp.where(j == 3, 0, 2 * j + 2), j == 3),
    )
    y_halo = 2 * c

    def slab_shift(x0, m, x):
        return lax.rem(2 * SITES + x * 64 + m * 16 - (x0 + x) * 16, SITES)

    def strip_shift(x0, r, x):
        return lax.rem(2 * SITES + r * 16 + x * 8 - (x0 + x) * 16 - y_halo * 4, SITES)

    for r, (x0, other) in enumerate(slabs):
        out = jnp.zeros((8, SITES), F32)
        for m in range(4):
            source = rcv1[m, 0:8]
            if r > 0:
                source = jnp.where(other, rcv1[5 + m, 0:8], source)
            for x in range(2):
                moved = pltpu.roll(source, slab_shift(x0, m, x), 1)
                out = jnp.where(lane // 16 == x * 4 + m, moved, out)
        geo[:, r * SITES : (r + 1) * SITES] = out
    out = jnp.zeros((8, SITES), F32)
    for r, (x0, other) in enumerate(slabs):
        source = rcv1[4, 0:8]
        if r > 0:
            source = jnp.where(other, rcv1[9, 0:8], source)
        for x in range(2):
            moved = pltpu.roll(source, strip_shift(x0, r, x), 1)
            out = jnp.where(lane // 8 == r * 2 + x, moved, out)
    geo[:, 3 * SITES : 4 * SITES] = out

    lane16 = iota((16, SITES), 1)
    index = jnp.zeros((16, SITES), F32)
    for m in range(4):
        for x in range(2):
            moved = pltpu.roll(rcv1[m, 8:24], slab_shift(2 * j, m, x), 1)
            index = jnp.where(lane16 // 16 == x * 4 + m, moved, index)
    index = index.astype(jnp.int32)
    z = index & 3
    y = ((index >> 2) & 7) - 2 + lane16 // 16 % 4 * 4
    x = (index >> 5) - 2 - 2 * j
    inner = (x & 1) * 64 + y * 4 + z + jnp.where(x < 0, LEFT, jnp.where(x > 1, RIGHT, 0))
    outer = (x & 1) * 8 + (y & 1) * 4 + z + jnp.where(x < 0, ACROSS + 16, jnp.where(x > 1, ACROSS + 32, ACROSS))
    beyond = jnp.where(c == 0, y - 16, -1 - y) >= 0
    place = jnp.where((y >= 0) & (y < 16), inner, jnp.where(beyond, outer, -1))
    ext_row = iota((EXT, SITES), 0)
    for k in range(SLOTS):
        hit = ext_row == place[k : k + 1]
        oh[:, k * SITES : (k + 1) * SITES] = jnp.where(hit, 1.0, 0.0).astype(BF16)

    gathered = dot(split3(geo[:, 0:EXT]), oh[...])
    gathered = gathered[0:8] + gathered[8:16] + gathered[16:24]
    for k in range(SLOTS):
        gs[k * 8 : k * 8 + 8, :] = gathered[:, k * SITES : (k + 1) * SITES]
    ext_hot = (geo[4:5, 0:EXT].astype(jnp.int32) == iota((16, EXT), 0)).astype(F32)
    u0 = dot(lifted_table, ext_hot[0:10], TN).astype(BF16)
    u[0] = dot(u0, oh[...])

    present = geo[3:4, 0:SITES]
    own_hot = ext_hot[:, 0:SITES]

    def species_weights(layer):
        for k in range(4):
            mix[layer, k] = dot_exact(pw_ref[layer, :, k, :], own_hot[0:10], TN)

    species_weights(0)
    h0 = dot(emb_ref[...].astype(F32), own_hot[0:10], TN) * present

    def rows_of(ref, m):
        return ref[pl.ds(m, SLOTS, stride=8), :]

    disp = [rows_of(gs, c) - geo[c : c + 1, 0:SITES] for c in range(3)]
    w = rows_of(gs, 3) * present
    squared = disp[0] * disp[0] + disp[1] * disp[1] + disp[2] * disp[2]
    dist = jnp.sqrt(jnp.where(w > 0, squared, 1.0))
    inv = 1.0 / dist
    nx, ny, nz = [c * inv for c in disp]
    scaled = jnp.minimum(dist * (1.0 / CUTOFF), 1.0)
    u2 = scaled * scaled
    u5 = u2 * u2 * scaled
    u6 = u5 * scaled
    env = 1.0 - 28.0 * u6 + 48.0 * u6 * scaled - 21.0 * u6 * u2
    env = jnp.where(scaled < 1.0, env, 0.0)
    gap = 1.0 - scaled
    slope = (-168.0 / CUTOFF) * u5 * gap * gap
    env_w = env * w
    slope_w = slope * w
    ye_scale = FACTOR * env_w
    harmonics = [
        ROOT3 * nx,
        ROOT3 * ny,
        ROOT3 * nz,
        ROOT15 * nx * ny,
        ROOT15 * ny * nz,
        0.5 * ROOT5 * (3.0 * nz * nz - 1.0),
        ROOT15 * nx * nz,
        0.5 * ROOT15 * (nx * nx - ny * ny),
    ]
    ye[0, 0:SLOTS] = ye_scale
    for m in range(8):
        ye[m + 1, 0:SLOTS] = ye_scale * harmonics[m]
    theta = math.pi * scaled
    sin1 = jnp.sin(theta)
    cos1 = jnp.cos(theta)
    twice = 2.0 * cos1
    sin_before, cos_before = jnp.zeros_like(sin1), jnp.ones_like(cos1)
    sin_m, cos_m = sin1, cos1
    amplitude = math.sqrt(2.0 / CUTOFF) * inv
    for m in range(BES):
        value = amplitude * sin_m
        bs[pl.ds(m, SLOTS, stride=8), :] = value
        bd[m, 0:SLOTS] = amplitude * ((m + 1) * math.pi / CUTOFF) * cos_m - value * inv
        sin_m, sin_before = twice * sin_m - sin_before, sin_m
        cos_m, cos_before = twice * cos_m - cos_before, cos_m

    def radial(layer):
        hidden = jnp.concatenate([bs[k * 8 : k * 8 + 8, :] for k in range(SLOTS)], axis=1)
        hidden = hidden.astype(BF16)
        for step, ref in enumerate((w1_ref, w2_ref, w3_ref)):
            z = dot(ref[layer], hidden, TN)
            g, slope_g = silu_parts(z)
            dsilu[layer, step] = slope_g
            hidden = g.astype(BF16)
        q[layer] = dot(w4_ref[layer], hidden, TN)

    def aggregate(layer):
        def body(block, carry):
            c0 = pl.multiple_of(block * 32, 32)
            acc = [jnp.zeros((32, SITES), F32) for _ in range(9)]
            for k in range(SLOTS):
                lanes = slice(k * SITES, (k + 1) * SITES)
                uk = u[layer, pl.ds(c0, 32), lanes]
                v = [q[layer, pl.ds(L * CH + c0, 32), lanes] * uk for L in range(3)]
                for m in range(9):
                    degree = 0 if m == 0 else (1 if m < 4 else 2)
                    acc[m] = acc[m] + ye[m, k : k + 1, :] * v[degree]
            for m in range(9):
                a[layer, m, pl.ds(c0, 32), :] = acc[m]
            p = [mix[layer, j, pl.ds(c0, 32), :] for j in range(4)]
            first = acc[1] * acc[1] + acc[2] * acc[2] + acc[3] * acc[3]
            second = acc[4] * acc[4] + acc[5] * acc[5] + acc[6] * acc[6]
            second = second + acc[7] * acc[7] + acc[8] * acc[8]
            result = p[0] * acc[0] + p[1] * acc[0] * acc[0] + p[2] * first + p[3] * second
            msg[pl.ds(c0, 32), :] = result.astype(BF16)
            return carry

        lax.fori_loop(0, CH // 32, body, 0)

    def aggregate_back(layer, msg_grad_ref, with_du):
        def body(block, carry):
            c0 = pl.multiple_of(block * 32, 32)
            g = msg_grad_ref[pl.ds(c0, 32), :]
            p = [mix[layer, j, pl.ds(c0, 32), :] for j in range(4)]
            a0 = a[layer, 0, pl.ds(c0, 32), :]
            scale1 = 2.0 * p[2] * g
            scale2 = 2.0 * p[3] * g
            da = [g * (p[0] + 2.0 * p[1] * a0)]
            for m in range(1, 9):
                da.append((scale1 if m < 4 else scale2) * a[layer, m, pl.ds(c0, 32), :])
            for k in range(SLOTS):
                lanes = slice(k * SITES, (k + 1) * SITES)
                uk = u[layer, pl.ds(c0, 32), lanes]
                qk = [q[layer, pl.ds(L * CH + c0, 32), lanes] for L in range(3)]
                v = [one * uk for one in qk]
                dv = [None, None, None]
                for m in range(9):
                    degree = 0 if m == 0 else (1 if m < 4 else 2)
                    term = ye[m, k : k + 1, :] * da[m]
                    dv[degree] = term if dv[degree] is None else dv[degree] + term
                    part = da[m] * v[degree]
                    part = part[0:8] + part[8:16] + part[16:24] + part[24:32]
                    at = (m * SLOTS + k) * 8
                    s_acc[at : at + 8, :] += part
                for L in range(3):
                    dq[pl.ds(L * CH + c0, 32), lanes] = (dv[L] * uk).astype(BF16)
                if with_du:
                    total = dv[0] * qk[0] + dv[1] * qk[1] + dv[2] * qk[2]
                    du[pl.ds(c0, 32), lanes] = total.astype(BF16)
            return carry

        lax.fori_loop(0, CH // 32, body, 0)

    def radial_back(layer):
        grad = dot(w4_ref[layer], dq[...])
        for step, ref in ((2, w3_ref), (1, w2_ref), (0, w1_ref)):
            dz = (grad * dsilu[layer, step]).astype(BF16)
            grad = dot(ref[layer], dz)
        return grad

    radial(0)
    aggregate(0)
    mixed = dot(ow_ref[0], msg[...], TN)
    h1 = (h0 + present * mixed).astype(BF16)
    u1 = dot(up_ref[1], h1, TN).astype(BF16)
    snd2[...] = dot(ps[128:272, :], u1, NT).astype(BF16)
    for r, (there, device, start, size) in enumerate(regions):
        source = snd2.at[0:128] if r < 2 else snd2.at[128:144]
        start = regions[facing[r]][2]
        send(there, None, device, source, rcv2.at[start : start + size], 1, r, facing[r])
    species_weights(1)
    radial(1)
    near = dot(u1, oh[0:SITES, :])
    for r, (there, _, start, size) in enumerate(regions):
        receive(there, rcv2.at[start : start + size], 1, r)
    u[1] = near + dot(rcv2[...], oh[SITES:EXT, :], TN)
    aggregate(1)
    mixed = dot(ow_ref[1], msg[...], TN)
    h2 = (h1.astype(F32) + present * mixed).astype(BF16)

    diagonal = iota((CH, CH), 0) == iota((CH, CH), 1)
    linear = jnp.sum(jnp.where(diagonal, rl_ref[...], 0.0), axis=1, keepdims=True)
    small = iota((16, 16), 0) == iota((16, 16), 1)
    last = jnp.sum(jnp.where(small, rlast_ref[...], 0.0), axis=1, keepdims=True)
    z = dot(rh_ref[...], h2)
    g, slope_g = silu_parts(z)
    energy = jnp.sum(h1.astype(F32) * linear, axis=0, keepdims=True)
    energy = present * (energy + jnp.sum(g * last, axis=0, keepdims=True))
    dz = (present * last * slope_g).astype(BF16)
    dh2 = dot(rh_ref[...], dz, TN)
    dmixed = (present * dh2).astype(BF16)
    message_grad = dot(ow_ref[1], dmixed)
    bm = nb
    bm[...] = message_grad
    aggregate_back(1, bm, True)
    snd3[...] = dot(oh[SITES:EXT, :], du[...], NT).astype(BF16)
    for r, (there, device, start, size) in enumerate(regions):
        target = regions[facing[r]][2]
        source = snd3.at[start : start + size]
        send(there, None, device, source, rcv3.at[target : target + size], 2, r, facing[r])
    near = dot(du[...], oh[0:SITES, :], NT)
    bessel_grad = radial_back(1)
    for r, (there, _, start, size) in enumerate(regions):
        receive(there, rcv3.at[start : start + size], 2, r)
    du1 = near + dot(rcv3[...], ps[...], TN)
    dh1 = dh2 + linear * present + dot(up_ref[1], du1.astype(BF16))
    dmixed = (present * dh1).astype(BF16)
    bm[...] = dot(ow_ref[0], dmixed)
    aggregate_back(0, bm, False)
    bessel_grad = bessel_grad + radial_back(0)

    for k in range(SLOTS):
        gs[k * 8 : k * 8 + 8, :] = bessel_grad[:, k * SITES : (k + 1) * SITES]
    dr = rows_of(gs, 0) * bd[0, 0:SLOTS]
    for m in range(1, BES):
        dr = dr + rows_of(gs, m) * bd[m, 0:SLOTS]

    def total_of(m):
        at = m * SLOTS * 8
        out = s_acc[pl.ds(at, SLOTS, stride=8), :]
        for j in range(1, 8):
            out = out + s_acc[pl.ds(at + j, SLOTS, stride=8), :]
        return FACTOR * out

    sums = [total_of(m) for m in range(9)]
    d_env = sums[0]
    for m in range(8):
        d_env = d_env + sums[m + 1] * harmonics[m]
    dr = dr + d_env * slope_w
    dy = [env_w * one for one in sums[1:]]
    dnx = ROOT3 * dy[0] + ROOT15 * (dy[3] * ny + dy[6] * nz + dy[7] * nx)
    dny = ROOT3 * dy[1] + ROOT15 * (dy[3] * nx + dy[4] * nz - dy[7] * ny)
    dnz = ROOT3 * dy[2] + ROOT15 * (dy[4] * ny + dy[6] * nx) + (3.0 * ROOT5) * dy[5] * nz
    radial_part = dr - inv * (dnx * nx + dny * ny + dnz * nz)
    gs[...] = jnp.zeros_like(gs)
    centre = []
    for axis, (dn, n) in enumerate(((dnx, nx), (dny, ny), (dnz, nz))):
        dd = dn * inv + radial_part * n
        gs[pl.ds(axis, SLOTS, stride=8), :] = dd
        centre.append(jnp.sum(dd, axis=0, keepdims=True))
    edge_grad = jnp.concatenate([gs[k * 8 : k * 8 + 8, :] for k in range(SLOTS)], axis=1)
    scattered = dot(split3(edge_grad), oh[...], NT)
    geo[:, 0:EXT] = scattered[0:8] + scattered[8:16] + scattered[16:24]
    for axis in range(3):
        geo[axis : axis + 1, 0:SITES] = geo[axis : axis + 1, 0:SITES] - centre[axis]
    geo[3:4, 0:SITES] = energy

    for m in range(4):
        tiles = [jnp.zeros((8, SITES), F32) for _ in range(2)]
        for r, (x0, other) in enumerate(slabs):
            for x in range(2):
                moved = pltpu.roll(geo[:, r * SITES : (r + 1) * SITES], lax.rem(SITES - slab_shift(x0, m, x), SITES), 1)
                tiles[0] = jnp.where(lane // 16 == jnp.where(other, -1, x0 + x), moved, tiles[0])
                if r > 0:
                    tiles[1] = jnp.where(lane // 16 == jnp.where(other, x0 + x, -1), moved, tiles[1])
        snd4[m] = tiles[0]
        snd4[5 + m] = tiles[1]
    tiles = [jnp.zeros((8, SITES), F32) for _ in range(2)]
    for r, (x0, other) in enumerate(slabs):
        for x in range(2):
            moved = pltpu.roll(geo[:, 3 * SITES :], lax.rem(SITES - strip_shift(x0, r, x), SITES), 1)
            at = 2 * (x0 + x) + c
            tiles[0] = jnp.where(lane // 8 == jnp.where(other, -1, at), moved, tiles[0])
            tiles[1] = jnp.where(lane // 8 == jnp.where(other, at, -1), moved, tiles[1])
    snd4[4] = tiles[0]
    snd4[9] = tiles[1]
    for at in (5, 6, 7, 8, 9, 0, 1, 2, 3, 4):
        there, here, device = owners[at]
        slot = j if at < 5 else jnp.where(j == 0, 5, 4)
        slot = slot + (6 if at % 5 == 4 else 0)
        send(there, here, device, snd4.at[at], rcv4.at[slot], 3, at, slot)
    for at, (there, here, _, _) in enumerate(readers):
        wanted = there if here is None else there | here
        receive(wanted, rcv4.at[at], 3, at)
    back = rcv4[0]
    for at in range(1, 12):
        back = back + rcv4[at]

    rows = [jnp.broadcast_to(-back[axis : axis + 1], (16, SITES)) for axis in range(3)]
    rows.append(jnp.broadcast_to(back[3:4], (16, SITES)))
    full = jnp.where(yz_mask[0:64], jnp.concatenate(rows, axis=0), 0.0)
    out = dot_exact(full, x_pick, NT)
    for y in range(4):
        for axis in range(3):
            force_ref[axis, y] = out[axis * 16 + y * 4 : axis * 16 + y * 4 + 4, 0:8]
        en_ref[y] = out[48 + y * 4 : 52 + y * 4, 0:8]
    for there, remote in sent:

        @pl.when(there)
        def _():
            remote().wait_send()


def shards(
    positions,
    occupied,
    species,
    neighbours,
    embedding,
    radial_first,
    radial_second,
    radial_third,
    radial_last,
    up_weight,
    product_weight,
    out_weight,
    read_linear,
    read_hidden,
    read_last,
):
    n_gx = lax.axis_size("gx")
    vmem = pl.BlockSpec(memory_space=pltpu.VMEM)
    operands = (
        positions.transpose(0, 2, 3, 1),
        occupied.transpose(1, 2, 0),
        species.transpose(1, 2, 0),
        neighbours,
        embedding,
        radial_first,
        radial_second,
        radial_third,
        radial_last,
        up_weight,
        product_weight,
        out_weight,
        read_linear,
        read_hidden.T,
        read_last.reshape(1, -1),
    )
    energies, forces = pl.pallas_call(
        functools.partial(kernel, n_gx),
        out_shape=(
            jax.ShapeDtypeStruct((4, 4, 8), F32),
            jax.ShapeDtypeStruct((3, 4, 4, 8), F32),
        ),
        in_specs=[pl.BlockSpec(memory_space=pltpu.HBM)] * 15,
        out_specs=(vmem, vmem),
        scratch_shapes=[pltpu.VMEM(one.shape, one.dtype) for one in operands]
        + [
            pltpu.VMEM((80, SITES), F32),
            pltpu.VMEM((SITES, SITES), F32),
            pltpu.VMEM((24, SITES), F32),
            pltpu.VMEM((8, 4 * SITES), F32),
            pltpu.VMEM((GHOSTS, SITES), BF16),
            pltpu.VMEM((EXT, EDGES), BF16),
            pltpu.VMEM((10, 24, SITES), F32),
            pltpu.VMEM((144, CH), BF16),
            pltpu.VMEM((GHOSTS, CH), BF16),
            pltpu.VMEM((GHOSTS, CH), BF16),
            pltpu.VMEM((GHOSTS, CH), BF16),
            pltpu.VMEM((10, 8, SITES), F32),
            pltpu.VMEM((12, 8, SITES), F32),
            pltpu.VMEM((SLOTS * 8, SITES), F32),
            pltpu.VMEM((SLOTS * 8, SITES), F32),
            pltpu.VMEM((9, 16, SITES), F32),
            pltpu.VMEM((BES, 16, SITES), F32),
            pltpu.VMEM((LAYERS, 4, CH, SITES), F32),
            pltpu.VMEM((LAYERS, 3, RAD, EDGES), F32),
            pltpu.VMEM((LAYERS, 3 * CH, EDGES), F32),
            pltpu.VMEM((LAYERS, CH, EDGES), F32),
            pltpu.VMEM((LAYERS, 9, CH, SITES), F32),
            pltpu.VMEM((CH, SITES), BF16),
            pltpu.VMEM((3 * CH, EDGES), BF16),
            pltpu.VMEM((CH, EDGES), BF16),
            pltpu.VMEM((9 * SLOTS * 8, SITES), F32),
            pltpu.SemaphoreType.DMA((15,)),
            pltpu.SemaphoreType.DMA((4, 12)),
            pltpu.SemaphoreType.DMA((4, 12)),
        ],
        compiler_params=pltpu.CompilerParams(
            collective_id=0, has_side_effects=True, vmem_limit_bytes=48 * 1024 * 1024
        ),
    )(*[pltpu.with_memory_space_constraint(one, pltpu.HBM) for one in operands])
    return energies.transpose(2, 0, 1), forces.transpose(0, 3, 1, 2)


def solution(mesh):
    in_specs = (
        P(None, "gx", "gy", None),
        P("gx", "gy", None),
        P("gx", "gy", None),
        P("gx", "gy", None, None),
        P(),
        P(),
        P(),
        P(),
        P(),
        P(),
        P(),
        P(),
        P(),
        P(),
        P(),
    )
    out_specs = (P("gx", "gy", None), P(None, "gx", "gy", None))
    return jax.shard_map(shards, mesh=mesh, in_specs=in_specs, out_specs=out_specs, check_vma=False)
```

```python
import functools
import math

import jax
import jax.numpy as jnp
from jax import lax
from jax.experimental import pallas as pl
from jax.experimental.pallas import tpu as pltpu
from jax.sharding import PartitionSpec as P

F32 = jnp.float32
BF16 = jnp.bfloat16
MESH = pl.DeviceIdType.MESH
CUTOFF = 5.0
SLOTS = 12
SITES = 128
EDGES = SITES * SLOTS
GHOSTS = 304
EXT = SITES + GHOSTS
CH = 128
RAD = 64
BES = 8
LAYERS = 2

LEFT, RIGHT, ACROSS = 128, 256, 384

NT = (((1,), (1,)), ((), ()))
TN = (((0,), (0,)), ((), ()))
NN = (((1,), (0,)), ((), ()))


def dot(a, b, dims=NN):
    return lax.dot_general(a, b, dims, preferred_element_type=F32)


def dot_exact(a, b, dims=NN):
    return lax.dot_general(a, b, dims, preferred_element_type=F32, precision=lax.Precision.HIGHEST)


def iota(shape, dim):
    return lax.broadcasted_iota(jnp.int32, shape, dim)


def split3(x):
    high = x.astype(BF16).astype(F32)
    rest = x - high
    middle = rest.astype(BF16).astype(F32)
    return jnp.concatenate([high, middle, rest - middle], axis=0).astype(BF16)


def split2(x):
    high = x.astype(BF16).astype(F32)
    return jnp.concatenate([high, x - high], axis=0).astype(BF16)


def silu_parts(z):
    s = 0.5 + 0.5 * jnp.tanh(0.5 * z)
    g = z * s
    return g, s + g * (1.0 - s)


ROOT3 = math.sqrt(3.0)
ROOT5 = math.sqrt(5.0)
ROOT15 = math.sqrt(15.0)
FACTOR = 1.0 / math.sqrt(SLOTS)
GROUP = 4


def kernel(n_gx, *refs):
    inputs, refs = refs[:15], refs[15:]
    (en_ref, force_ref), refs = refs[:2], refs[2:]
    held, refs = refs[:15], refs[15:]
    (raw, nb, tile, geo, ps, oh, rcv1, snd2, rcv2, snd3, rcv3, snd4, rcv4), refs = refs[:13], refs[13:]
    (gs, bs, ye, bd, mix, dsilu, q, u, a, msg, dq, du, s_acc), refs = refs[:13], refs[13:]
    (w1_t, w2_t, w3_t, w4_t, ow_t, up_t, fq, rows_held), refs = refs[:8], refs[8:]
    fetch_sem, send_sem, recv_sem = refs
    (pos_ref, occ_ref, spec_ref, nbr_ref, emb_ref, w1_ref, w2_ref, w3_ref, w4_ref), more = held[:9], held[9:]
    up_ref, pw_ref, ow_ref, rl_ref, rh_ref, rlast_ref = more

    fetches = []
    for i in range(15):
        fetch = pltpu.make_async_copy(inputs[i], held[i], fetch_sem.at[i])
        fetch.start()
        fetches.append(fetch)

    gx = lax.axis_index("gx")
    gy = lax.axis_index("gy")

    def computed_at(x_block):
        return jnp.where(x_block // 16 % 2 == 1, x_block // 16 * 16 + 12 - x_block // 4 % 4 * 4 + x_block % 4, x_block)

    block = computed_at(gx)
    j, c = gy // 2, gy % 2
    own_half, own_slot = gy // 4, gy % 4
    edge = (gy == 3) | (gy == 4)
    halo_gy = 4 - c
    first, last_gx = gx == 0, gx == n_gx - 1
    has_left = jnp.logical_not((j == 0) & (block == 0))
    has_right = jnp.logical_not((j == 3) & (block == n_gx - 1))
    has_other = ((j == 0) | (j == 3)) & has_left & has_right
    other_gx = jnp.where(j == 0, block - 1, block + 1)
    left = (computed_at(jnp.where(j == 0, block - 1, block)), jnp.where(j == 0, 6, 2 * j - 2))
    right = (computed_at(jnp.where(j == 3, block + 1, block)), jnp.where(j == 3, 0, 2 * j + 2))
    always = gx >= 0
    regions = (
        (has_left, (left[0], left[1] + c), 0, 128),
        (has_right, (right[0], right[1] + c), 128, 128),
        (always, (gx, 2 * j + 1 - c), 256, 16),
        (has_left, (left[0], left[1] + 1 - c), 272, 16),
        (has_right, (right[0], right[1] + 1 - c), 288, 16),
    )
    facing = (1, 0, 2, 4, 3)
    owners = []
    for group in range(2):
        for m in range(5):
            owner_gy = 4 * c + m if m < 4 else halo_gy
            if group == 0:
                here = (owner_gy == gy) & (block == gx)
                owners.append((jnp.logical_not(here), here, (block, owner_gy)))
            else:
                owners.append((has_other, None, (other_gx, owner_gy)))
    readers = []
    for side in range(2):
        half = own_half if side == 0 else 1 - own_half
        slot = own_slot if side == 0 else 4
        wanted = always if side == 0 else edge
        for p in range(4):
            here = (2 * p + half == gy) & (block == gx)
            readers.append((wanted & jnp.logical_not(here), wanted & here, (computed_at(gx), 2 * p + half), slot))
        readers.append((wanted & jnp.logical_not(first), None, (computed_at(gx - 1), 6 + half), slot + 5))
        readers.append((wanted & jnp.logical_not(last_gx), None, (computed_at(gx + 1), half), slot + 5))

    rcv1[...] = jnp.zeros_like(rcv1)
    rcv2[...] = jnp.zeros_like(rcv2)
    rcv3[...] = jnp.zeros_like(rcv3)
    rcv4[...] = jnp.zeros_like(rcv4)
    barrier = pltpu.get_barrier_semaphore()

    def greet(there, device):
        @pl.when(there)
        def _():
            pl.semaphore_signal(barrier, inc=1, device_id=device, device_id_type=MESH)

    for there, _, device in owners:
        greet(there, device)
    for there, device, _, _ in regions:
        greet(there, device)
    greetings = jnp.int32(0)
    for there, _, _, _ in readers + list(regions):
        greetings = greetings + there.astype(jnp.int32)

    sent = []

    def send(there, here, device, source, target, phase, at, slot):
        def remote():
            return pltpu.make_async_remote_copy(
                src_ref=source,
                dst_ref=target,
                send_sem=send_sem.at[phase, at],
                recv_sem=recv_sem.at[phase, slot],
                device_id=device,
                device_id_type=MESH,
            )

        @pl.when(there)
        def _():
            remote().start()

        if here is not None:

            @pl.when(here)
            def _():
                pltpu.make_async_copy(source, target, recv_sem.at[phase, slot]).start()

        sent.append((there, remote))

    def receive(there, target, phase, slot):
        @pl.when(there)
        def _():
            pltpu.make_async_copy(target, target, recv_sem.at[phase, slot]).wait()

    raw[...] = jnp.zeros_like(raw)
    nb[...] = jnp.zeros_like(nb)
    tile[...] = jnp.zeros_like(tile)
    x_pick = (iota((SITES, SITES), 0) == iota((SITES, SITES), 1) // 16)
    x_pick = jnp.where(x_pick, 1.0, 0.0).astype(BF16)
    yz_mask = iota((80, SITES), 0) % 16 == iota((80, SITES), 1) % 16
    for i in range(4):
        fetches[i].wait()
    for y in range(4):
        for axis in range(3):
            raw[axis * 16 + y * 4 : axis * 16 + y * 4 + 4, 0:8] = pos_ref[axis, y]
        raw[48 + y * 4 : 52 + y * 4, 0:8] = occ_ref[y].astype(F32)
        raw[64 + y * 4 : 68 + y * 4, 0:8] = spec_ref[y].astype(F32)
    for x in range(8):
        for y in range(4):
            nb[x * 16 + y * 4 : x * 16 + y * 4 + 4, 0:SLOTS] = nbr_ref[x, y].astype(F32)
    spread = dot(split3(raw[...]), x_pick)
    spread = jnp.where(yz_mask, spread[0:80] + spread[80:160] + spread[160:240], 0.0)
    for f in range(5):
        tile[f : f + 1, :] = jnp.sum(spread[f * 16 : f * 16 + 16], axis=0, keepdims=True)
    tile[8:24, :] = nb[...].T[0:16]

    pl.semaphore_wait(barrier, greetings)
    for at in (4, 5, 0, 1, 2, 3, 10, 11, 6, 7, 8, 9):
        there, here, device, slot = readers[at]
        rows = 24 if at < 4 else 8
        send(there, here, device, tile.at[0:rows], rcv1.at[slot, 0:rows], 0, at, slot)

    rows = iota((GHOSTS, SITES), 0)
    y_strip = 14 * (1 - c)
    strip = rows % 16 // 8 * 64 + (y_strip + rows % 8 // 4) * 4 + rows % 4
    hit = jnp.where(rows < 256, rows % 128, strip) == iota((GHOSTS, SITES), 1)
    ps[...] = jnp.where(hit, 1.0, 0.0).astype(BF16)
    for i in range(4, 15):
        fetches[i].wait()
    for layer in range(LAYERS):
        for ref, turned in ((w1_ref, w1_t), (w2_ref, w2_t), (w3_ref, w3_t), (w4_ref, w4_t), (ow_ref, ow_t)):
            turned[layer] = ref[layer].T
    up_t[...] = up_ref[1].T
    lifted_table = dot(emb_ref[...], up_ref[0]).astype(BF16).astype(F32)
    s_acc[...] = jnp.zeros_like(s_acc)
    geo[...] = jnp.zeros_like(geo)

    for slot in range(4):
        receive(always, rcv1.at[slot, 0:24], 0, slot)

    lane = iota((8, SITES), 1)
    no = gx < 0
    slabs = (
        (2 * j, no),
        (jnp.where(j == 0, 6, 2 * j - 2), j == 0),
        (jnp.where(j == 3, 0, 2 * j + 2), j == 3),
    )
    y_halo = 2 * c

    def slab_shift(x0, m, x):
        return lax.rem(2 * SITES + x * 64 + m * 16 - (x0 + x) * 16, SITES)

    def strip_shift(x0, r, x):
        return lax.rem(2 * SITES + r * 16 + x * 8 - (x0 + x) * 16 - y_halo * 4, SITES)

    def slab(r):
        x0, other = slabs[r]
        out = jnp.zeros((8, SITES), F32)
        for m in range(4):
            source = rcv1[m, 0:8]
            if r > 0:
                source = jnp.where(other, rcv1[5 + m, 0:8], source)
            for x in range(2):
                moved = pltpu.roll(source, slab_shift(x0, m, x), 1)
                out = jnp.where(lane // 16 == x * 4 + m, moved, out)
        geo[:, r * SITES : (r + 1) * SITES] = out

    slab(0)

    lane16 = iota((16, SITES), 1)
    index = jnp.zeros((16, SITES), F32)
    for m in range(4):
        for x in range(2):
            moved = pltpu.roll(rcv1[m, 8:24], slab_shift(2 * j, m, x), 1)
            index = jnp.where(lane16 // 16 == x * 4 + m, moved, index)
    index = index.astype(jnp.int32)
    z = index & 3
    y = ((index >> 2) & 7) - 2 + lane16 // 16 % 4 * 4
    x = (index >> 5) - 2 - 2 * j
    inner = (x & 1) * 64 + y * 4 + z + jnp.where(x < 0, LEFT, jnp.where(x > 1, RIGHT, 0))
    outer = (x & 1) * 8 + (y & 1) * 4 + z + jnp.where(x < 0, ACROSS + 16, jnp.where(x > 1, ACROSS + 32, ACROSS))
    beyond = jnp.where(c == 0, y - 16, -1 - y) >= 0
    place = jnp.where((y >= 0) & (y < 16), inner, jnp.where(beyond, outer, -1))
    ext_row = iota((EXT, SITES), 0)
    for k in range(SLOTS):
        hit = ext_row == place[k : k + 1]
        oh[:, k * SITES : (k + 1) * SITES] = jnp.where(hit, 1.0, 0.0).astype(BF16)

    present = geo[3:4, 0:SITES]
    own_hot = (geo[4:5, 0:SITES].astype(jnp.int32) == iota((16, SITES), 0)).astype(F32)

    def species_weights(layer):
        for k in range(4):
            mix[layer, k] = dot_exact(pw_ref[layer, :, k, :], own_hot[0:10], TN)

    species_weights(0)
    h0 = dot(emb_ref[...].astype(F32), own_hot[0:10], TN) * present

    for slot in range(4, 10):
        receive(always if slot < 5 else has_other, rcv1.at[slot, 0:8], 0, slot)
    slab(1)
    slab(2)
    out = jnp.zeros((8, SITES), F32)
    for r, (x0, other) in enumerate(slabs):
        source = rcv1[4, 0:8]
        if r > 0:
            source = jnp.where(other, rcv1[9, 0:8], source)
        for x in range(2):
            moved = pltpu.roll(source, strip_shift(x0, r, x), 1)
            out = jnp.where(lane // 8 == r * 2 + x, moved, out)
    geo[:, 3 * SITES : 4 * SITES] = out

    gathered = dot(split3(geo[:, 0:EXT]), oh[...])
    gathered = gathered[0:8] + gathered[8:16] + gathered[16:24]
    for k in range(SLOTS):
        gs[k * 8 : k * 8 + 8, :] = gathered[:, k * SITES : (k + 1) * SITES]
    ext_hot = (geo[4:5, 0:EXT].astype(jnp.int32) == iota((16, EXT), 0)).astype(F32)
    u0 = dot(lifted_table, ext_hot[0:10], TN).astype(BF16)
    u[0] = dot(u0, oh[...]).astype(BF16)

    def rows_of(ref, m):
        return ref[pl.ds(m, SLOTS, stride=8), :]

    disp = [rows_of(gs, c) - geo[c : c + 1, 0:SITES] for c in range(3)]
    w = rows_of(gs, 3) * present
    squared = disp[0] * disp[0] + disp[1] * disp[1] + disp[2] * disp[2]
    dist = jnp.sqrt(jnp.where(w > 0, squared, 1.0))
    inv = 1.0 / dist
    nx, ny, nz = [c * inv for c in disp]
    scaled = jnp.minimum(dist * (1.0 / CUTOFF), 1.0)
    u2 = scaled * scaled
    u5 = u2 * u2 * scaled
    u6 = u5 * scaled
    env = 1.0 - 28.0 * u6 + 48.0 * u6 * scaled - 21.0 * u6 * u2
    env = jnp.where(scaled < 1.0, env, 0.0)
    gap = 1.0 - scaled
    slope = (-168.0 / CUTOFF) * u5 * gap * gap
    env_w = env * w
    slope_w = slope * w
    ye_scale = FACTOR * env_w
    harmonics = [
        ROOT3 * nx,
        ROOT3 * ny,
        ROOT3 * nz,
        ROOT15 * nx * ny,
        ROOT15 * ny * nz,
        0.5 * ROOT5 * (3.0 * nz * nz - 1.0),
        ROOT15 * nx * nz,
        0.5 * ROOT15 * (nx * nx - ny * ny),
    ]
    for m in range(9):
        one = ye_scale if m == 0 else ye_scale * harmonics[m - 1]
        for k in range(SLOTS):
            ye[m, k] = jnp.broadcast_to(one[k : k + 1], (16, SITES)).astype(BF16)
    theta = math.pi * scaled
    sin1 = jnp.sin(theta)
    cos1 = jnp.cos(theta)
    twice = 2.0 * cos1
    sin_before, cos_before = jnp.zeros_like(sin1), jnp.ones_like(cos1)
    sin_m, cos_m = sin1, cos1
    amplitude = math.sqrt(2.0 / CUTOFF) * inv
    for m in range(BES):
        value = amplitude * sin_m
        bs[pl.ds(m, SLOTS, stride=8), :] = value
        bd[m, 0:SLOTS] = amplitude * ((m + 1) * math.pi / CUTOFF) * cos_m - value * inv
        sin_m, sin_before = twice * sin_m - sin_before, sin_m
        cos_m, cos_before = twice * cos_m - cos_before, cos_m

    def radial(layer):
        hidden = jnp.concatenate([bs[k * 8 : k * 8 + 8, :] for k in range(SLOTS)], axis=1)
        hidden = hidden.astype(BF16)
        for step, ref in enumerate((w1_t, w2_t, w3_t)):
            z = dot(ref[layer], hidden)
            g, slope_g = silu_parts(z)
            dsilu[layer, step] = slope_g
            hidden = g.astype(BF16)
        q[layer] = dot(w4_t[layer], hidden).astype(BF16)

    def harmonic(m, k):
        return jnp.concatenate([ye[m, k], ye[m, k]], axis=0)

    def aggregate(layer):
        def body(block, carry):
            c0 = pl.multiple_of(block * 32, 32)
            acc = [None] * 9
            for first_k in range(0, SLOTS, GROUP):
                some = [None] * 9
                for k in range(first_k, first_k + GROUP):
                    lanes = slice(k * SITES, (k + 1) * SITES)
                    uk = u[layer, pl.ds(c0, 32), lanes]
                    v = [q[layer, pl.ds(L * CH + c0, 32), lanes] * uk for L in range(3)]
                    for m in range(9):
                        term = harmonic(m, k) * v[0 if m == 0 else (1 if m < 4 else 2)]
                        some[m] = term if some[m] is None else some[m] + term
                for m in range(9):
                    one = some[m].astype(F32)
                    acc[m] = one if acc[m] is None else acc[m] + one
            for m in range(9):
                a[layer, m, pl.ds(c0, 32), :] = acc[m]
            p = [mix[layer, j, pl.ds(c0, 32), :] for j in range(4)]
            first = acc[1] * acc[1] + acc[2] * acc[2] + acc[3] * acc[3]
            second = acc[4] * acc[4] + acc[5] * acc[5] + acc[6] * acc[6]
            second = second + acc[7] * acc[7] + acc[8] * acc[8]
            result = p[0] * acc[0] + p[1] * acc[0] * acc[0] + p[2] * first + p[3] * second
            msg[pl.ds(c0, 32), :] = result.astype(BF16)
            return carry

        lax.fori_loop(0, CH // 32, body, 0)

    def slopes(layer, c0):
        p = [mix[layer, j, pl.ds(c0, 32), :] for j in range(1, 4)]
        out = [mix[layer, 0, pl.ds(c0, 32), :] + 2.0 * p[0] * a[layer, 0, pl.ds(c0, 32), :]]
        for m in range(1, 9):
            out.append((2.0 * p[1 if m < 4 else 2]) * a[layer, m, pl.ds(c0, 32), :])
        return out

    def by_degree(da, k):
        out = [harmonic(0, k) * da[0], None, None]
        for m in range(1, 9):
            degree = 1 if m < 4 else 2
            term = harmonic(m, k) * da[m]
            out[degree] = term if out[degree] is None else out[degree] + term
        return out

    def blocks(body):
        def step(block, carry):
            body(pl.multiple_of(block * 32, 32))
            return carry

        lax.fori_loop(0, CH // 32, step, 0)

    def prepare_first(c0):
        t = slopes(0, c0)
        for m in range(9):
            a[0, m, pl.ds(c0, 32), :] = t[m]
        t = [one.astype(BF16) for one in t]
        for k in range(SLOTS):
            lanes = slice(k * SITES, (k + 1) * SITES)
            uk = u[0, pl.ds(c0, 32), lanes]
            for L, one in enumerate(by_degree(t, k)):
                fq[pl.ds(L * CH + c0, 32), lanes] = one * uk

    def features_back(c0):
        g = bm[pl.ds(c0, 32), :]
        da = [g * one for one in slopes(1, c0)]
        for m in range(9):
            a[1, m, pl.ds(c0, 32), :] = da[m]
        da = [one.astype(BF16) for one in da]
        for k in range(SLOTS):
            lanes = slice(k * SITES, (k + 1) * SITES)
            uk = u[1, pl.ds(c0, 32), lanes]
            dv = by_degree(da, k)
            total = dv[0] * q[1, pl.ds(c0, 32), lanes]
            for L in range(1, 3):
                total = total + dv[L] * q[1, pl.ds(L * CH + c0, 32), lanes]
            du[pl.ds(c0, 32), lanes] = total
            for L in range(3):
                dq[pl.ds(L * CH + c0, 32), lanes] = dv[L] * uk

    def angular_back(layer, c0):
        da = [a[layer, m, pl.ds(c0, 32), :] for m in range(9)]
        if layer == 0:
            g = bm[pl.ds(c0, 32), :]
            da = [g * one for one in da]
            g = g.astype(BF16)
        da = [one.astype(BF16) for one in da]
        for k in range(SLOTS):
            lanes = slice(k * SITES, (k + 1) * SITES)
            uk = u[layer, pl.ds(c0, 32), lanes]
            v = [q[layer, pl.ds(L * CH + c0, 32), lanes] * uk for L in range(3)]
            for m in range(9):
                part = da[m] * v[0 if m == 0 else (1 if m < 4 else 2)]
                at = (m * SLOTS + k) * 8
                part = (part[0:16] + part[16:32]).astype(F32)
                s_acc[at : at + 8, :] += part[0:8] + part[8:16]
            if layer == 0:
                for L in range(3):
                    dq[pl.ds(L * CH + c0, 32), lanes] = g * fq[pl.ds(L * CH + c0, 32), lanes]

    def radial_back(layer):
        grad = dot(w4_ref[layer], dq[...])
        for step, ref in ((2, w3_ref), (1, w2_ref), (0, w1_ref)):
            dz = (grad * dsilu[layer, step]).astype(BF16)
            grad = dot(ref[layer], dz)
        return grad

    bm = nb
    radial(0)
    aggregate(0)
    mixed = dot(ow_t[0], msg[...])
    h1 = (h0 + present * mixed).astype(BF16)
    u1_rows = dot(h1, up_ref[1], TN)
    rows_held[...] = u1_rows
    snd2[0:128] = u1_rows.astype(BF16)
    y_rows = pl.multiple_of(y_strip * 4, 8)
    strip = [rows_held[pl.ds(y_rows + x * 64, 8), :] for x in range(2)]
    snd2[128:144] = jnp.concatenate(strip, axis=0).astype(BF16)
    u1 = dot(up_t[...], h1).astype(BF16)
    for r, (there, device, start, size) in enumerate(regions):
        source = snd2.at[0:128] if r < 2 else snd2.at[128:144]
        start = regions[facing[r]][2]
        send(there, None, device, source, rcv2.at[start : start + size], 1, r, facing[r])
    species_weights(1)
    blocks(prepare_first)
    radial(1)
    near = dot(u1, oh[0:SITES, :])
    for r, (there, _, start, size) in enumerate(regions):
        receive(there, rcv2.at[start : start + size], 1, r)
    u[1] = (near + dot(rcv2[...], oh[SITES:EXT, :], TN)).astype(BF16)
    aggregate(1)
    mixed = dot(ow_t[1], msg[...])
    h2 = (h1.astype(F32) + present * mixed).astype(BF16)

    diagonal = iota((CH, CH), 0) == iota((CH, CH), 1)
    linear = jnp.sum(jnp.where(diagonal, rl_ref[...], 0.0), axis=1, keepdims=True)
    small = iota((16, 16), 0) == iota((16, 16), 1)
    last = jnp.sum(jnp.where(small, rlast_ref[...], 0.0), axis=1, keepdims=True)
    z = dot(rh_ref[...], h2)
    g, slope_g = silu_parts(z)
    energy = jnp.sum(h1.astype(F32) * linear, axis=0, keepdims=True)
    energy = present * (energy + jnp.sum(g * last, axis=0, keepdims=True))
    dz = (present * last * slope_g).astype(BF16)
    dh2 = dot(rh_ref[...], dz, TN)
    dmixed = (present * dh2).astype(BF16)
    message_grad = dot(ow_ref[1], dmixed)
    bm[...] = message_grad
    blocks(features_back)
    snd3[...] = dot(oh[SITES:EXT, :], du[...], NT).astype(BF16)
    for r, (there, device, start, size) in enumerate(regions):
        target = regions[facing[r]][2]
        source = snd3.at[start : start + size]
        send(there, None, device, source, rcv3.at[target : target + size], 2, r, facing[r])
    near = dot(du[...], oh[0:SITES, :], NT)
    bessel_grad = radial_back(1)
    blocks(functools.partial(angular_back, 1))
    for r, (there, _, start, size) in enumerate(regions):
        receive(there, rcv3.at[start : start + size], 2, r)
    du1 = near + dot(rcv3[...], ps[...], TN)
    dh1 = dh2 + linear * present + dot(up_ref[1], du1.astype(BF16))
    dmixed = (present * dh1).astype(BF16)
    bm[...] = dot(ow_ref[0], dmixed)
    blocks(functools.partial(angular_back, 0))
    bessel_grad = bessel_grad + radial_back(0)

    for k in range(SLOTS):
        gs[k * 8 : k * 8 + 8, :] = bessel_grad[:, k * SITES : (k + 1) * SITES]
    dr = rows_of(gs, 0) * bd[0, 0:SLOTS]
    for m in range(1, BES):
        dr = dr + rows_of(gs, m) * bd[m, 0:SLOTS]

    def total_of(m):
        at = m * SLOTS * 8
        out = s_acc[pl.ds(at, SLOTS, stride=8), :]
        for j in range(1, 8):
            out = out + s_acc[pl.ds(at + j, SLOTS, stride=8), :]
        return FACTOR * out

    sums = [total_of(m) for m in range(9)]
    d_env = sums[0]
    for m in range(8):
        d_env = d_env + sums[m + 1] * harmonics[m]
    dr = dr + d_env * slope_w
    dy = [env_w * one for one in sums[1:]]
    dnx = ROOT3 * dy[0] + ROOT15 * (dy[3] * ny + dy[6] * nz + dy[7] * nx)
    dny = ROOT3 * dy[1] + ROOT15 * (dy[3] * nx + dy[4] * nz - dy[7] * ny)
    dnz = ROOT3 * dy[2] + ROOT15 * (dy[4] * ny + dy[6] * nx) + (3.0 * ROOT5) * dy[5] * nz
    radial_part = dr - inv * (dnx * nx + dny * ny + dnz * nz)
    gs[...] = jnp.zeros_like(gs)
    centre = []
    for axis, (dn, n) in enumerate(((dnx, nx), (dny, ny), (dnz, nz))):
        dd = dn * inv + radial_part * n
        gs[pl.ds(axis, SLOTS, stride=8), :] = dd
        centre.append(jnp.sum(dd, axis=0, keepdims=True))
    edge_grad = jnp.concatenate([gs[k * 8 : k * 8 + 8, :] for k in range(SLOTS)], axis=1)
    scattered = dot(split3(edge_grad), oh[...], NT)
    geo[:, 0:EXT] = scattered[0:8] + scattered[8:16] + scattered[16:24]
    for axis in range(3):
        geo[axis : axis + 1, 0:SITES] = geo[axis : axis + 1, 0:SITES] - centre[axis]
    geo[3:4, 0:SITES] = energy

    for m in range(4):
        tiles = [jnp.zeros((8, SITES), F32) for _ in range(2)]
        for r, (x0, other) in enumerate(slabs):
            for x in range(2):
                moved = pltpu.roll(geo[:, r * SITES : (r + 1) * SITES], lax.rem(SITES - slab_shift(x0, m, x), SITES), 1)
                tiles[0] = jnp.where(lane // 16 == jnp.where(other, -1, x0 + x), moved, tiles[0])
                if r > 0:
                    tiles[1] = jnp.where(lane // 16 == jnp.where(other, x0 + x, -1), moved, tiles[1])
        snd4[m] = tiles[0]
        snd4[5 + m] = tiles[1]
    tiles = [jnp.zeros((8, SITES), F32) for _ in range(2)]
    for r, (x0, other) in enumerate(slabs):
        for x in range(2):
            moved = pltpu.roll(geo[:, 3 * SITES :], lax.rem(SITES - strip_shift(x0, r, x), SITES), 1)
            at = 2 * (x0 + x) + c
            tiles[0] = jnp.where(lane // 8 == jnp.where(other, -1, at), moved, tiles[0])
            tiles[1] = jnp.where(lane // 8 == jnp.where(other, at, -1), moved, tiles[1])
    snd4[4] = tiles[0]
    snd4[9] = tiles[1]
    for at in (5, 6, 7, 8, 9, 0, 1, 2, 3, 4):
        there, here, device = owners[at]
        slot = j if at < 5 else jnp.where(j == 0, 5, 4)
        slot = slot + (6 if at % 5 == 4 else 0)
        send(there, here, device, snd4.at[at], rcv4.at[slot], 3, at, slot)

    def settle(some):
        for there, remote in some:

            @pl.when(there)
            def _():
                remote().wait_send()

    settle(sent[:-10])
    for at, (there, here, _, _) in enumerate(readers):
        wanted = there if here is None else there | here
        receive(wanted, rcv4.at[at], 3, at)
    back = rcv4[0]
    for at in range(1, 12):
        back = back + rcv4[at]

    rows = [jnp.broadcast_to(-back[axis : axis + 1], (16, SITES)) for axis in range(3)]
    rows.append(jnp.broadcast_to(back[3:4], (16, SITES)))
    full = jnp.where(yz_mask[0:64], jnp.concatenate(rows, axis=0), 0.0)
    out = dot(split3(full), x_pick, NT)
    out = out[0:64] + out[64:128] + out[128:192]
    for y in range(4):
        for axis in range(3):
            force_ref[axis, y] = out[axis * 16 + y * 4 : axis * 16 + y * 4 + 4, 0:8]
        en_ref[y] = out[48 + y * 4 : 52 + y * 4, 0:8]
    settle(sent[-10:])


def shards(
    positions,
    occupied,
    species,
    neighbours,
    embedding,
    radial_first,
    radial_second,
    radial_third,
    radial_last,
    up_weight,
    product_weight,
    out_weight,
    read_linear,
    read_hidden,
    read_last,
):
    n_gx = lax.axis_size("gx")
    vmem = pl.BlockSpec(memory_space=pltpu.VMEM)
    operands = (
        positions.transpose(0, 2, 3, 1),
        occupied.transpose(1, 2, 0),
        species.transpose(1, 2, 0),
        neighbours,
        embedding,
        radial_first,
        radial_second,
        radial_third,
        radial_last,
        up_weight,
        product_weight,
        out_weight,
        read_linear,
        read_hidden.T,
        read_last.reshape(1, -1),
    )
    energies, forces = pl.pallas_call(
        functools.partial(kernel, n_gx),
        out_shape=(
            jax.ShapeDtypeStruct((4, 4, 8), F32),
            jax.ShapeDtypeStruct((3, 4, 4, 8), F32),
        ),
        in_specs=[pl.BlockSpec(memory_space=pltpu.HBM)] * 15,
        out_specs=(vmem, vmem),
        scratch_shapes=[pltpu.VMEM(one.shape, one.dtype) for one in operands]
        + [
            pltpu.VMEM((80, SITES), F32),
            pltpu.VMEM((SITES, SITES), F32),
            pltpu.VMEM((24, SITES), F32),
            pltpu.VMEM((8, 4 * SITES), F32),
            pltpu.VMEM((GHOSTS, SITES), BF16),
            pltpu.VMEM((EXT, EDGES), BF16),
            pltpu.VMEM((10, 24, SITES), F32),
            pltpu.VMEM((144, CH), BF16),
            pltpu.VMEM((GHOSTS, CH), BF16),
            pltpu.VMEM((GHOSTS, CH), BF16),
            pltpu.VMEM((GHOSTS, CH), BF16),
            pltpu.VMEM((10, 8, SITES), F32),
            pltpu.VMEM((12, 8, SITES), F32),
            pltpu.VMEM((SLOTS * 8, SITES), F32),
            pltpu.VMEM((SLOTS * 8, SITES), F32),
            pltpu.VMEM((9, SLOTS, 16, SITES), BF16),
            pltpu.VMEM((BES, 16, SITES), F32),
            pltpu.VMEM((LAYERS, 4, CH, SITES), F32),
            pltpu.VMEM((LAYERS, 3, RAD, EDGES), F32),
            pltpu.VMEM((LAYERS, 3 * CH, EDGES), BF16),
            pltpu.VMEM((LAYERS, CH, EDGES), BF16),
            pltpu.VMEM((LAYERS, 9, CH, SITES), F32),
            pltpu.VMEM((CH, SITES), BF16),
            pltpu.VMEM((3 * CH, EDGES), BF16),
            pltpu.VMEM((CH, EDGES), BF16),
            pltpu.VMEM((9 * SLOTS * 8, SITES), F32),
            pltpu.VMEM((LAYERS, RAD, BES), BF16),
            pltpu.VMEM((LAYERS, RAD, RAD), BF16),
            pltpu.VMEM((LAYERS, RAD, RAD), BF16),
            pltpu.VMEM((LAYERS, 3 * CH, RAD), BF16),
            pltpu.VMEM((LAYERS, CH, CH), BF16),
            pltpu.VMEM((CH, CH), BF16),
            pltpu.VMEM((3 * CH, EDGES), BF16),
            pltpu.VMEM((SITES, CH), F32),
            pltpu.SemaphoreType.DMA((15,)),
            pltpu.SemaphoreType.DMA((4, 12)),
            pltpu.SemaphoreType.DMA((4, 12)),
        ],
        compiler_params=pltpu.CompilerParams(
            collective_id=0, has_side_effects=True, vmem_limit_bytes=48 * 1024 * 1024
        ),
    )(*[pltpu.with_memory_space_constraint(one, pltpu.HBM) for one in operands])
    return energies.transpose(2, 0, 1), forces.transpose(0, 3, 1, 2)


def solution(mesh):
    in_specs = (
        P(None, "gx", "gy", None),
        P("gx", "gy", None),
        P("gx", "gy", None),
        P("gx", "gy", None, None),
        P(),
        P(),
        P(),
        P(),
        P(),
        P(),
        P(),
        P(),
        P(),
        P(),
        P(),
    )
    out_specs = (P("gx", "gy", None), P(None, "gx", "gy", None))
    return jax.shard_map(shards, mesh=mesh, in_specs=in_specs, out_specs=out_specs, check_vma=False)
```

```python
import functools
import math

import jax
import jax.numpy as jnp
from jax import lax
from jax.experimental import pallas as pl
from jax.experimental.pallas import tpu as pltpu
from jax.sharding import PartitionSpec as P

F32 = jnp.float32
BF16 = jnp.bfloat16
MESH = pl.DeviceIdType.MESH
CUTOFF = 5.0
SLOTS = 12
SITES = 128
EDGES = SITES * SLOTS
GHOSTS = 304
EXT = SITES + GHOSTS
CH = 128
RAD = 64
BES = 8
LAYERS = 2

LEFT, RIGHT, ACROSS = 128, 256, 384

NT = (((1,), (1,)), ((), ()))
TN = (((0,), (0,)), ((), ()))
NN = (((1,), (0,)), ((), ()))


def dot(a, b, dims=NN):
    return lax.dot_general(a, b, dims, preferred_element_type=F32)


def dot_exact(a, b, dims=NN):
    return lax.dot_general(a, b, dims, preferred_element_type=F32, precision=lax.Precision.HIGHEST)


def iota(shape, dim):
    return lax.broadcasted_iota(jnp.int32, shape, dim)


def split3(x):
    high = x.astype(BF16).astype(F32)
    rest = x - high
    middle = rest.astype(BF16).astype(F32)
    return jnp.concatenate([high, middle, rest - middle], axis=0).astype(BF16)


def split2(x):
    high = x.astype(BF16).astype(F32)
    return jnp.concatenate([high, x - high], axis=0).astype(BF16)


def silu_parts(z):
    s = 0.5 + 0.5 * jnp.tanh(0.5 * z)
    g = z * s
    return g, s + g * (1.0 - s)


ROOT3 = math.sqrt(3.0)
ROOT5 = math.sqrt(5.0)
ROOT15 = math.sqrt(15.0)
FACTOR = 1.0 / math.sqrt(SLOTS)
GROUP = 4


def kernel(n_gx, *refs):
    inputs, refs = refs[:15], refs[15:]
    (en_ref, force_ref), refs = refs[:2], refs[2:]
    held, refs = refs[:15], refs[15:]
    (raw, nb, tile, geo, ps, oh, rcv1, snd2, rcv2, snd3, rcv3, snd4, rcv4), refs = refs[:13], refs[13:]
    (gs, bs, ye, bd, mix, dsilu, q, u, a, msg, dq, du, s_acc), refs = refs[:13], refs[13:]
    (w1_t, w2_t, w3_t, w4_t, ow_t, up_t, fq, rows_held), refs = refs[:8], refs[8:]
    fetch_sem, send_sem, recv_sem = refs
    (pos_ref, occ_ref, spec_ref, nbr_ref, emb_ref, w1_ref, w2_ref, w3_ref, w4_ref), more = held[:9], held[9:]
    up_ref, pw_ref, ow_ref, rl_ref, rh_ref, rlast_ref = more

    gx = lax.axis_index("gx")
    gy = lax.axis_index("gy")

    def computed_at(x_block):
        return jnp.where(x_block // 16 % 2 == 1, x_block // 16 * 16 + 12 - x_block // 4 % 4 * 4 + x_block % 4, x_block)

    block = computed_at(gx)
    j, c = gy // 2, gy % 2
    own_half, own_slot = gy // 4, gy % 4
    edge = (gy == 3) | (gy == 4)
    halo_gy = 4 - c
    first, last_gx = gx == 0, gx == n_gx - 1
    has_left = jnp.logical_not((j == 0) & (block == 0))
    has_right = jnp.logical_not((j == 3) & (block == n_gx - 1))
    has_other = ((j == 0) | (j == 3)) & has_left & has_right
    other_gx = jnp.where(j == 0, block - 1, block + 1)
    left = (computed_at(jnp.where(j == 0, block - 1, block)), jnp.where(j == 0, 6, 2 * j - 2))
    right = (computed_at(jnp.where(j == 3, block + 1, block)), jnp.where(j == 3, 0, 2 * j + 2))
    always = gx >= 0
    regions = (
        (has_left, (left[0], left[1] + c), 0, 128),
        (has_right, (right[0], right[1] + c), 128, 128),
        (always, (gx, 2 * j + 1 - c), 256, 16),
        (has_left, (left[0], left[1] + 1 - c), 272, 16),
        (has_right, (right[0], right[1] + 1 - c), 288, 16),
    )
    facing = (1, 0, 2, 4, 3)
    owners = []
    for group in range(2):
        for m in range(5):
            owner_gy = 4 * c + m if m < 4 else halo_gy
            if group == 0:
                here = (owner_gy == gy) & (block == gx)
                owners.append((jnp.logical_not(here), here, (block, owner_gy)))
            else:
                owners.append((has_other, None, (other_gx, owner_gy)))
    readers = []
    for side in range(2):
        half = own_half if side == 0 else 1 - own_half
        slot = own_slot if side == 0 else 4
        wanted = always if side == 0 else edge
        for p in range(4):
            here = (2 * p + half == gy) & (block == gx)
            readers.append((wanted & jnp.logical_not(here), wanted & here, (computed_at(gx), 2 * p + half), slot))
        readers.append((wanted & jnp.logical_not(first), None, (computed_at(gx - 1), 6 + half), slot + 5))
        readers.append((wanted & jnp.logical_not(last_gx), None, (computed_at(gx + 1), half), slot + 5))

    rcv1[...] = jnp.zeros_like(rcv1)
    rcv2[...] = jnp.zeros_like(rcv2)
    rcv3[...] = jnp.zeros_like(rcv3)
    rcv4[...] = jnp.zeros_like(rcv4)
    barrier = pltpu.get_barrier_semaphore()

    def greet(there, device):
        @pl.when(there)
        def _():
            pl.semaphore_signal(barrier, inc=1, device_id=device, device_id_type=MESH)

    for there, _, device in owners[5:]:
        greet(there, device)
    for there, device, _, _ in regions[:2] + regions[3:] + regions[2:3]:
        greet(there, device)
    for there, _, device in owners[:5]:
        greet(there, device)
    fetches = []
    for i in range(15):
        fetch = pltpu.make_async_copy(inputs[i], held[i], fetch_sem.at[i])
        fetch.start()
        fetches.append(fetch)
    greetings = jnp.int32(0)
    for there, _, _, _ in readers + list(regions):
        greetings = greetings + there.astype(jnp.int32)

    sent = []

    def send(there, here, device, source, target, phase, at, slot):
        def remote():
            return pltpu.make_async_remote_copy(
                src_ref=source,
                dst_ref=target,
                send_sem=send_sem.at[phase, at],
                recv_sem=recv_sem.at[phase, slot],
                device_id=device,
                device_id_type=MESH,
            )

        @pl.when(there)
        def _():
            remote().start()

        if here is not None:

            @pl.when(here)
            def _():
                pltpu.make_async_copy(source, target, recv_sem.at[phase, slot]).start()

        sent.append((there, remote))

    def receive(there, target, phase, slot):
        @pl.when(there)
        def _():
            pltpu.make_async_copy(target, target, recv_sem.at[phase, slot]).wait()

    raw[...] = jnp.zeros_like(raw)
    nb[...] = jnp.zeros_like(nb)
    tile[...] = jnp.zeros_like(tile)
    x_pick = (iota((SITES, SITES), 0) == iota((SITES, SITES), 1) // 16)
    x_pick = jnp.where(x_pick, 1.0, 0.0).astype(BF16)
    yz_mask = iota((80, SITES), 0) % 16 == iota((80, SITES), 1) % 16
    for i in range(3):
        fetches[i].wait()
    for y in range(4):
        for axis in range(3):
            raw[axis * 16 + y * 4 : axis * 16 + y * 4 + 4, 0:8] = pos_ref[axis, y]
        raw[48 + y * 4 : 52 + y * 4, 0:8] = occ_ref[y].astype(F32)
        raw[64 + y * 4 : 68 + y * 4, 0:8] = spec_ref[y].astype(F32)
    spread = dot(split3(raw[...]), x_pick)
    spread = jnp.where(yz_mask, spread[0:80] + spread[80:160] + spread[160:240], 0.0)
    for f in range(5):
        tile[f : f + 1, :] = jnp.sum(spread[f * 16 : f * 16 + 16], axis=0, keepdims=True)

    pl.semaphore_wait(barrier, greetings)

    def send_tile(at, rows):
        there, here, device, slot = readers[at]
        send(there, here, device, tile.at[0:rows], rcv1.at[slot, 0:rows], 0, at, slot)

    for at in (4, 5, 10, 11):
        send_tile(at, 8)
    fetches[3].wait()
    for x in range(8):
        for y in range(4):
            nb[x * 16 + y * 4 : x * 16 + y * 4 + 4, 0:SLOTS] = nbr_ref[x, y].astype(F32)
    tile[8:24, :] = nb[...].T[0:16]
    for at in range(4):
        send_tile(at, 24)
    for at in range(6, 10):
        send_tile(at, 8)

    rows = iota((GHOSTS, SITES), 0)
    y_strip = 14 * (1 - c)
    strip = rows % 16 // 8 * 64 + (y_strip + rows % 8 // 4) * 4 + rows % 4
    hit = jnp.where(rows < 256, rows % 128, strip) == iota((GHOSTS, SITES), 1)
    ps[...] = jnp.where(hit, 1.0, 0.0).astype(BF16)
    for i in range(4, 15):
        fetches[i].wait()
    for layer in range(LAYERS):
        for ref, turned in ((w1_ref, w1_t), (w2_ref, w2_t), (w3_ref, w3_t), (w4_ref, w4_t), (ow_ref, ow_t)):
            turned[layer] = ref[layer].T
    up_t[...] = up_ref[1].T
    lifted_table = dot(emb_ref[...], up_ref[0]).astype(BF16).astype(F32)
    s_acc[...] = jnp.zeros_like(s_acc)
    geo[...] = jnp.zeros_like(geo)

    for slot in range(4):
        receive(always, rcv1.at[slot, 0:24], 0, slot)

    lane = iota((8, SITES), 1)
    no = gx < 0
    slabs = (
        (2 * j, no),
        (jnp.where(j == 0, 6, 2 * j - 2), j == 0),
        (jnp.where(j == 3, 0, 2 * j + 2), j == 3),
    )
    y_halo = 2 * c

    def slab_shift(x0, m, x):
        return lax.rem(2 * SITES + x * 64 + m * 16 - (x0 + x) * 16, SITES)

    def strip_shift(x0, r, x):
        return lax.rem(2 * SITES + r * 16 + x * 8 - (x0 + x) * 16 - y_halo * 4, SITES)

    def slab(r):
        x0, other = slabs[r]
        out = jnp.zeros((8, SITES), F32)
        for m in range(4):
            source = rcv1[m, 0:8]
            if r > 0:
                source = jnp.where(other, rcv1[5 + m, 0:8], source)
            for x in range(2):
                moved = pltpu.roll(source, slab_shift(x0, m, x), 1)
                out = jnp.where(lane // 16 == x * 4 + m, moved, out)
        geo[:, r * SITES : (r + 1) * SITES] = out

    slab(0)

    lane16 = iota((16, SITES), 1)
    index = jnp.zeros((16, SITES), F32)
    for m in range(4):
        for x in range(2):
            moved = pltpu.roll(rcv1[m, 8:24], slab_shift(2 * j, m, x), 1)
            index = jnp.where(lane16 // 16 == x * 4 + m, moved, index)
    index = index.astype(jnp.int32)
    z = index & 3
    y = ((index >> 2) & 7) - 2 + lane16 // 16 % 4 * 4
    x = (index >> 5) - 2 - 2 * j
    inner = (x & 1) * 64 + y * 4 + z + jnp.where(x < 0, LEFT, jnp.where(x > 1, RIGHT, 0))
    outer = (x & 1) * 8 + (y & 1) * 4 + z + jnp.where(x < 0, ACROSS + 16, jnp.where(x > 1, ACROSS + 32, ACROSS))
    beyond = jnp.where(c == 0, y - 16, -1 - y) >= 0
    place = jnp.where((y >= 0) & (y < 16), inner, jnp.where(beyond, outer, -1))
    ext_row = iota((EXT, SITES), 0)
    for k in range(SLOTS):
        hit = ext_row == place[k : k + 1]
        oh[:, k * SITES : (k + 1) * SITES] = jnp.where(hit, 1.0, 0.0).astype(BF16)

    present = geo[3:4, 0:SITES]
    own_hot = (geo[4:5, 0:SITES].astype(jnp.int32) == iota((16, SITES), 0)).astype(F32)

    def species_weights(layer):
        for k in range(4):
            mix[layer, k] = dot_exact(pw_ref[layer, :, k, :], own_hot[0:10], TN)

    species_weights(0)
    h0 = dot(emb_ref[...].astype(F32), own_hot[0:10], TN) * present

    for slot in range(4, 10):
        receive(always if slot < 5 else has_other, rcv1.at[slot, 0:8], 0, slot)
    slab(1)
    slab(2)
    out = jnp.zeros((8, SITES), F32)
    for r, (x0, other) in enumerate(slabs):
        source = rcv1[4, 0:8]
        if r > 0:
            source = jnp.where(other, rcv1[9, 0:8], source)
        for x in range(2):
            moved = pltpu.roll(source, strip_shift(x0, r, x), 1)
            out = jnp.where(lane // 8 == r * 2 + x, moved, out)
    geo[:, 3 * SITES : 4 * SITES] = out

    gathered = dot(split3(geo[:, 0:EXT]), oh[...])
    gathered = gathered[0:8] + gathered[8:16] + gathered[16:24]
    for k in range(SLOTS):
        gs[k * 8 : k * 8 + 8, :] = gathered[:, k * SITES : (k + 1) * SITES]
    ext_hot = (geo[4:5, 0:EXT].astype(jnp.int32) == iota((16, EXT), 0)).astype(F32)
    u0 = dot(lifted_table, ext_hot[0:10], TN).astype(BF16)
    u[0] = dot(u0, oh[...]).astype(BF16)

    def rows_of(ref, m):
        return ref[pl.ds(m, SLOTS, stride=8), :]

    disp = [rows_of(gs, c) - geo[c : c + 1, 0:SITES] for c in range(3)]
    w = rows_of(gs, 3) * present
    squared = disp[0] * disp[0] + disp[1] * disp[1] + disp[2] * disp[2]
    dist = jnp.sqrt(jnp.where(w > 0, squared, 1.0))
    inv = 1.0 / dist
    nx, ny, nz = [c * inv for c in disp]
    scaled = jnp.minimum(dist * (1.0 / CUTOFF), 1.0)
    u2 = scaled * scaled
    u5 = u2 * u2 * scaled
    u6 = u5 * scaled
    env = 1.0 - 28.0 * u6 + 48.0 * u6 * scaled - 21.0 * u6 * u2
    env = jnp.where(scaled < 1.0, env, 0.0)
    gap = 1.0 - scaled
    slope = (-168.0 / CUTOFF) * u5 * gap * gap
    env_w = env * w
    slope_w = slope * w
    ye_scale = FACTOR * env_w
    harmonics = [
        ROOT3 * nx,
        ROOT3 * ny,
        ROOT3 * nz,
        ROOT15 * nx * ny,
        ROOT15 * ny * nz,
        0.5 * ROOT5 * (3.0 * nz * nz - 1.0),
        ROOT15 * nx * nz,
        0.5 * ROOT15 * (nx * nx - ny * ny),
    ]
    for m in range(9):
        one = ye_scale if m == 0 else ye_scale * harmonics[m - 1]
        for k in range(SLOTS):
            ye[m, k] = jnp.broadcast_to(one[k : k + 1], (16, SITES)).astype(BF16)
    theta = math.pi * scaled
    sin1 = jnp.sin(theta)
    cos1 = jnp.cos(theta)
    twice = 2.0 * cos1
    sin_before, cos_before = jnp.zeros_like(sin1), jnp.ones_like(cos1)
    sin_m, cos_m = sin1, cos1
    amplitude = math.sqrt(2.0 / CUTOFF) * inv
    for m in range(BES):
        value = amplitude * sin_m
        bs[pl.ds(m, SLOTS, stride=8), :] = value
        bd[m, 0:SLOTS] = amplitude * ((m + 1) * math.pi / CUTOFF) * cos_m - value * inv
        sin_m, sin_before = twice * sin_m - sin_before, sin_m
        cos_m, cos_before = twice * cos_m - cos_before, cos_m

    def radial(layer):
        hidden = jnp.concatenate([bs[k * 8 : k * 8 + 8, :] for k in range(SLOTS)], axis=1)
        hidden = hidden.astype(BF16)
        for step, ref in enumerate((w1_t, w2_t, w3_t)):
            z = dot(ref[layer], hidden)
            g, slope_g = silu_parts(z)
            dsilu[layer, step] = slope_g
            hidden = g.astype(BF16)
        q[layer] = dot(w4_t[layer], hidden).astype(BF16)

    def harmonic(m, k):
        return jnp.concatenate([ye[m, k], ye[m, k]], axis=0)

    def aggregate(layer):
        def body(block, carry):
            c0 = pl.multiple_of(block * 32, 32)
            acc = [None] * 9
            for first_k in range(0, SLOTS, GROUP):
                some = [None] * 9
                for k in range(first_k, first_k + GROUP):
                    lanes = slice(k * SITES, (k + 1) * SITES)
                    uk = u[layer, pl.ds(c0, 32), lanes]
                    v = [q[layer, pl.ds(L * CH + c0, 32), lanes] * uk for L in range(3)]
                    for m in range(9):
                        term = harmonic(m, k) * v[0 if m == 0 else (1 if m < 4 else 2)]
                        some[m] = term if some[m] is None else some[m] + term
                for m in range(9):
                    one = some[m].astype(F32)
                    acc[m] = one if acc[m] is None else acc[m] + one
            for m in range(9):
                a[layer, m, pl.ds(c0, 32), :] = acc[m]
            p = [mix[layer, j, pl.ds(c0, 32), :] for j in range(4)]
            first = acc[1] * acc[1] + acc[2] * acc[2] + acc[3] * acc[3]
            second = acc[4] * acc[4] + acc[5] * acc[5] + acc[6] * acc[6]
            second = second + acc[7] * acc[7] + acc[8] * acc[8]
            result = p[0] * acc[0] + p[1] * acc[0] * acc[0] + p[2] * first + p[3] * second
            msg[pl.ds(c0, 32), :] = result.astype(BF16)
            return carry

        lax.fori_loop(0, CH // 32, body, 0)

    def slopes(layer, c0):
        p = [mix[layer, j, pl.ds(c0, 32), :] for j in range(1, 4)]
        out = [mix[layer, 0, pl.ds(c0, 32), :] + 2.0 * p[0] * a[layer, 0, pl.ds(c0, 32), :]]
        for m in range(1, 9):
            out.append((2.0 * p[1 if m < 4 else 2]) * a[layer, m, pl.ds(c0, 32), :])
        return out

    def by_degree(da, k):
        out = [harmonic(0, k) * da[0], None, None]
        for m in range(1, 9):
            degree = 1 if m < 4 else 2
            term = harmonic(m, k) * da[m]
            out[degree] = term if out[degree] is None else out[degree] + term
        return out

    def blocks(body):
        def step(block, carry):
            body(pl.multiple_of(block * 32, 32))
            return carry

        lax.fori_loop(0, CH // 32, step, 0)

    def prepare_first(c0):
        t = slopes(0, c0)
        for m in range(9):
            a[0, m, pl.ds(c0, 32), :] = t[m]
        t = [one.astype(BF16) for one in t]
        for k in range(SLOTS):
            lanes = slice(k * SITES, (k + 1) * SITES)
            uk = u[0, pl.ds(c0, 32), lanes]
            for L, one in enumerate(by_degree(t, k)):
                fq[pl.ds(L * CH + c0, 32), lanes] = one * uk

    def features_back(c0):
        g = bm[pl.ds(c0, 32), :]
        da = [g * one for one in slopes(1, c0)]
        for m in range(9):
            a[1, m, pl.ds(c0, 32), :] = da[m]
        da = [one.astype(BF16) for one in da]
        for k in range(SLOTS):
            lanes = slice(k * SITES, (k + 1) * SITES)
            uk = u[1, pl.ds(c0, 32), lanes]
            dv = by_degree(da, k)
            total = dv[0] * q[1, pl.ds(c0, 32), lanes]
            for L in range(1, 3):
                total = total + dv[L] * q[1, pl.ds(L * CH + c0, 32), lanes]
            du[pl.ds(c0, 32), lanes] = total
            for L in range(3):
                dq[pl.ds(L * CH + c0, 32), lanes] = dv[L] * uk

    def angular_back(layer, c0):
        da = [a[layer, m, pl.ds(c0, 32), :] for m in range(9)]
        if layer == 0:
            g = bm[pl.ds(c0, 32), :]
            da = [g * one for one in da]
            g = g.astype(BF16)
        da = [one.astype(BF16) for one in da]
        for k in range(SLOTS):
            lanes = slice(k * SITES, (k + 1) * SITES)
            uk = u[layer, pl.ds(c0, 32), lanes]
            v = [q[layer, pl.ds(L * CH + c0, 32), lanes] * uk for L in range(3)]
            for m in range(9):
                part = da[m] * v[0 if m == 0 else (1 if m < 4 else 2)]
                at = (m * SLOTS + k) * 8
                part = (part[0:16] + part[16:32]).astype(F32)
                s_acc[at : at + 8, :] += part[0:8] + part[8:16]
            if layer == 0:
                for L in range(3):
                    dq[pl.ds(L * CH + c0, 32), lanes] = g * fq[pl.ds(L * CH + c0, 32), lanes]

    def radial_back(layer):
        grad = dot(w4_ref[layer], dq[...])
        for step, ref in ((2, w3_ref), (1, w2_ref), (0, w1_ref)):
            dz = (grad * dsilu[layer, step]).astype(BF16)
            grad = dot(ref[layer], dz)
        return grad

    bm = nb
    radial(0)
    aggregate(0)
    mixed = dot(ow_t[0], msg[...])
    h1 = (h0 + present * mixed).astype(BF16)
    u1_rows = dot(h1, up_ref[1], TN)
    rows_held[...] = u1_rows
    snd2[0:128] = u1_rows.astype(BF16)
    y_rows = pl.multiple_of(y_strip * 4, 8)
    strip = [rows_held[pl.ds(y_rows + x * 64, 8), :] for x in range(2)]
    snd2[128:144] = jnp.concatenate(strip, axis=0).astype(BF16)
    u1 = dot(up_t[...], h1).astype(BF16)
    for r, (there, device, start, size) in enumerate(regions):
        source = snd2.at[0:128] if r < 2 else snd2.at[128:144]
        start = regions[facing[r]][2]
        send(there, None, device, source, rcv2.at[start : start + size], 1, r, facing[r])
    species_weights(1)
    blocks(prepare_first)
    radial(1)
    near = dot(u1, oh[0:SITES, :])
    for r, (there, _, start, size) in enumerate(regions):
        receive(there, rcv2.at[start : start + size], 1, r)
    u[1] = (near + dot(rcv2[...], oh[SITES:EXT, :], TN)).astype(BF16)
    aggregate(1)
    mixed = dot(ow_t[1], msg[...])
    h2 = (h1.astype(F32) + present * mixed).astype(BF16)

    diagonal = iota((CH, CH), 0) == iota((CH, CH), 1)
    linear = jnp.sum(jnp.where(diagonal, rl_ref[...], 0.0), axis=1, keepdims=True)
    small = iota((16, 16), 0) == iota((16, 16), 1)
    last = jnp.sum(jnp.where(small, rlast_ref[...], 0.0), axis=1, keepdims=True)
    z = dot(rh_ref[...], h2)
    g, slope_g = silu_parts(z)
    energy = jnp.sum(h1.astype(F32) * linear, axis=0, keepdims=True)
    energy = present * (energy + jnp.sum(g * last, axis=0, keepdims=True))
    dz = (present * last * slope_g).astype(BF16)
    dh2 = dot(rh_ref[...], dz, TN)
    dmixed = (present * dh2).astype(BF16)
    message_grad = dot(ow_ref[1], dmixed)
    bm[...] = message_grad
    blocks(features_back)
    snd3[...] = dot(oh[SITES:EXT, :], du[...], NT).astype(BF16)
    for r, (there, device, start, size) in enumerate(regions):
        target = regions[facing[r]][2]
        source = snd3.at[start : start + size]
        send(there, None, device, source, rcv3.at[target : target + size], 2, r, facing[r])
    near = dot(du[...], oh[0:SITES, :], NT)
    bessel_grad = radial_back(1)
    blocks(functools.partial(angular_back, 1))
    for r, (there, _, start, size) in enumerate(regions):
        receive(there, rcv3.at[start : start + size], 2, r)
    du1 = near + dot(rcv3[...], ps[...], TN)
    dh1 = dh2 + linear * present + dot(up_ref[1], du1.astype(BF16))
    dmixed = (present * dh1).astype(BF16)
    bm[...] = dot(ow_ref[0], dmixed)
    blocks(functools.partial(angular_back, 0))
    bessel_grad = bessel_grad + radial_back(0)

    for k in range(SLOTS):
        gs[k * 8 : k * 8 + 8, :] = bessel_grad[:, k * SITES : (k + 1) * SITES]
    dr = rows_of(gs, 0) * bd[0, 0:SLOTS]
    for m in range(1, BES):
        dr = dr + rows_of(gs, m) * bd[m, 0:SLOTS]

    def total_of(m):
        at = m * SLOTS * 8
        out = s_acc[pl.ds(at, SLOTS, stride=8), :]
        for j in range(1, 8):
            out = out + s_acc[pl.ds(at + j, SLOTS, stride=8), :]
        return FACTOR * out

    sums = [total_of(m) for m in range(9)]
    d_env = sums[0]
    for m in range(8):
        d_env = d_env + sums[m + 1] * harmonics[m]
    dr = dr + d_env * slope_w
    dy = [env_w * one for one in sums[1:]]
    dnx = ROOT3 * dy[0] + ROOT15 * (dy[3] * ny + dy[6] * nz + dy[7] * nx)
    dny = ROOT3 * dy[1] + ROOT15 * (dy[3] * nx + dy[4] * nz - dy[7] * ny)
    dnz = ROOT3 * dy[2] + ROOT15 * (dy[4] * ny + dy[6] * nx) + (3.0 * ROOT5) * dy[5] * nz
    radial_part = dr - inv * (dnx * nx + dny * ny + dnz * nz)
    gs[...] = jnp.zeros_like(gs)
    centre = []
    for axis, (dn, n) in enumerate(((dnx, nx), (dny, ny), (dnz, nz))):
        dd = dn * inv + radial_part * n
        gs[pl.ds(axis, SLOTS, stride=8), :] = dd
        centre.append(jnp.sum(dd, axis=0, keepdims=True))
    edge_grad = jnp.concatenate([gs[k * 8 : k * 8 + 8, :] for k in range(SLOTS)], axis=1)
    scattered = dot(split3(edge_grad), oh[...], NT)
    geo[:, 0:EXT] = scattered[0:8] + scattered[8:16] + scattered[16:24]
    for axis in range(3):
        geo[axis : axis + 1, 0:SITES] = geo[axis : axis + 1, 0:SITES] - centre[axis]
    geo[3:4, 0:SITES] = energy

    for group in (1, 0):
        for m in range(5):
            out = jnp.zeros((8, SITES), F32)
            for r, (x0, other) in enumerate(slabs):
                if group == 1 and r == 0:
                    continue
                for x in range(2):
                    if m < 4:
                        part, shift = r, slab_shift(x0, m, x)
                        at, width = x0 + x, 16
                    else:
                        part, shift = 3, strip_shift(x0, r, x)
                        at, width = 2 * (x0 + x) + c, 8
                    moved = pltpu.roll(geo[:, part * SITES : (part + 1) * SITES], lax.rem(SITES - shift, SITES), 1)
                    at = jnp.where(other, at, -1) if group == 1 else jnp.where(other, -1, at)
                    out = jnp.where(lane // width == at, moved, out)
            snd4[5 * group + m] = out
        for at in range(5 * group, 5 * group + 5):
            there, here, device = owners[at]
            slot = j if group == 0 else jnp.where(j == 0, 5, 4)
            slot = slot + (6 if at % 5 == 4 else 0)
            send(there, here, device, snd4.at[at], rcv4.at[slot], 3, at, slot)

    def settle(some):
        for there, remote in some:

            @pl.when(there)
            def _():
                remote().wait_send()

    settle(sent[:-10])
    for at, (there, here, _, _) in enumerate(readers):
        wanted = there if here is None else there | here
        receive(wanted, rcv4.at[at], 3, at)
    back = rcv4[0]
    for at in range(1, 12):
        back = back + rcv4[at]

    rows = [jnp.broadcast_to(-back[axis : axis + 1], (16, SITES)) for axis in range(3)]
    rows.append(jnp.broadcast_to(back[3:4], (16, SITES)))
    full = jnp.where(yz_mask[0:64], jnp.concatenate(rows, axis=0), 0.0)
    out = dot(split3(full), x_pick, NT)
    out = out[0:64] + out[64:128] + out[128:192]
    for y in range(4):
        for axis in range(3):
            force_ref[axis, y] = out[axis * 16 + y * 4 : axis * 16 + y * 4 + 4, 0:8]
        en_ref[y] = out[48 + y * 4 : 52 + y * 4, 0:8]
    settle(sent[-10:])


def shards(
    positions,
    occupied,
    species,
    neighbours,
    embedding,
    radial_first,
    radial_second,
    radial_third,
    radial_last,
    up_weight,
    product_weight,
    out_weight,
    read_linear,
    read_hidden,
    read_last,
):
    n_gx = lax.axis_size("gx")
    vmem = pl.BlockSpec(memory_space=pltpu.VMEM)
    operands = (
        positions.transpose(0, 2, 3, 1),
        occupied.transpose(1, 2, 0),
        species.transpose(1, 2, 0),
        neighbours,
        embedding,
        radial_first,
        radial_second,
        radial_third,
        radial_last,
        up_weight,
        product_weight,
        out_weight,
        read_linear,
        read_hidden.T,
        read_last.reshape(1, -1),
    )
    energies, forces = pl.pallas_call(
        functools.partial(kernel, n_gx),
        out_shape=(
            jax.ShapeDtypeStruct((4, 4, 8), F32),
            jax.ShapeDtypeStruct((3, 4, 4, 8), F32),
        ),
        in_specs=[pl.BlockSpec(memory_space=pltpu.HBM)] * 15,
        out_specs=(vmem, vmem),
        scratch_shapes=[pltpu.VMEM(one.shape, one.dtype) for one in operands]
        + [
            pltpu.VMEM((80, SITES), F32),
            pltpu.VMEM((SITES, SITES), F32),
            pltpu.VMEM((24, SITES), F32),
            pltpu.VMEM((8, 4 * SITES), F32),
            pltpu.VMEM((GHOSTS, SITES), BF16),
            pltpu.VMEM((EXT, EDGES), BF16),
            pltpu.VMEM((10, 24, SITES), F32),
            pltpu.VMEM((144, CH), BF16),
            pltpu.VMEM((GHOSTS, CH), BF16),
            pltpu.VMEM((GHOSTS, CH), BF16),
            pltpu.VMEM((GHOSTS, CH), BF16),
            pltpu.VMEM((10, 8, SITES), F32),
            pltpu.VMEM((12, 8, SITES), F32),
            pltpu.VMEM((SLOTS * 8, SITES), F32),
            pltpu.VMEM((SLOTS * 8, SITES), F32),
            pltpu.VMEM((9, SLOTS, 16, SITES), BF16),
            pltpu.VMEM((BES, 16, SITES), F32),
            pltpu.VMEM((LAYERS, 4, CH, SITES), F32),
            pltpu.VMEM((LAYERS, 3, RAD, EDGES), F32),
            pltpu.VMEM((LAYERS, 3 * CH, EDGES), BF16),
            pltpu.VMEM((LAYERS, CH, EDGES), BF16),
            pltpu.VMEM((LAYERS, 9, CH, SITES), F32),
            pltpu.VMEM((CH, SITES), BF16),
            pltpu.VMEM((3 * CH, EDGES), BF16),
            pltpu.VMEM((CH, EDGES), BF16),
            pltpu.VMEM((9 * SLOTS * 8, SITES), F32),
            pltpu.VMEM((LAYERS, RAD, BES), BF16),
            pltpu.VMEM((LAYERS, RAD, RAD), BF16),
            pltpu.VMEM((LAYERS, RAD, RAD), BF16),
            pltpu.VMEM((LAYERS, 3 * CH, RAD), BF16),
            pltpu.VMEM((LAYERS, CH, CH), BF16),
            pltpu.VMEM((CH, CH), BF16),
            pltpu.VMEM((3 * CH, EDGES), BF16),
            pltpu.VMEM((SITES, CH), F32),
            pltpu.SemaphoreType.DMA((15,)),
            pltpu.SemaphoreType.DMA((4, 12)),
            pltpu.SemaphoreType.DMA((4, 12)),
        ],
        compiler_params=pltpu.CompilerParams(
            collective_id=0, has_side_effects=True, vmem_limit_bytes=48 * 1024 * 1024
        ),
    )(*[pltpu.with_memory_space_constraint(one, pltpu.HBM) for one in operands])
    return energies.transpose(2, 0, 1), forces.transpose(0, 3, 1, 2)


def solution(mesh):
    in_specs = (
        P(None, "gx", "gy", None),
        P("gx", "gy", None),
        P("gx", "gy", None),
        P("gx", "gy", None, None),
        P(),
        P(),
        P(),
        P(),
        P(),
        P(),
        P(),
        P(),
        P(),
        P(),
        P(),
    )
    out_specs = (P("gx", "gy", None), P(None, "gx", "gy", None))
    return jax.shard_map(shards, mesh=mesh, in_specs=in_specs, out_specs=out_specs, check_vma=False)
```

```python
import functools
import math

import jax
import jax.numpy as jnp
from jax import lax
from jax.experimental import pallas as pl
from jax.experimental.pallas import tpu as pltpu
from jax.sharding import PartitionSpec as P

F32 = jnp.float32
BF16 = jnp.bfloat16
MESH = pl.DeviceIdType.MESH
CUTOFF = 5.0
SLOTS = 12
SITES = 128
EDGES = SITES * SLOTS
GHOSTS = 304
EXT = SITES + GHOSTS
CH = 128
RAD = 64
BES = 8
LAYERS = 2

LEFT, RIGHT, ACROSS = 128, 256, 384

NT = (((1,), (1,)), ((), ()))
TN = (((0,), (0,)), ((), ()))
NN = (((1,), (0,)), ((), ()))


def dot(a, b, dims=NN):
    return lax.dot_general(a, b, dims, preferred_element_type=F32)


def dot_exact(a, b, dims=NN):
    return lax.dot_general(a, b, dims, preferred_element_type=F32, precision=lax.Precision.HIGHEST)


def iota(shape, dim):
    return lax.broadcasted_iota(jnp.int32, shape, dim)


def split3(x):
    high = x.astype(BF16).astype(F32)
    rest = x - high
    middle = rest.astype(BF16).astype(F32)
    return jnp.concatenate([high, middle, rest - middle], axis=0).astype(BF16)


def split2(x):
    high = x.astype(BF16).astype(F32)
    return jnp.concatenate([high, x - high], axis=0).astype(BF16)


def silu_parts(z):
    s = 0.5 + 0.5 * jnp.tanh(0.5 * z)
    g = z * s
    return g, s + g * (1.0 - s)


ROOT3 = math.sqrt(3.0)
ROOT5 = math.sqrt(5.0)
ROOT15 = math.sqrt(15.0)
FACTOR = 1.0 / math.sqrt(SLOTS)
GROUP = 4


def kernel(n_gx, *refs):
    inputs, refs = refs[:15], refs[15:]
    out_ref, refs = refs[0], refs[1:]
    held, refs = refs[:15], refs[15:]
    (raw, nb, tile, geo, ps, oh, rcv1, snd2, rcv2, snd3, rcv3, snd4, rcv4), refs = refs[:13], refs[13:]
    (gs, bs, ye, bd, mix, dsilu, q, u, a, msg, dq, du, s_acc), refs = refs[:13], refs[13:]
    (w1_t, w2_t, w3_t, w4_t, ow_t, up_t, fq, rows_held), refs = refs[:8], refs[8:]
    fetch_sem, send_sem, recv_sem = refs
    (pos_ref, occ_ref, spec_ref, nbr_ref, emb_ref, w1_ref, w2_ref, w3_ref, w4_ref), more = held[:9], held[9:]
    up_ref, pw_ref, ow_ref, rl_ref, rh_ref, rlast_ref = more

    gx = lax.axis_index("gx")
    gy = lax.axis_index("gy")

    def computed_at(x_block):
        return jnp.where(x_block // 16 % 2 == 1, x_block // 16 * 16 + 12 - x_block // 4 % 4 * 4 + x_block % 4, x_block)

    block = computed_at(gx)
    j, c = gy // 2, gy % 2
    own_half, own_slot = gy // 4, gy % 4
    edge = (gy == 3) | (gy == 4)
    halo_gy = 4 - c
    first, last_gx = gx == 0, gx == n_gx - 1
    has_left = jnp.logical_not((j == 0) & (block == 0))
    has_right = jnp.logical_not((j == 3) & (block == n_gx - 1))
    has_other = ((j == 0) | (j == 3)) & has_left & has_right
    other_gx = jnp.where(j == 0, block - 1, block + 1)
    left = (computed_at(jnp.where(j == 0, block - 1, block)), jnp.where(j == 0, 6, 2 * j - 2))
    right = (computed_at(jnp.where(j == 3, block + 1, block)), jnp.where(j == 3, 0, 2 * j + 2))
    always = gx >= 0
    regions = (
        (has_left, (left[0], left[1] + c), 0, 128),
        (has_right, (right[0], right[1] + c), 128, 128),
        (always, (gx, 2 * j + 1 - c), 256, 16),
        (has_left, (left[0], left[1] + 1 - c), 272, 16),
        (has_right, (right[0], right[1] + 1 - c), 288, 16),
    )
    facing = (1, 0, 2, 4, 3)
    owners = []
    for group in range(2):
        for m in range(5):
            owner_gy = 4 * c + m if m < 4 else halo_gy
            if group == 0:
                here = (owner_gy == gy) & (block == gx)
                owners.append((jnp.logical_not(here), here, (block, owner_gy)))
            else:
                owners.append((has_other, None, (other_gx, owner_gy)))
    readers = []
    for side in range(2):
        half = own_half if side == 0 else 1 - own_half
        slot = own_slot if side == 0 else 4
        wanted = always if side == 0 else edge
        for p in range(4):
            here = (2 * p + half == gy) & (block == gx)
            readers.append((wanted & jnp.logical_not(here), wanted & here, (computed_at(gx), 2 * p + half), slot))
        readers.append((wanted & jnp.logical_not(first), None, (computed_at(gx - 1), 6 + half), slot + 5))
        readers.append((wanted & jnp.logical_not(last_gx), None, (computed_at(gx + 1), half), slot + 5))

    rcv1[...] = jnp.zeros_like(rcv1)
    rcv2[...] = jnp.zeros_like(rcv2)
    rcv3[...] = jnp.zeros_like(rcv3)
    rcv4[...] = jnp.zeros_like(rcv4)
    barrier = pltpu.get_barrier_semaphore()

    def greet(there, device):
        @pl.when(there)
        def _():
            pl.semaphore_signal(barrier, inc=1, device_id=device, device_id_type=MESH)

    for there, _, device in owners[5:]:
        greet(there, device)
    for there, device, _, _ in regions[:2] + regions[3:] + regions[2:3]:
        greet(there, device)
    for there, _, device in owners[:5]:
        greet(there, device)
    fetches = []
    for i in range(15):
        fetch = pltpu.make_async_copy(inputs[i], held[i], fetch_sem.at[i])
        fetch.start()
        fetches.append(fetch)
    greetings = jnp.int32(0)
    for there, _, _, _ in readers + list(regions):
        greetings = greetings + there.astype(jnp.int32)

    sent = []

    def send(there, here, device, source, target, phase, at, slot):
        def remote():
            return pltpu.make_async_remote_copy(
                src_ref=source,
                dst_ref=target,
                send_sem=send_sem.at[phase, at],
                recv_sem=recv_sem.at[phase, slot],
                device_id=device,
                device_id_type=MESH,
            )

        @pl.when(there)
        def _():
            remote().start()

        if here is not None:

            @pl.when(here)
            def _():
                pltpu.make_async_copy(source, target, recv_sem.at[phase, slot]).start()

        sent.append((there, remote))

    def receive(there, target, phase, slot):
        @pl.when(there)
        def _():
            pltpu.make_async_copy(target, target, recv_sem.at[phase, slot]).wait()

    raw[...] = jnp.zeros_like(raw)
    nb[...] = jnp.zeros_like(nb)
    tile[...] = jnp.zeros_like(tile)
    x_pick = (iota((SITES, SITES), 0) == iota((SITES, SITES), 1) // 16)
    x_pick = jnp.where(x_pick, 1.0, 0.0).astype(BF16)
    yz_mask = iota((80, SITES), 0) % 16 == iota((80, SITES), 1) % 16
    for i in range(3):
        fetches[i].wait()
    for y in range(4):
        for axis in range(3):
            raw[axis * 16 + y * 4 : axis * 16 + y * 4 + 4, 0:8] = pos_ref[axis, y]
        raw[48 + y * 4 : 52 + y * 4, 0:8] = occ_ref[y].astype(F32)
        raw[64 + y * 4 : 68 + y * 4, 0:8] = spec_ref[y].astype(F32)
    spread = dot(split3(raw[...]), x_pick)
    spread = jnp.where(yz_mask, spread[0:80] + spread[80:160] + spread[160:240], 0.0)
    for f in range(5):
        tile[f : f + 1, :] = jnp.sum(spread[f * 16 : f * 16 + 16], axis=0, keepdims=True)

    pl.semaphore_wait(barrier, greetings)

    def send_tile(at, rows):
        there, here, device, slot = readers[at]
        send(there, here, device, tile.at[0:rows], rcv1.at[slot, 0:rows], 0, at, slot)

    for at in (4, 5, 10, 11):
        send_tile(at, 8)
    fetches[3].wait()
    for x in range(8):
        for y in range(4):
            nb[x * 16 + y * 4 : x * 16 + y * 4 + 4, 0:SLOTS] = nbr_ref[x, y].astype(F32)
    tile[8:24, :] = nb[...].T[0:16]
    for at in range(4):
        send_tile(at, 24)
    for at in range(6, 10):
        send_tile(at, 8)

    rows = iota((GHOSTS, SITES), 0)
    y_strip = 14 * (1 - c)
    strip = rows % 16 // 8 * 64 + (y_strip + rows % 8 // 4) * 4 + rows % 4
    hit = jnp.where(rows < 256, rows % 128, strip) == iota((GHOSTS, SITES), 1)
    ps[...] = jnp.where(hit, 1.0, 0.0).astype(BF16)
    for i in range(4, 15):
        fetches[i].wait()
    for layer in range(LAYERS):
        for ref, turned in ((w1_ref, w1_t), (w2_ref, w2_t), (w3_ref, w3_t), (w4_ref, w4_t), (ow_ref, ow_t)):
            turned[layer] = ref[layer].T
    up_t[...] = up_ref[1].T
    lifted_table = dot(emb_ref[...], up_ref[0]).astype(BF16).astype(F32)
    s_acc[...] = jnp.zeros_like(s_acc)
    geo[...] = jnp.zeros_like(geo)

    for slot in range(4):
        receive(always, rcv1.at[slot, 0:24], 0, slot)

    lane = iota((8, SITES), 1)
    no = gx < 0
    slabs = (
        (2 * j, no),
        (jnp.where(j == 0, 6, 2 * j - 2), j == 0),
        (jnp.where(j == 3, 0, 2 * j + 2), j == 3),
    )
    y_halo = 2 * c

    def slab_shift(x0, m, x):
        return lax.rem(2 * SITES + x * 64 + m * 16 - (x0 + x) * 16, SITES)

    def strip_shift(x0, r, x):
        return lax.rem(2 * SITES + r * 16 + x * 8 - (x0 + x) * 16 - y_halo * 4, SITES)

    def slab(r):
        x0, other = slabs[r]
        out = jnp.zeros((8, SITES), F32)
        for m in range(4):
            source = rcv1[m, 0:8]
            if r > 0:
                source = jnp.where(other, rcv1[5 + m, 0:8], source)
            for x in range(2):
                moved = pltpu.roll(source, slab_shift(x0, m, x), 1)
                out = jnp.where(lane // 16 == x * 4 + m, moved, out)
        geo[:, r * SITES : (r + 1) * SITES] = out

    slab(0)

    lane16 = iota((16, SITES), 1)
    index = jnp.zeros((16, SITES), F32)
    for m in range(4):
        for x in range(2):
            moved = pltpu.roll(rcv1[m, 8:24], slab_shift(2 * j, m, x), 1)
            index = jnp.where(lane16 // 16 == x * 4 + m, moved, index)
    index = index.astype(jnp.int32)
    z = index & 3
    y = ((index >> 2) & 7) - 2 + lane16 // 16 % 4 * 4
    x = (index >> 5) - 2 - 2 * j
    inner = (x & 1) * 64 + y * 4 + z + jnp.where(x < 0, LEFT, jnp.where(x > 1, RIGHT, 0))
    outer = (x & 1) * 8 + (y & 1) * 4 + z + jnp.where(x < 0, ACROSS + 16, jnp.where(x > 1, ACROSS + 32, ACROSS))
    beyond = jnp.where(c == 0, y - 16, -1 - y) >= 0
    place = jnp.where((y >= 0) & (y < 16), inner, jnp.where(beyond, outer, -1))
    ext_row = iota((EXT, SITES), 0)
    for k in range(SLOTS):
        hit = ext_row == place[k : k + 1]
        oh[:, k * SITES : (k + 1) * SITES] = jnp.where(hit, 1.0, 0.0).astype(BF16)

    present = geo[3:4, 0:SITES]
    own_hot = (geo[4:5, 0:SITES].astype(jnp.int32) == iota((16, SITES), 0)).astype(F32)

    def species_weights(layer):
        for k in range(4):
            mix[layer, k] = dot_exact(pw_ref[layer, :, k, :], own_hot[0:10], TN)

    species_weights(0)
    h0 = dot(emb_ref[...].astype(F32), own_hot[0:10], TN) * present

    for slot in range(4, 10):
        receive(always if slot < 5 else has_other, rcv1.at[slot, 0:8], 0, slot)
    slab(1)
    slab(2)
    out = jnp.zeros((8, SITES), F32)
    for r, (x0, other) in enumerate(slabs):
        source = rcv1[4, 0:8]
        if r > 0:
            source = jnp.where(other, rcv1[9, 0:8], source)
        for x in range(2):
            moved = pltpu.roll(source, strip_shift(x0, r, x), 1)
            out = jnp.where(lane // 8 == r * 2 + x, moved, out)
    geo[:, 3 * SITES : 4 * SITES] = out

    gathered = dot(split3(geo[:, 0:EXT]), oh[...])
    gathered = gathered[0:8] + gathered[8:16] + gathered[16:24]
    for k in range(SLOTS):
        gs[k * 8 : k * 8 + 8, :] = gathered[:, k * SITES : (k + 1) * SITES]
    ext_hot = (geo[4:5, 0:EXT].astype(jnp.int32) == iota((16, EXT), 0)).astype(F32)
    u0 = dot(lifted_table, ext_hot[0:10], TN).astype(BF16)
    u[0] = dot(u0, oh[...]).astype(BF16)

    def rows_of(ref, m):
        return ref[pl.ds(m, SLOTS, stride=8), :]

    disp = [rows_of(gs, c) - geo[c : c + 1, 0:SITES] for c in range(3)]
    w = rows_of(gs, 3) * present
    squared = disp[0] * disp[0] + disp[1] * disp[1] + disp[2] * disp[2]
    dist = jnp.sqrt(jnp.where(w > 0, squared, 1.0))
    inv = 1.0 / dist
    nx, ny, nz = [c * inv for c in disp]
    scaled = jnp.minimum(dist * (1.0 / CUTOFF), 1.0)
    u2 = scaled * scaled
    u5 = u2 * u2 * scaled
    u6 = u5 * scaled
    env = 1.0 - 28.0 * u6 + 48.0 * u6 * scaled - 21.0 * u6 * u2
    env = jnp.where(scaled < 1.0, env, 0.0)
    gap = 1.0 - scaled
    slope = (-168.0 / CUTOFF) * u5 * gap * gap
    env_w = env * w
    slope_w = slope * w
    ye_scale = FACTOR * env_w
    harmonics = [
        ROOT3 * nx,
        ROOT3 * ny,
        ROOT3 * nz,
        ROOT15 * nx * ny,
        ROOT15 * ny * nz,
        0.5 * ROOT5 * (3.0 * nz * nz - 1.0),
        ROOT15 * nx * nz,
        0.5 * ROOT15 * (nx * nx - ny * ny),
    ]
    for m in range(9):
        one = ye_scale if m == 0 else ye_scale * harmonics[m - 1]
        for k in range(SLOTS):
            ye[m, k] = jnp.broadcast_to(one[k : k + 1], (16, SITES)).astype(BF16)
    theta = math.pi * scaled
    sin1 = jnp.sin(theta)
    cos1 = jnp.cos(theta)
    twice = 2.0 * cos1
    sin_before, cos_before = jnp.zeros_like(sin1), jnp.ones_like(cos1)
    sin_m, cos_m = sin1, cos1
    amplitude = math.sqrt(2.0 / CUTOFF) * inv
    for m in range(BES):
        value = amplitude * sin_m
        bs[pl.ds(m, SLOTS, stride=8), :] = value
        bd[m, 0:SLOTS] = amplitude * ((m + 1) * math.pi / CUTOFF) * cos_m - value * inv
        sin_m, sin_before = twice * sin_m - sin_before, sin_m
        cos_m, cos_before = twice * cos_m - cos_before, cos_m

    def radial(layer):
        hidden = jnp.concatenate([bs[k * 8 : k * 8 + 8, :] for k in range(SLOTS)], axis=1)
        hidden = hidden.astype(BF16)
        for step, ref in enumerate((w1_t, w2_t, w3_t)):
            z = dot(ref[layer], hidden)
            g, slope_g = silu_parts(z)
            dsilu[layer, step] = slope_g
            hidden = g.astype(BF16)
        q[layer] = dot(w4_t[layer], hidden).astype(BF16)

    def harmonic(m, k):
        return jnp.concatenate([ye[m, k], ye[m, k]], axis=0)

    def aggregate(layer):
        def body(block, carry):
            c0 = pl.multiple_of(block * 32, 32)
            acc = [None] * 9
            for first_k in range(0, SLOTS, GROUP):
                some = [None] * 9
                for k in range(first_k, first_k + GROUP):
                    lanes = slice(k * SITES, (k + 1) * SITES)
                    uk = u[layer, pl.ds(c0, 32), lanes]
                    v = [q[layer, pl.ds(L * CH + c0, 32), lanes] * uk for L in range(3)]
                    for m in range(9):
                        term = harmonic(m, k) * v[0 if m == 0 else (1 if m < 4 else 2)]
                        some[m] = term if some[m] is None else some[m] + term
                for m in range(9):
                    one = some[m].astype(F32)
                    acc[m] = one if acc[m] is None else acc[m] + one
            for m in range(9):
                a[layer, m, pl.ds(c0, 32), :] = acc[m]
            p = [mix[layer, j, pl.ds(c0, 32), :] for j in range(4)]
            first = acc[1] * acc[1] + acc[2] * acc[2] + acc[3] * acc[3]
            second = acc[4] * acc[4] + acc[5] * acc[5] + acc[6] * acc[6]
            second = second + acc[7] * acc[7] + acc[8] * acc[8]
            result = p[0] * acc[0] + p[1] * acc[0] * acc[0] + p[2] * first + p[3] * second
            msg[pl.ds(c0, 32), :] = result.astype(BF16)
            return carry

        lax.fori_loop(0, CH // 32, body, 0)

    def slopes(layer, c0):
        p = [mix[layer, j, pl.ds(c0, 32), :] for j in range(1, 4)]
        out = [mix[layer, 0, pl.ds(c0, 32), :] + 2.0 * p[0] * a[layer, 0, pl.ds(c0, 32), :]]
        for m in range(1, 9):
            out.append((2.0 * p[1 if m < 4 else 2]) * a[layer, m, pl.ds(c0, 32), :])
        return out

    def by_degree(da, k):
        out = [harmonic(0, k) * da[0], None, None]
        for m in range(1, 9):
            degree = 1 if m < 4 else 2
            term = harmonic(m, k) * da[m]
            out[degree] = term if out[degree] is None else out[degree] + term
        return out

    def blocks(body):
        def step(block, carry):
            body(pl.multiple_of(block * 32, 32))
            return carry

        lax.fori_loop(0, CH // 32, step, 0)

    def prepare_first(c0):
        t = slopes(0, c0)
        for m in range(9):
            a[0, m, pl.ds(c0, 32), :] = t[m]
        t = [one.astype(BF16) for one in t]
        for k in range(SLOTS):
            lanes = slice(k * SITES, (k + 1) * SITES)
            uk = u[0, pl.ds(c0, 32), lanes]
            for L, one in enumerate(by_degree(t, k)):
                fq[pl.ds(L * CH + c0, 32), lanes] = one * uk

    def features_back(c0):
        g = bm[pl.ds(c0, 32), :]
        da = [g * one for one in slopes(1, c0)]
        for m in range(9):
            a[1, m, pl.ds(c0, 32), :] = da[m]
        da = [one.astype(BF16) for one in da]
        for k in range(SLOTS):
            lanes = slice(k * SITES, (k + 1) * SITES)
            uk = u[1, pl.ds(c0, 32), lanes]
            dv = by_degree(da, k)
            total = dv[0] * q[1, pl.ds(c0, 32), lanes]
            for L in range(1, 3):
                total = total + dv[L] * q[1, pl.ds(L * CH + c0, 32), lanes]
            du[pl.ds(c0, 32), lanes] = total
            for L in range(3):
                dq[pl.ds(L * CH + c0, 32), lanes] = dv[L] * uk

    def angular_back(layer, c0):
        da = [a[layer, m, pl.ds(c0, 32), :] for m in range(9)]
        if layer == 0:
            g = bm[pl.ds(c0, 32), :]
            da = [g * one for one in da]
            g = g.astype(BF16)
        da = [one.astype(BF16) for one in da]
        for k in range(SLOTS):
            lanes = slice(k * SITES, (k + 1) * SITES)
            uk = u[layer, pl.ds(c0, 32), lanes]
            v = [q[layer, pl.ds(L * CH + c0, 32), lanes] * uk for L in range(3)]
            for m in range(9):
                part = da[m] * v[0 if m == 0 else (1 if m < 4 else 2)]
                at = (m * SLOTS + k) * 8
                part = (part[0:16] + part[16:32]).astype(F32)
                s_acc[at : at + 8, :] += part[0:8] + part[8:16]
            if layer == 0:
                for L in range(3):
                    dq[pl.ds(L * CH + c0, 32), lanes] = g * fq[pl.ds(L * CH + c0, 32), lanes]

    def radial_back(layer):
        grad = dot(w4_ref[layer], dq[...])
        for step, ref in ((2, w3_ref), (1, w2_ref), (0, w1_ref)):
            dz = (grad * dsilu[layer, step]).astype(BF16)
            grad = dot(ref[layer], dz)
        return grad

    bm = nb
    radial(0)
    aggregate(0)
    mixed = dot(ow_t[0], msg[...])
    h1 = (h0 + present * mixed).astype(BF16)
    u1_rows = dot(h1, up_ref[1], TN)
    rows_held[...] = u1_rows
    snd2[0:128] = u1_rows.astype(BF16)
    y_rows = pl.multiple_of(y_strip * 4, 8)
    strip = [rows_held[pl.ds(y_rows + x * 64, 8), :] for x in range(2)]
    snd2[128:144] = jnp.concatenate(strip, axis=0).astype(BF16)
    u1 = dot(up_t[...], h1).astype(BF16)
    for r, (there, device, start, size) in enumerate(regions):
        source = snd2.at[0:128] if r < 2 else snd2.at[128:144]
        start = regions[facing[r]][2]
        send(there, None, device, source, rcv2.at[start : start + size], 1, r, facing[r])
    species_weights(1)
    blocks(prepare_first)
    radial(1)
    near = dot(u1, oh[0:SITES, :])
    for r, (there, _, start, size) in enumerate(regions):
        receive(there, rcv2.at[start : start + size], 1, r)
    u[1] = (near + dot(rcv2[...], oh[SITES:EXT, :], TN)).astype(BF16)
    aggregate(1)
    mixed = dot(ow_t[1], msg[...])
    h2 = (h1.astype(F32) + present * mixed).astype(BF16)

    diagonal = iota((CH, CH), 0) == iota((CH, CH), 1)
    linear = jnp.sum(jnp.where(diagonal, rl_ref[...], 0.0), axis=1, keepdims=True)
    small = iota((16, 16), 0) == iota((16, 16), 1)
    last = jnp.sum(jnp.where(small, rlast_ref[...], 0.0), axis=1, keepdims=True)
    z = dot(rh_ref[...], h2)
    g, slope_g = silu_parts(z)
    energy = jnp.sum(h1.astype(F32) * linear, axis=0, keepdims=True)
    energy = present * (energy + jnp.sum(g * last, axis=0, keepdims=True))
    dz = (present * last * slope_g).astype(BF16)
    dh2 = dot(rh_ref[...], dz, TN)
    dmixed = (present * dh2).astype(BF16)
    message_grad = dot(ow_ref[1], dmixed)
    bm[...] = message_grad
    blocks(features_back)
    snd3[...] = dot(oh[SITES:EXT, :], du[...], NT).astype(BF16)
    for r, (there, device, start, size) in enumerate(regions):
        target = regions[facing[r]][2]
        source = snd3.at[start : start + size]
        send(there, None, device, source, rcv3.at[target : target + size], 2, r, facing[r])
    near = dot(du[...], oh[0:SITES, :], NT)
    bessel_grad = radial_back(1)
    blocks(functools.partial(angular_back, 1))
    for r, (there, _, start, size) in enumerate(regions):
        receive(there, rcv3.at[start : start + size], 2, r)
    du1 = near + dot(rcv3[...], ps[...], TN)
    dh1 = dh2 + linear * present + dot(up_ref[1], du1.astype(BF16))
    dmixed = (present * dh1).astype(BF16)
    bm[...] = dot(ow_ref[0], dmixed)
    blocks(functools.partial(angular_back, 0))
    bessel_grad = bessel_grad + radial_back(0)

    for k in range(SLOTS):
        gs[k * 8 : k * 8 + 8, :] = bessel_grad[:, k * SITES : (k + 1) * SITES]
    dr = rows_of(gs, 0) * bd[0, 0:SLOTS]
    for m in range(1, BES):
        dr = dr + rows_of(gs, m) * bd[m, 0:SLOTS]

    def total_of(m):
        at = m * SLOTS * 8
        out = s_acc[pl.ds(at, SLOTS, stride=8), :]
        for j in range(1, 8):
            out = out + s_acc[pl.ds(at + j, SLOTS, stride=8), :]
        return FACTOR * out

    sums = [total_of(m) for m in range(9)]
    d_env = sums[0]
    for m in range(8):
        d_env = d_env + sums[m + 1] * harmonics[m]
    dr = dr + d_env * slope_w
    dy = [env_w * one for one in sums[1:]]
    dnx = ROOT3 * dy[0] + ROOT15 * (dy[3] * ny + dy[6] * nz + dy[7] * nx)
    dny = ROOT3 * dy[1] + ROOT15 * (dy[3] * nx + dy[4] * nz - dy[7] * ny)
    dnz = ROOT3 * dy[2] + ROOT15 * (dy[4] * ny + dy[6] * nx) + (3.0 * ROOT5) * dy[5] * nz
    radial_part = dr - inv * (dnx * nx + dny * ny + dnz * nz)
    gs[...] = jnp.zeros_like(gs)
    centre = []
    for axis, (dn, n) in enumerate(((dnx, nx), (dny, ny), (dnz, nz))):
        dd = dn * inv + radial_part * n
        gs[pl.ds(axis, SLOTS, stride=8), :] = dd
        centre.append(jnp.sum(dd, axis=0, keepdims=True))
    edge_grad = jnp.concatenate([gs[k * 8 : k * 8 + 8, :] for k in range(SLOTS)], axis=1)
    scattered = dot(split3(edge_grad), oh[...], NT)
    geo[:, 0:EXT] = scattered[0:8] + scattered[8:16] + scattered[16:24]
    for axis in range(3):
        geo[axis : axis + 1, 0:SITES] = geo[axis : axis + 1, 0:SITES] - centre[axis]
    geo[3:4, 0:SITES] = energy

    for group in (1, 0):
        for m in range(5):
            out = jnp.zeros((8, SITES), F32)
            for r, (x0, other) in enumerate(slabs):
                if group == 1 and r == 0:
                    continue
                for x in range(2):
                    if m < 4:
                        part, shift = r, slab_shift(x0, m, x)
                        at, width = x0 + x, 16
                    else:
                        part, shift = 3, strip_shift(x0, r, x)
                        at, width = 2 * (x0 + x) + c, 8
                    moved = pltpu.roll(geo[:, part * SITES : (part + 1) * SITES], lax.rem(SITES - shift, SITES), 1)
                    at = jnp.where(other, at, -1) if group == 1 else jnp.where(other, -1, at)
                    out = jnp.where(lane // width == at, moved, out)
            snd4[5 * group + m] = out
        for at in range(5 * group, 5 * group + 5):
            there, here, device = owners[at]
            slot = j if group == 0 else jnp.where(j == 0, 5, 4)
            slot = slot + (6 if at % 5 == 4 else 0)
            send(there, here, device, snd4.at[at], rcv4.at[slot], 3, at, slot)

    def settle(some):
        for there, remote in some:

            @pl.when(there)
            def _():
                remote().wait_send()

    settle(sent[:-10])
    for at, (there, here, _, _) in enumerate(readers):
        wanted = there if here is None else there | here
        receive(wanted, rcv4.at[at], 3, at)
    back = rcv4[0]
    for at in range(1, 12):
        back = back + rcv4[at]

    rows = [jnp.broadcast_to(-back[axis : axis + 1], (16, SITES)) for axis in range(3)]
    rows.append(jnp.broadcast_to(back[3:4], (16, SITES)))
    full = jnp.where(yz_mask[0:64], jnp.concatenate(rows, axis=0), 0.0)
    out = dot(split3(full), x_pick, NT)
    out = out[0:64] + out[64:128] + out[128:192]
    for y in range(4):
        for axis in range(3):
            out_ref[axis, y] = out[axis * 16 + y * 4 : axis * 16 + y * 4 + 4, 0:8]
        out_ref[3, y] = out[48 + y * 4 : 52 + y * 4, 0:8]
    settle(sent[-10:])


def shards(
    positions,
    occupied,
    species,
    neighbours,
    embedding,
    radial_first,
    radial_second,
    radial_third,
    radial_last,
    up_weight,
    product_weight,
    out_weight,
    read_linear,
    read_hidden,
    read_last,
):
    n_gx = lax.axis_size("gx")
    vmem = pl.BlockSpec(memory_space=pltpu.VMEM)
    operands = (
        positions.transpose(0, 2, 3, 1),
        occupied.transpose(1, 2, 0),
        species.transpose(1, 2, 0),
        neighbours,
        embedding,
        radial_first,
        radial_second,
        radial_third,
        radial_last,
        up_weight,
        product_weight,
        out_weight,
        read_linear,
        read_hidden.T,
        read_last.reshape(1, -1),
    )
    out = pl.pallas_call(
        functools.partial(kernel, n_gx),
        out_shape=jax.ShapeDtypeStruct((4, 4, 4, 8), F32),
        in_specs=[pl.BlockSpec(memory_space=pltpu.HBM)] * 15,
        out_specs=vmem,
        scratch_shapes=[pltpu.VMEM(one.shape, one.dtype) for one in operands]
        + [
            pltpu.VMEM((80, SITES), F32),
            pltpu.VMEM((SITES, SITES), F32),
            pltpu.VMEM((24, SITES), F32),
            pltpu.VMEM((8, 4 * SITES), F32),
            pltpu.VMEM((GHOSTS, SITES), BF16),
            pltpu.VMEM((EXT, EDGES), BF16),
            pltpu.VMEM((10, 24, SITES), F32),
            pltpu.VMEM((144, CH), BF16),
            pltpu.VMEM((GHOSTS, CH), BF16),
            pltpu.VMEM((GHOSTS, CH), BF16),
            pltpu.VMEM((GHOSTS, CH), BF16),
            pltpu.VMEM((10, 8, SITES), F32),
            pltpu.VMEM((12, 8, SITES), F32),
            pltpu.VMEM((SLOTS * 8, SITES), F32),
            pltpu.VMEM((SLOTS * 8, SITES), F32),
            pltpu.VMEM((9, SLOTS, 16, SITES), BF16),
            pltpu.VMEM((BES, 16, SITES), F32),
            pltpu.VMEM((LAYERS, 4, CH, SITES), F32),
            pltpu.VMEM((LAYERS, 3, RAD, EDGES), F32),
            pltpu.VMEM((LAYERS, 3 * CH, EDGES), BF16),
            pltpu.VMEM((LAYERS, CH, EDGES), BF16),
            pltpu.VMEM((LAYERS, 9, CH, SITES), F32),
            pltpu.VMEM((CH, SITES), BF16),
            pltpu.VMEM((3 * CH, EDGES), BF16),
            pltpu.VMEM((CH, EDGES), BF16),
            pltpu.VMEM((9 * SLOTS * 8, SITES), F32),
            pltpu.VMEM((LAYERS, RAD, BES), BF16),
            pltpu.VMEM((LAYERS, RAD, RAD), BF16),
            pltpu.VMEM((LAYERS, RAD, RAD), BF16),
            pltpu.VMEM((LAYERS, 3 * CH, RAD), BF16),
            pltpu.VMEM((LAYERS, CH, CH), BF16),
            pltpu.VMEM((CH, CH), BF16),
            pltpu.VMEM((3 * CH, EDGES), BF16),
            pltpu.VMEM((SITES, CH), F32),
            pltpu.SemaphoreType.DMA((15,)),
            pltpu.SemaphoreType.DMA((4, 12)),
            pltpu.SemaphoreType.DMA((4, 12)),
        ],
        compiler_params=pltpu.CompilerParams(
            collective_id=0, has_side_effects=True, vmem_limit_bytes=48 * 1024 * 1024
        ),
    )(*[pltpu.with_memory_space_constraint(one, pltpu.HBM) for one in operands])
    return out[3].transpose(2, 0, 1), out[:3].transpose(0, 3, 1, 2)


def solution(mesh):
    in_specs = (
        P(None, "gx", "gy", None),
        P("gx", "gy", None),
        P("gx", "gy", None),
        P("gx", "gy", None, None),
        P(),
        P(),
        P(),
        P(),
        P(),
        P(),
        P(),
        P(),
        P(),
        P(),
        P(),
    )
    out_specs = (P("gx", "gy", None), P(None, "gx", "gy", None))
    return jax.shard_map(shards, mesh=mesh, in_specs=in_specs, out_specs=out_specs, check_vma=False)
```
